32 devices in a mesh: grp: 2 (over y), row: 4 (over x, core), col: 4 (over z).
Axes of the slice: x: 2, y: 2, z: 4, core: 2. Of those that a mesh axis runs over, the one named last changes fastest.
Arguments:
- level_one: bfloat16 [128, 256, 192], P(('grp', 'row'), 'col'), parts along dimension 0, may hold values from -6 to 6
- level_two: bfloat16 [64, 128, 384], P(('grp', 'row'), 'col'), parts along dimension 0, may hold values from -6 to 6
- level_three: bfloat16 [32, 64, 768], P(('grp', 'row'), None, 'col'), parts along dimension 0, may hold values from -6 to 6
- level_four: bfloat16 [16, 32, 1536], P(('grp', 'row'), None, 'col'), parts along dimension 0, may hold values from -10.5 to 10.5
- bin_weight: bfloat16 [4, 1536, 256], P(None, 'col'), may hold values from -0.21875 to 0.21875
- neck_feature: bfloat16 [3, 3, 1536, 256], P(None, None, 'col'), may hold values from -0.0546875 to 0.0546875
- neck_pooled: bfloat16 [3, 3, 1024, 256], P(None, None, 'col'), may hold values from -0.0546875 to 0.0546875
- lateral_one: bfloat16 [192, 256], replicated, may hold values from -0.625 to 0.625
- lateral_two: bfloat16 [384, 256], replicated, may hold values from -0.4375 to 0.4375
- lateral_three: bfloat16 [768, 256], replicated, may hold values from -0.3125 to 0.3125
- smooth_weight: bfloat16 [3, 3, 3, 256, 256], replicated, may hold values from -0.1875 to 0.1875
- join_weight: bfloat16 [3, 3, 1024, 256], replicated, may hold values from -0.09375 to 0.09375
- biases: float32 [12, 256], replicated, may hold values from -2 to 2
Outputs:
- joined: bfloat16 [128, 256, 256], P(('grp', 'row'), 'col'), parts along dimension 0
The draws below stay inside these ranges and needn't reach their ends.
There are 2 independent parts, one for each index of `grp`. The reference program is written for one: setup_inputs(seed, part) draws one part's arguments, and reference() takes and returns one part's arrays. A program takes and returns all parts, laid end to end along the dimension named above; an argument that names none is the same for every part. Nothing has to cross between parts.
All inputs are finite; a program needn't handle non-finite values.
Results may differ from the reference program's by a relative error of at most 0.015.
Values may be sent and summed in bfloat16 or wider, within the bound.
No kernel may reach another device: no remote copies, remote signals or barrier semaphores. Data moves between devices by JAX's collectives and lax.ppermute only.
A program may use at most 64 MiB of HBM per device.

```python
import math
import jax
import jax.numpy as jnp
from jax import lax

C1 = 192
C2 = 384
C3 = 768
C4 = 1536
CH = 256
NH1 = 64
NW1 = 256
NH2 = 32
NW2 = 128
NH3 = 16
NW3 = 64
NH4 = 8
NW4 = 32


def draw_level_four(key, part):
    pieces = jax.random.split(jax.random.fold_in(key, 41), 6)
    shape = (NH4, NW4, C4)
    down = jnp.arange(NH4, dtype=jnp.float32)[:, None, None]
    across = jnp.arange(NW4, dtype=jnp.float32)[None, :, None]
    level_mean = jnp.clip(jax.random.normal(pieces[1], (C4,), jnp.float32), -3.0, 3.0)
    wave_size = jnp.clip(jax.random.normal(pieces[2], (C4,), jnp.float32), -2.0, 2.0)
    freq_down = jax.random.randint(pieces[3], (C4,), 1, 4).astype(jnp.float32)
    freq_across = jax.random.randint(pieces[4], (C4,), 0, 4).astype(jnp.float32)
    phase = jax.random.uniform(pieces[5], (C4,), jnp.float32, -math.pi, math.pi)
    noise = 0.6 * jnp.clip(jax.random.normal(pieces[0], shape, jnp.float32), -4.0, 4.0)
    trend = 0.5 + 1.5 * down / NH4
    wave = jnp.cos(2.0 * math.pi * (freq_down * down / NH4 + freq_across * across / NW4) + phase)
    return (noise + level_mean * trend + wave_size * wave).astype(jnp.bfloat16)


def level_of(key, shape, cuts, smallest, high):
    def one(dim, shards_of):
        heights = jax.random.uniform(jax.random.fold_in(jax.random.fold_in(key, 6), dim), (shards_of,), jnp.float32, smallest / len(cuts), high / len(cuts))
        return jnp.repeat(jnp.exp(heights), shape[dim] // shards_of).reshape((-1,) + (1,) * (len(shape) - dim - 1))

    loudness = one(*cuts[0])
    for cut in cuts[1:]:
        loudness = loudness * one(*cut)
    return loudness


def normal_values(key, dims, deviation, limit, cuts=(), kind=jnp.bfloat16):
    factor_of = level_of(key, dims, cuts, -0.22, 0.18) if cuts else 1.0
    array = jax.random.normal(key, dims, jnp.float32) * deviation * factor_of
    return jnp.minimum(jnp.maximum(array, -limit), limit).astype(kind)


def setup_inputs(seed: int = 0, part: int = 0) -> dict:
    seeds = jax.random.split(jax.random.key(seed), 14)
    part_keys = jax.random.split(jax.random.fold_in(seeds[13], part), 14)
    level_one = normal_values(part_keys[0], (NH1, NW1, C1), 1.0, 6.0, ((0, 4), (1, 4)))
    level_two = normal_values(part_keys[1], (NH2, NW2, C2), 1.0, 6.0, ((0, 4), (1, 4)))
    level_three = normal_values(part_keys[2], (NH3, NW3, C3), 1.0, 6.0, ((0, 4), (2, 4)))
    level_four = draw_level_four(jax.random.fold_in(jax.random.fold_in(seeds[13], part), 71), part)
    bin_weight = normal_values(seeds[4], (4, C4, CH), (C4 // 2) ** -0.5, 0.21875, ((1, 4),))
    neck_feature = normal_values(seeds[5], (3, 3, C4, CH), (9 * (C4 + 4 * CH) // 2) ** -0.5, 0.0546875, ((2, 4),))
    neck_pooled = normal_values(seeds[6], (3, 3, 4 * CH, CH), (9 * (C4 + 4 * CH) // 2) ** -0.5, 0.0546875, ((2, 4),))
    lateral_one = normal_values(seeds[7], (C1, CH), (C1 // 2) ** -0.5, 0.625)
    lateral_two = normal_values(seeds[8], (C2, CH), (C2 // 2) ** -0.5, 0.4375)
    lateral_three = normal_values(seeds[9], (C3, CH), (C3 // 2) ** -0.5, 0.3125)
    smooth_weight = normal_values(seeds[10], (3, 3, 3, CH, CH), (9 * CH // 2) ** -0.5, 0.1875)
    join_weight = normal_values(seeds[11], (3, 3, 4 * CH, CH), (9 * 4 * CH // 2) ** -0.5, 0.09375)
    biases = normal_values(seeds[12], (12, CH), 0.3, 2.0, (), jnp.float32)
    return dict(level_one=level_one, level_two=level_two, level_three=level_three, level_four=level_four, bin_weight=bin_weight, neck_feature=neck_feature, neck_pooled=neck_pooled, lateral_one=lateral_one, lateral_two=lateral_two, lateral_three=lateral_three, smooth_weight=smooth_weight, join_weight=join_weight, biases=biases)


highest = lax.Precision.HIGHEST
bin_sides = (1, 2, 3, 6)


def pool_matrix(bin_side, extent, first, length):
    cell_index = jnp.arange(bin_side, dtype=jnp.int32)[:, None]
    position = first + jnp.arange(length, dtype=jnp.int32)[None, :]
    cell_first = (cell_index * extent) // bin_side
    cell_end = ((cell_index + 1) * extent + bin_side - 1) // bin_side
    inside = (position >= cell_first) & (position < cell_end)
    return inside.astype(jnp.float32) / (cell_end - cell_first).astype(jnp.float32)


def stretch_rows(position, bin_side, extent):
    source = jnp.clip((position + 0.5) * bin_side / extent - 0.5, 0.0, bin_side - 1.0)
    targets = jnp.arange(bin_side, dtype=jnp.float32)[None, :]
    return jnp.maximum(0.0, 1.0 - jnp.abs(source[:, None] - targets))


def taps_sum(padded, weight):
    height = padded.shape[0] - 2
    breadth = padded.shape[1] - 2
    channels = padded.shape[2]
    summed = jnp.zeros((height * breadth, weight.shape[-1]), jnp.float32)
    for row_tap in range(3):
        for col_tap in range(3):
            window = padded[row_tap:row_tap + height, col_tap:col_tap + breadth].reshape(height * breadth, channels)
            summed = summed + jnp.dot(window, weight[row_tap, col_tap], preferred_element_type=jnp.float32)
    return summed.reshape(height, breadth, -1)


def conv_same(feature, weight):
    return taps_sum(jnp.pad(feature, ((1, 1), (1, 1), (0, 0))), weight)


def project(feature, weight):
    height, breadth, channels = feature.shape
    result = jnp.dot(feature.reshape(height * breadth, channels), weight, preferred_element_type=jnp.float32)
    return result.reshape(height, breadth, -1)


def upscale(feature, factor):
    height, breadth = feature.shape[0], feature.shape[1]
    row_weights = stretch_rows(jnp.arange(height * factor, dtype=jnp.float32), height, height * factor)
    col_weights = stretch_rows(jnp.arange(breadth * factor, dtype=jnp.float32), breadth, breadth * factor)
    result = jnp.einsum("oh,hwc->owc", row_weights, feature.astype(jnp.float32), precision=highest)
    return jnp.einsum("pw,owc->opc", col_weights, result, precision=highest)


def reference(level_one, level_two, level_three, level_four, bin_weight, neck_feature, neck_pooled,
              lateral_one, lateral_two, lateral_three, smooth_weight, join_weight, biases):
    grid_rows, grid_cols = level_four.shape[0], level_four.shape[1]
    coarse = level_four.astype(jnp.float32)
    bin_maps = []
    for number, bin_side in enumerate(bin_sides):
        pool_down = pool_matrix(bin_side, grid_rows, 0, grid_rows)
        pool_across = pool_matrix(bin_side, grid_cols, 0, grid_cols)
        pooled = jnp.einsum("ih,hwc->iwc", pool_down, coarse, precision=highest)
        pooled = jnp.einsum("jw,iwc->ijc", pool_across, pooled, precision=highest)
        mapped = jnp.einsum("ijc,cd->ijd", pooled, bin_weight[number].astype(jnp.float32), precision=highest)
        binned = jax.nn.relu(mapped + biases[number])
        stretch_down = stretch_rows(jnp.arange(grid_rows, dtype=jnp.float32), bin_side, grid_rows)
        stretch_across = stretch_rows(jnp.arange(grid_cols, dtype=jnp.float32), bin_side, grid_cols)
        spread = jnp.einsum("hi,ijd->hjd", stretch_down, binned, precision=highest)
        spread = jnp.einsum("wj,hjd->hwd", stretch_across, spread, precision=highest)
        bin_maps.append(spread)
    ppm_maps = jnp.concatenate(bin_maps, axis=2).astype(jnp.bfloat16)
    stacked = jnp.concatenate([level_four, ppm_maps], axis=2)
    neck_weight = jnp.concatenate([neck_feature, neck_pooled], axis=2)
    pyramid_four = jax.nn.relu(conv_same(stacked, neck_weight) + biases[4]).astype(jnp.bfloat16)
    pyramid_three = (jax.nn.relu(project(level_three, lateral_three) + biases[7])
                     + upscale(pyramid_four, 2)).astype(jnp.bfloat16)
    pyramid_two = (jax.nn.relu(project(level_two, lateral_two) + biases[6])
                   + upscale(pyramid_three, 2)).astype(jnp.bfloat16)
    pyramid_one = (jax.nn.relu(project(level_one, lateral_one) + biases[5])
                   + upscale(pyramid_two, 2)).astype(jnp.bfloat16)
    smooth_one = jax.nn.relu(conv_same(pyramid_one, smooth_weight[0]) + biases[8]).astype(jnp.bfloat16)
    smooth_two = jax.nn.relu(conv_same(pyramid_two, smooth_weight[1]) + biases[9]).astype(jnp.bfloat16)
    smooth_three = jax.nn.relu(conv_same(pyramid_three, smooth_weight[2]) + biases[10]).astype(jnp.bfloat16)
    stacked_top = jnp.concatenate([
        smooth_one,
        upscale(smooth_two, 2).astype(jnp.bfloat16),
        upscale(smooth_three, 4).astype(jnp.bfloat16),
        upscale(pyramid_four, 8).astype(jnp.bfloat16)], axis=2)
    return jax.nn.relu(conv_same(stacked_top, join_weight) + biases[11]).astype(jnp.bfloat16)
```

```python
import jax
import jax.numpy as jnp
from jax import lax
from jax.sharding import PartitionSpec as P

highest = lax.Precision.HIGHEST
bin_sides = (1, 2, 3, 6)
rim = 2
f32 = jnp.float32
bf16 = jnp.bfloat16


def others(value, axis):
    count = lax.axis_size(axis)
    for shift in range(1, count):
        yield lax.ppermute(value, axis, [(i, (i + shift) % count) for i in range(count)])


def windows_sum(padded, axis, dim, pitch, width, join):
    count = lax.axis_size(axis)
    here = lax.axis_index(axis)

    def window_for(target):
        return lax.dynamic_slice_in_dim(padded, target * pitch, width, dim)

    pieces = [window_for(here)]
    for shift in range(1, count):
        target = lax.rem(here + shift, count)
        pieces.append(
            lax.ppermute(window_for(target), axis, [(i, (i + shift) % count) for i in range(count)])
        )
    return join(pieces)


def edge_swap(low_out, high_out, axis):
    count = lax.axis_size(axis)
    forward = [(i, i + 1) for i in range(count - 1)]
    backward = [(target, source) for source, target in forward]
    return lax.ppermute(high_out, axis, forward), lax.ppermute(low_out, axis, backward)


def cell_table(size):
    branch, row, col = [], [], []
    for number, side in enumerate(bin_sides):
        for i in range(side):
            for j in range(side):
                branch.append(number)
                row.append(i)
                col.append(j)
    return (
        jnp.array(branch, jnp.int32),
        jnp.array(row, jnp.int32),
        jnp.array(col, jnp.int32),
        jnp.array([bin_sides[b] for b in branch], jnp.int32),
    )


def pool_inside(index, side, extent):
    position = jnp.arange(extent, dtype=jnp.int32)[None, :]
    first = (index * extent // side)[:, None]
    end = (((index + 1) * extent + side - 1) // side)[:, None]
    inside = ((position >= first) & (position < end)).astype(f32)
    return inside, (end - first).astype(f32)


def spread_weights(position, index, side, extent):
    sides = side.astype(f32)[None, :]
    source = (position.astype(f32)[:, None] + 0.5) * sides / extent - 0.5
    source = jnp.minimum(jnp.maximum(source, 0.0), sides - 1.0)
    return jnp.maximum(0.0, 1.0 - jnp.abs(source - index.astype(f32)[None, :]))


def stretch(first_out, length_out, first_in, length_in, factor, extent):
    output = (first_out + jnp.arange(length_out, dtype=jnp.int32)).astype(f32)
    source = jnp.clip((output + 0.5) / factor - 0.5, 0.0, extent - 1.0)
    targets = (first_in + jnp.arange(length_in, dtype=jnp.int32)).astype(f32)
    inside = ((output >= 0.0) & (output < extent * factor)).astype(f32)
    return jnp.maximum(0.0, 1.0 - jnp.abs(source[:, None] - targets[None, :])) * inside[:, None]


def conv(feature, weight, padding):
    return lax.conv_general_dilated(
        feature[None],
        weight,
        (1, 1),
        padding,
        dimension_numbers=("NHWC", "HWIO", "NHWC"),
        preferred_element_type=f32,
    )[0]


def project(feature, weight):
    height, breadth, channels = feature.shape
    result = jnp.dot(
        feature.reshape(height * breadth, channels), weight, preferred_element_type=f32
    )
    return result.reshape(height, breadth, -1)


def local(
    level_one,
    level_two,
    level_three,
    level_four,
    bin_weight,
    neck_feature,
    neck_pooled,
    lateral_one,
    lateral_two,
    lateral_three,
    smooth_weight,
    join_weight,
    biases,
):
    row_here = lax.axis_index("row")
    col_here = lax.axis_index("col")
    row_count = lax.axis_size("row")
    col_count = lax.axis_size("col")
    rows4, grid_cols, part_four = level_four.shape
    grid_rows = rows4 * row_count
    cols4 = grid_cols // col_count
    channels = bin_weight.shape[2]

    four = lax.all_gather(level_four, "row", axis=0, tiled=True)
    branch, cell_row, cell_col, cell_side = cell_table(None)
    cells = branch.shape[0]
    in_rows, row_size = pool_inside(cell_row, cell_side, grid_rows)
    in_cols, col_size = pool_inside(cell_col, cell_side, grid_cols)
    inside = (in_rows[:, :, None] * in_cols[:, None, :]).reshape(cells, -1).astype(bf16)
    pooled = jnp.dot(inside, four.reshape(-1, part_four), preferred_element_type=f32)
    pooled = (pooled / (row_size * col_size)).astype(bf16)
    terms = []
    offset = 0
    for number, side in enumerate(bin_sides):
        terms.append(
            jnp.dot(
                pooled[offset : offset + side * side],
                bin_weight[number],
                preferred_element_type=f32,
            )
        )
        offset += side * side
    bin_term = jnp.concatenate(terms, axis=0).astype(bf16)
    bin_total = bin_term.astype(f32)
    for other in others(bin_term, "col"):
        bin_total = bin_total + other.astype(f32)

    lat_one = jax.nn.relu(project(level_one, lateral_one) + biases[5]).astype(bf16)
    lat_two = jax.nn.relu(project(level_two, lateral_two) + biases[6]).astype(bf16)
    cols3 = level_three.shape[1] // col_count
    three_wide = windows_sum(
        jnp.pad(level_three, ((0, 0), (rim, rim), (0, 0))),
        "col",
        1,
        cols3,
        cols3 + 2 * rim,
        lambda pieces: pieces,
    )
    share_three = level_three.shape[2]
    three_sum = jnp.zeros((), f32)
    for shift, piece in enumerate(three_wide):
        source = lax.rem(col_here - shift + col_count, col_count)
        weight = lax.dynamic_slice_in_dim(lateral_three, source * share_three, share_three, 0)
        three_sum = three_sum + project(piece, weight)
    lat_three = jax.nn.relu(three_sum + biases[7])
    rows3 = level_three.shape[0]
    first_col3 = col_here * cols3 - rim
    place = first_col3 + jnp.arange(cols3 + 2 * rim, dtype=jnp.int32)
    in_three = ((place >= 0) & (place < cols3 * col_count))[None, :, None]
    lat_three = jnp.where(in_three, lat_three, 0.0).astype(bf16)

    levels = [lat_one, lat_two, lat_three]

    def pack(parts):
        return jnp.concatenate([p.reshape(-1, channels) for p in parts], axis=0)

    def unpack(packed, shapes):
        result, start = [], 0
        for shape in shapes:
            size = shape[0] * shape[1]
            result.append(packed[start : start + size].reshape(shape + (channels,)))
            start += size
        return result

    shapes = [(rim, level.shape[1]) for level in levels]
    above, below = edge_swap(
        pack([level[:rim] for level in levels]), pack([level[-rim:] for level in levels]), "row"
    )
    levels = [
        jnp.concatenate([a, level, b], axis=0)
        for a, level, b in zip(unpack(above, shapes), levels, unpack(below, shapes))
    ]
    sided = levels[:2]
    shapes = [(level.shape[0], rim) for level in sided]
    before, after = edge_swap(
        pack([level[:, :rim] for level in sided]), pack([level[:, -rim:] for level in sided]), "col"
    )
    wide_one, wide_two = [
        jnp.concatenate([a, level, b], axis=1)
        for a, level, b in zip(unpack(before, shapes), sided, unpack(after, shapes))
    ]
    wide_three = levels[2]

    first_row = row_here * rows4
    span = rows4 + 2 * rim + 2
    place_rows = first_row - rim - 1 + jnp.arange(span, dtype=jnp.int32)
    in_grid = ((place_rows >= 0) & (place_rows < grid_rows)).astype(f32)
    four_span = lax.dynamic_slice_in_dim(
        jnp.pad(four, ((rim + 1, rim + 1), (0, 0), (0, 0))), first_row, span, 0
    )
    binned = jax.nn.relu(bin_total + biases[branch])
    spread_rows = spread_weights(place_rows, cell_row, cell_side, grid_rows) * in_grid[:, None]
    spread_cols = spread_weights(
        jnp.arange(grid_cols, dtype=jnp.int32), cell_col, cell_side, grid_cols
    )
    spread = (spread_rows[:, None, :] * spread_cols[None, :, :]).reshape(-1, cells)
    share_ppm = neck_pooled.shape[2]
    branches = len(bin_sides)
    lane_branch = jnp.arange(branches * channels, dtype=jnp.int32) // channels
    sorted_bins = jnp.where(
        branch[:, None] == lane_branch[None, :], jnp.tile(binned, (1, branches)), 0.0
    )
    sorted_bins = lax.dynamic_slice_in_dim(sorted_bins, col_here * share_ppm, share_ppm, 1)
    ppm = jnp.dot(spread, sorted_bins, precision=highest).astype(bf16)
    ppm = ppm.reshape(span, grid_cols, share_ppm)
    around = ((0, 0), (1, 1))
    neck_term = conv(four_span, neck_feature, around) + conv(ppm, neck_pooled, around)
    neck_pad = jnp.pad(neck_term.astype(bf16), ((0, 0), (rim, rim), (0, 0)))
    top_sum = windows_sum(
        neck_pad,
        "col",
        1,
        cols4,
        cols4 + 2 * rim,
        lambda pieces: sum(p.astype(f32) for p in pieces),
    )
    top = jax.nn.relu(top_sum + biases[4]).astype(bf16)

    def upscale(source, level_rows, level_cols, factor, border_in, border_out):
        high, wide = source.shape[0], source.shape[1]
        out_high = level_rows * factor + 2 * border_out
        out_wide = level_cols * factor + 2 * border_out
        down = stretch(
            row_here * level_rows * factor - border_out,
            out_high,
            row_here * level_rows - border_in,
            high,
            factor,
            level_rows * row_count,
        )
        across = stretch(
            col_here * level_cols * factor - border_out,
            out_wide,
            col_here * level_cols - border_in,
            wide,
            factor,
            level_cols * col_count,
        )
        matrix = (down[:, None, :, None] * across[None, :, None, :]).reshape(
            out_high * out_wide, high * wide
        )
        result = jnp.dot(
            matrix.astype(bf16), source.reshape(high * wide, -1), preferred_element_type=f32
        )
        return result.reshape(out_high, out_wide, -1)

    rows2, cols2 = level_two.shape[0], level_two.shape[1]
    rows1, cols1 = level_one.shape[0], level_one.shape[1]
    pyr_three = (wide_three.astype(f32) + upscale(top, rows4, cols4, 2, rim, rim)).astype(bf16)
    pyr_two = (wide_two.astype(f32) + upscale(pyr_three, rows3, cols3, 2, rim, rim)).astype(bf16)
    pyr_one = (wide_one.astype(f32) + upscale(pyr_two, rows2, cols2, 2, rim, rim)).astype(bf16)
    valid = ((0, 0), (0, 0))
    smooth_one = jax.nn.relu(conv(pyr_one, smooth_weight[0], valid) + biases[8])
    smooth_two = jax.nn.relu(conv(pyr_two, smooth_weight[1], valid) + biases[9]).astype(bf16)
    smooth_three = jax.nn.relu(conv(pyr_three, smooth_weight[2], valid) + biases[10]).astype(bf16)

    def in_image(length, here, count):
        place = here * length - 1 + jnp.arange(length + 2, dtype=jnp.int32)
        return (place >= 0) & (place < length * count)

    mask = (
        in_image(rows1, row_here, row_count)[:, None] & in_image(cols1, col_here, col_count)[None, :]
    )
    smooth_one = jnp.where(mask[:, :, None], smooth_one, 0.0).astype(bf16)
    stacked_top = jnp.concatenate(
        [
            smooth_one,
            upscale(smooth_two, rows2, cols2, 2, 1, 1).astype(bf16),
            upscale(smooth_three, rows3, cols3, 4, 1, 1).astype(bf16),
            upscale(top, rows4, cols4, 8, rim, 1).astype(bf16),
        ],
        axis=2,
    )
    return jax.nn.relu(conv(stacked_top, join_weight, valid) + biases[11]).astype(bf16)


def solution(mesh):
    placed = (
        P(("grp", "row"), "col", None),
        P(("grp", "row"), "col", None),
        P(("grp", "row"), None, "col"),
        P(("grp", "row"), None, "col"),
        P(None, "col", None),
        P(None, None, "col", None),
        P(None, None, "col", None),
        P(),
        P(),
        P(),
        P(),
        P(),
        P(),
    )
    return jax.shard_map(
        local, mesh=mesh, in_specs=placed, out_specs=P(("grp", "row"), "col", None), check_vma=False
    )
```

```python
import functools

import jax
import jax.numpy as jnp
from jax import lax
from jax.experimental import pallas as pl
from jax.experimental.pallas import tpu as pltpu
from jax.sharding import PartitionSpec as P

highest = lax.Precision.HIGHEST
bin_sides = (1, 2, 3, 6)
rim = 2
f32 = jnp.float32
bf16 = jnp.bfloat16


def others(value, axis):
    count = lax.axis_size(axis)
    for shift in range(1, count):
        yield lax.ppermute(value, axis, [(i, (i + shift) % count) for i in range(count)])


def windows_sum(padded, axis, dim, pitch, width, join):
    count = lax.axis_size(axis)
    here = lax.axis_index(axis)

    def window_for(target):
        return lax.dynamic_slice_in_dim(padded, target * pitch, width, dim)

    pieces = [window_for(here)]
    for shift in range(1, count):
        target = lax.rem(here + shift, count)
        pieces.append(
            lax.ppermute(window_for(target), axis, [(i, (i + shift) % count) for i in range(count)])
        )
    return join(pieces)


def edge_swap(low_out, high_out, axis):
    count = lax.axis_size(axis)
    forward = [(i, i + 1) for i in range(count - 1)]
    backward = [(target, source) for source, target in forward]
    return lax.ppermute(high_out, axis, forward), lax.ppermute(low_out, axis, backward)


def cell_table(size):
    branch, row, col = [], [], []
    for number, side in enumerate(bin_sides):
        for i in range(side):
            for j in range(side):
                branch.append(number)
                row.append(i)
                col.append(j)
    return (
        jnp.array(branch, jnp.int32),
        jnp.array(row, jnp.int32),
        jnp.array(col, jnp.int32),
        jnp.array([bin_sides[b] for b in branch], jnp.int32),
    )


def pool_inside(index, side, extent):
    position = jnp.arange(extent, dtype=jnp.int32)[None, :]
    first = (index * extent // side)[:, None]
    end = (((index + 1) * extent + side - 1) // side)[:, None]
    inside = ((position >= first) & (position < end)).astype(f32)
    return inside, (end - first).astype(f32)


def spread_weights(position, index, side, extent):
    sides = side.astype(f32)[None, :]
    source = (position.astype(f32)[:, None] + 0.5) * sides / extent - 0.5
    source = jnp.minimum(jnp.maximum(source, 0.0), sides - 1.0)
    return jnp.maximum(0.0, 1.0 - jnp.abs(source - index.astype(f32)[None, :]))


def conv(feature, weight, padding):
    return lax.conv_general_dilated(
        feature[None],
        weight,
        (1, 1),
        padding,
        dimension_numbers=("NHWC", "HWIO", "NHWC"),
        preferred_element_type=f32,
    )[0]


def project(feature, weight):
    height, breadth, channels = feature.shape
    result = jnp.dot(
        feature.reshape(height * breadth, channels), weight, preferred_element_type=f32
    )
    return result.reshape(height, breadth, -1)


def floor_div(value, step):
    return jnp.floor((value + 0.5) / step)


def stretch_matrix(out_shape, out_first, in_shape, in_first, factor, extent):
    out_rows, out_pitch = out_shape
    in_rows, in_pitch = in_shape
    place = lax.broadcasted_iota(jnp.int32, (1, in_rows * in_pitch), 1).astype(f32)
    place_row = floor_div(place, in_pitch)
    place_col = place - place_row * in_pitch

    def weights(length, first_out, first_in, targets, whole):
        output = first_out + lax.broadcasted_iota(jnp.int32, (length, 1), 0).astype(f32)
        source = (output + 0.5) * (1.0 / factor) - 0.5
        source = jnp.minimum(jnp.maximum(source, 0.0), whole - 1.0)
        inside = jnp.where((output >= 0.0) & (output < whole * factor), 1.0, 0.0)
        return jnp.maximum(0.0, 1.0 - jnp.abs(source - (first_in + targets))) * inside

    down = weights(out_rows, out_first[0], in_first[0], place_row, extent[0])
    across = weights(out_pitch, out_first[1], in_first[1], place_col, extent[1])
    matrix = down[:, None, :] * across[None, :, :]
    return matrix.astype(bf16).reshape(out_rows * out_pitch, in_rows * in_pitch)


def tail_kernel(
    sizes,
    top_count,
    here_ref,
    *refs,
):
    (high1, wide1), (high2, wide2), (high3, wide3), (high4, wide4), (row_count, col_count) = sizes
    top_refs, refs = refs[:top_count], refs[top_count:]
    (
        lat1_ref,
        lat2_ref,
        lat3_ref,
        above_ref,
        below_ref,
        before_ref,
        after_ref,
        bias_ref,
        smooth_hbm,
        join_hbm,
        out_ref,
        top_buf,
        lat1_buf,
        lat2_buf,
        lat3_buf,
        pyr1_buf,
        pyr2_buf,
        pyr3_buf,
        acc_buf,
        sums_buf,
        stack_buf,
        smooth_w,
        join_w,
        sems,
    ) = refs
    smooth_copy = pltpu.make_async_copy(smooth_hbm, smooth_w, sems.at[0])
    join_copy = pltpu.make_async_copy(join_hbm, join_w, sems.at[1])
    smooth_copy.start()
    join_copy.start()
    row_here = here_ref[0].astype(f32)
    col_here = here_ref[1].astype(f32)
    channels = bias_ref.shape[1]

    def firsts(high, wide, border):
        return row_here * high - border, col_here * wide - border

    def extent(high, wide):
        return float(high * row_count), float(wide * col_count)

    start = 0
    for ref, buf, high, wide in (
        (lat1_ref, lat1_buf, high1, wide1),
        (lat2_ref, lat2_buf, high2, wide2),
    ):
        buf[...] = jnp.zeros_like(buf)
        buf[rim : rim + high, rim : rim + wide, :] = ref[...].astype(f32)
        for source, row in ((above_ref, 0), (below_ref, rim + high)):
            for step in range(rim):
                at = start + step * wide
                buf[row + step, rim : rim + wide, :] = source[at : at + wide, :].astype(f32)
        start += rim * wide
    lat3_buf[...] = jnp.zeros_like(lat3_buf)
    whole3 = wide3 + 2 * rim
    lat3_buf[rim : rim + high3, :whole3, :] = lat3_ref[...].astype(f32)
    for source, row in ((above_ref, 0), (below_ref, rim + high3)):
        both = source[start : start + rim * whole3, :].astype(f32)
        for step in range(rim):
            lat3_buf[row + step, :whole3, :] = both[step * whole3 : (step + 1) * whole3]
    start = 0
    for buf, high, wide in ((lat1_buf, high1, wide1), (lat2_buf, high2, wide2)):
        tall = high + 2 * rim
        for source, col in ((before_ref, 0), (after_ref, rim + wide)):
            sides = source[start : start + rim * tall, :].astype(f32)
            for row in range(tall):
                buf[row, col : col + rim, :] = sides[rim * row : rim * row + rim]
        start += rim * tall

    tall4, whole4 = high4 + 2 * rim, wide4 + 2 * rim
    top_sum = top_refs[0][...].astype(f32)
    for ref in top_refs[1:]:
        top_sum = top_sum + ref[...].astype(f32)
    top_buf[...] = jnp.zeros_like(top_buf)
    top_buf[:, :whole4, :] = jnp.maximum(top_sum + bias_ref[4:5, :][None], 0.0)
    pitch4 = top_buf.shape[1]
    top = top_buf[...].astype(bf16).reshape(tall4 * pitch4, channels)

    def dot(a, b):
        return jnp.dot(a, b, preferred_element_type=f32)

    def pyramid(lat_buf, high, wide, source, source_shape, source_first, source_size):
        rows, pitch = lat_buf.shape[:2]
        matrix = stretch_matrix(
            (rows, pitch), firsts(high, wide, rim), source_shape, source_first, 2, extent(*source_size)
        )
        total = lat_buf[...].reshape(rows * pitch, channels) + dot(matrix, source)
        return total.astype(bf16)

    first4 = firsts(high4, wide4, rim)
    pyr3_buf[...] = pyramid(lat3_buf, high3, wide3, top, (tall4, pitch4), first4, (high4, wide4))
    shape3 = lat3_buf.shape[:2]
    pyr2_buf[...] = pyramid(
        lat2_buf, high2, wide2, pyr3_buf[...], shape3, firsts(high3, wide3, rim), (high3, wide3)
    )
    shape2 = lat2_buf.shape[:2]
    pyr1_buf[...] = pyramid(
        lat1_buf, high1, wide1, pyr2_buf[...], shape2, firsts(high2, wide2, rim), (high2, wide2)
    )
    shape1 = lat1_buf.shape[:2]
    smooth_copy.wait()

    def conv(source, shape, weight_at, rows):
        pitch = shape[1]
        span = rows * pitch
        for col_tap in range(3):
            total = dot(source[0:span, :], weight_at(0, col_tap))
            for row_tap in (1, 2):
                total = total + dot(
                    source[row_tap * pitch : row_tap * pitch + span, :], weight_at(row_tap, col_tap)
                )
            yield col_tap, total.reshape(rows, pitch, channels)

    def smooth(number, source, shape, wide):
        rows, pitch = shape[0] - 2, shape[1]
        for col_tap, total in conv(
            source, shape, lambda i, j: smooth_w[number, i, j], rows
        ):
            acc_buf[col_tap, :rows, :pitch, :] = total
        whole = wide + 2
        total = (
            acc_buf[0, :rows, 0:whole, :]
            + acc_buf[1, :rows, 1 : whole + 1, :]
            + acc_buf[2, :rows, 2 : whole + 2, :]
        )
        return jnp.maximum(total + bias_ref[8 + number : 9 + number, :][None], 0.0)

    def smooth_flat(number, source, shape, wide):
        rows, pitch = shape[0] - 2, shape[1]
        value = smooth(number, source, shape, wide)
        sums_buf[:rows, :pitch, :] = jnp.zeros((rows, pitch, channels), f32)
        sums_buf[:rows, : wide + 2, :] = value
        return sums_buf[:rows, :pitch, :].astype(bf16).reshape(rows * pitch, channels)

    rows1, pitch1 = shape1[0] - 2, shape1[1]
    out_first = firsts(high1, wide1, 1)

    def raise_to_one(source, source_shape, source_first, factor, source_size):
        matrix = stretch_matrix(
            (rows1, pitch1), out_first, source_shape, source_first, factor, extent(*source_size)
        )
        return dot(matrix, source).astype(bf16)

    stack_buf[:, 3 * channels : 4 * channels] = raise_to_one(
        top, (tall4, pitch4), first4, 8, (high4, wide4)
    )
    smooth3 = smooth_flat(2, pyr3_buf, shape3, wide3)
    stack_buf[:, 2 * channels : 3 * channels] = raise_to_one(
        smooth3, (shape3[0] - 2, shape3[1]), firsts(high3, wide3, 1), 4, (high3, wide3)
    )
    smooth2 = smooth_flat(1, pyr2_buf, shape2, wide2)
    stack_buf[:, channels : 2 * channels] = raise_to_one(
        smooth2, (shape2[0] - 2, shape2[1]), firsts(high2, wide2, 1), 2, (high2, wide2)
    )
    value = smooth(0, pyr1_buf, shape1, wide1)
    down = out_first[0] + lax.broadcasted_iota(jnp.int32, (rows1, 1, 1), 0).astype(f32)
    across = out_first[1] + lax.broadcasted_iota(jnp.int32, (1, wide1 + 2, 1), 1).astype(f32)
    tall, broad = extent(high1, wide1)
    inside = (down >= 0.0) & (down < tall) & (across >= 0.0) & (across < broad)
    sums_buf[:rows1, : wide1 + 2, :] = jnp.where(inside, value, 0.0)
    stack_buf[:, 0:channels] = sums_buf[...].astype(bf16).reshape(rows1 * pitch1, channels)
    join_copy.wait()
    shape_join = (rows1, pitch1)
    for col_tap, total in conv(stack_buf, shape_join, lambda i, j: join_w[i, j], high1):
        acc_buf[col_tap, :high1] = total
    total = (
        acc_buf[0, :high1, 0:wide1, :]
        + acc_buf[1, :high1, 1 : wide1 + 1, :]
        + acc_buf[2, :high1, 2 : wide1 + 2, :]
    )
    out_ref[...] = jnp.maximum(total + bias_ref[11:12, :][None], 0.0).astype(bf16)


def pitch_of(width):
    return (width + 15) // 16 * 16


def tail(here, tops, lats, above, below, before, after, biases, smooth_weight, join_weight, sizes):
    (high1, wide1), (high2, wide2), (high3, wide3), (high4, wide4), _ = sizes
    channels = biases.shape[1]

    def window(high, wide):
        return high + 2 * rim, pitch_of(wide + 2 * rim)

    shapes = [window(high, wide) for high, wide in sizes[:4]]
    (rows1, pitch1), (rows2, pitch2), (rows3, pitch3), (rows4, pitch4) = shapes
    vmem = pl.BlockSpec(memory_space=pltpu.VMEM)
    anywhere = pl.BlockSpec(memory_space=pl.ANY)
    return pl.pallas_call(
        functools.partial(tail_kernel, sizes, len(tops)),
        out_shape=jax.ShapeDtypeStruct((high1, wide1, channels), bf16),
        in_specs=[pl.BlockSpec(memory_space=pltpu.SMEM)]
        + [vmem] * (len(tops) + 8)
        + [anywhere] * 2,
        out_specs=vmem,
        scratch_shapes=[
            pltpu.VMEM((rows4, pitch4, channels), f32),
            pltpu.VMEM((rows1, pitch1, channels), f32),
            pltpu.VMEM((rows2, pitch2, channels), f32),
            pltpu.VMEM((rows3, pitch3, channels), f32),
            pltpu.VMEM((rows1 * pitch1, channels), bf16),
            pltpu.VMEM((rows2 * pitch2, channels), bf16),
            pltpu.VMEM((rows3 * pitch3, channels), bf16),
            pltpu.VMEM((3, rows1 - 2, pitch1, channels), f32),
            pltpu.VMEM((rows1 - 2, pitch1, channels), f32),
            pltpu.VMEM(((rows1 - 2) * pitch1, 4 * channels), bf16),
            pltpu.VMEM(smooth_weight.shape, bf16),
            pltpu.VMEM(join_weight.shape, bf16),
            pltpu.SemaphoreType.DMA((2,)),
        ],
        compiler_params=pltpu.CompilerParams(vmem_limit_bytes=60 * 1024 * 1024),
        cost_estimate=pl.CostEstimate(
            flops=10_000_000_000, bytes_accessed=12_000_000, transcendentals=0
        ),
    )(here, *tops, *lats, above, below, before, after, biases, smooth_weight, join_weight)


def local(
    level_one,
    level_two,
    level_three,
    level_four,
    bin_weight,
    neck_feature,
    neck_pooled,
    lateral_one,
    lateral_two,
    lateral_three,
    smooth_weight,
    join_weight,
    biases,
):
    row_here = lax.axis_index("row")
    col_here = lax.axis_index("col")
    row_count = lax.axis_size("row")
    col_count = lax.axis_size("col")
    rows4, grid_cols, part_four = level_four.shape
    grid_rows = rows4 * row_count
    cols4 = grid_cols // col_count
    channels = bin_weight.shape[2]

    four = lax.all_gather(level_four, "row", axis=0, tiled=True)
    branch, cell_row, cell_col, cell_side = cell_table(None)
    cells = branch.shape[0]
    in_rows, row_size = pool_inside(cell_row, cell_side, grid_rows)
    in_cols, col_size = pool_inside(cell_col, cell_side, grid_cols)
    inside = (in_rows[:, :, None] * in_cols[:, None, :]).reshape(cells, -1).astype(bf16)
    pooled = jnp.dot(inside, four.reshape(-1, part_four), preferred_element_type=f32)
    pooled = (pooled / (row_size * col_size)).astype(bf16)
    terms = []
    offset = 0
    for number, side in enumerate(bin_sides):
        terms.append(
            jnp.dot(
                pooled[offset : offset + side * side],
                bin_weight[number],
                preferred_element_type=f32,
            )
        )
        offset += side * side
    bin_term = jnp.concatenate(terms, axis=0).astype(bf16)
    bin_total = bin_term.astype(f32)
    for other in others(bin_term, "col"):
        bin_total = bin_total + other.astype(f32)

    lat_one = jax.nn.relu(project(level_one, lateral_one) + biases[5]).astype(bf16)
    lat_two = jax.nn.relu(project(level_two, lateral_two) + biases[6]).astype(bf16)
    cols3 = level_three.shape[1] // col_count
    three_wide = windows_sum(
        jnp.pad(level_three, ((0, 0), (rim, rim), (0, 0))),
        "col",
        1,
        cols3,
        cols3 + 2 * rim,
        lambda pieces: pieces,
    )
    share_three = level_three.shape[2]
    three_sum = jnp.zeros((), f32)
    for shift, piece in enumerate(three_wide):
        source = lax.rem(col_here - shift + col_count, col_count)
        weight = lax.dynamic_slice_in_dim(lateral_three, source * share_three, share_three, 0)
        three_sum = three_sum + project(piece, weight)
    lat_three = jax.nn.relu(three_sum + biases[7])
    rows3 = level_three.shape[0]
    first_col3 = col_here * cols3 - rim
    place = first_col3 + jnp.arange(cols3 + 2 * rim, dtype=jnp.int32)
    in_three = ((place >= 0) & (place < cols3 * col_count))[None, :, None]
    lat_three = jnp.where(in_three, lat_three, 0.0).astype(bf16)

    levels = [lat_one, lat_two, lat_three]

    def pack(parts):
        return jnp.concatenate([p.reshape(-1, channels) for p in parts], axis=0)

    def unpack(packed, shapes):
        result, start = [], 0
        for shape in shapes:
            size = shape[0] * shape[1]
            result.append(packed[start : start + size].reshape(shape + (channels,)))
            start += size
        return result

    shapes = [(rim, level.shape[1]) for level in levels]
    above, below = edge_swap(
        pack([level[:rim] for level in levels]), pack([level[-rim:] for level in levels]), "row"
    )
    shapes = [(rim, level.shape[1]) for level in levels]

    def sides(value):
        return jnp.concatenate([value[:, :rim], value[:, -rim:]], axis=1)

    sided = [
        jnp.concatenate([sides(a), sides(level), sides(b)], axis=0)
        for a, level, b in zip(unpack(above, shapes)[:2], levels[:2], unpack(below, shapes)[:2])
    ]
    before, after = edge_swap(
        pack([level[:, :rim] for level in sided]), pack([level[:, -rim:] for level in sided]), "col"
    )

    first_row = row_here * rows4
    span = rows4 + 2 * rim + 2
    place_rows = first_row - rim - 1 + jnp.arange(span, dtype=jnp.int32)
    in_grid = ((place_rows >= 0) & (place_rows < grid_rows)).astype(f32)
    four_span = lax.dynamic_slice_in_dim(
        jnp.pad(four, ((rim + 1, rim + 1), (0, 0), (0, 0))), first_row, span, 0
    )
    binned = jax.nn.relu(bin_total + biases[branch])
    spread_rows = spread_weights(place_rows, cell_row, cell_side, grid_rows) * in_grid[:, None]
    spread_cols = spread_weights(
        jnp.arange(grid_cols, dtype=jnp.int32), cell_col, cell_side, grid_cols
    )
    spread = (spread_rows[:, None, :] * spread_cols[None, :, :]).reshape(-1, cells)
    share_ppm = neck_pooled.shape[2]
    branches = len(bin_sides)
    lane_branch = jnp.arange(branches * channels, dtype=jnp.int32) // channels
    sorted_bins = jnp.where(
        branch[:, None] == lane_branch[None, :], jnp.tile(binned, (1, branches)), 0.0
    )
    sorted_bins = lax.dynamic_slice_in_dim(sorted_bins, col_here * share_ppm, share_ppm, 1)
    ppm = jnp.dot(spread, sorted_bins, precision=highest).astype(bf16)
    ppm = ppm.reshape(span, grid_cols, share_ppm)
    around = ((0, 0), (1, 1))
    neck_term = conv(four_span, neck_feature, around) + conv(ppm, neck_pooled, around)
    neck_pad = jnp.pad(neck_term.astype(bf16), ((0, 0), (rim, rim), (0, 0)))
    tops = windows_sum(
        neck_pad,
        "col",
        1,
        cols4,
        cols4 + 2 * rim,
        lambda pieces: pieces,
    )
    sizes = (
        level_one.shape[:2],
        level_two.shape[:2],
        (rows3, cols3),
        (rows4, cols4),
        (row_count, col_count),
    )
    here = jnp.stack([row_here, col_here]).astype(jnp.int32)
    return tail(
        here,
        tops,
        levels,
        above,
        below,
        before,
        after,
        biases,
        smooth_weight,
        join_weight,
        sizes,
    )


def solution(mesh):
    placed = (
        P(("grp", "row"), "col", None),
        P(("grp", "row"), "col", None),
        P(("grp", "row"), None, "col"),
        P(("grp", "row"), None, "col"),
        P(None, "col", None),
        P(None, None, "col", None),
        P(None, None, "col", None),
        P(),
        P(),
        P(),
        P(),
        P(),
        P(),
    )
    return jax.shard_map(
        local, mesh=mesh, in_specs=placed, out_specs=P(("grp", "row"), "col", None), check_vma=False
    )
```

```python
import functools

import jax
import jax.numpy as jnp
import numpy as np
from jax import lax
from jax.experimental import pallas as pl
from jax.experimental.pallas import tpu as pltpu
from jax.sharding import PartitionSpec as P

highest = lax.Precision.HIGHEST
bin_sides = (1, 2, 3, 6)
rim = 2
f32 = jnp.float32
bf16 = jnp.bfloat16
vmem_spec = pl.BlockSpec(memory_space=pltpu.VMEM)
smem_spec = pl.BlockSpec(memory_space=pltpu.SMEM)
params = pltpu.CompilerParams(vmem_limit_bytes=24 * 1024 * 1024)


def shifted(value, axis, shift):
    count = lax.axis_size(axis)
    return lax.ppermute(value, axis, [(i, (i + shift) % count) for i in range(count)])


def edge_swap(low_out, high_out, axis):
    count = lax.axis_size(axis)
    forward = [(i, i + 1) for i in range(count - 1)]
    backward = [(target, source) for source, target in forward]
    return lax.ppermute(high_out, axis, forward), lax.ppermute(low_out, axis, backward)


def cell_table(extent_rows, extent_cols):
    rows = []
    for number, side in enumerate(bin_sides):
        for i in range(side):
            for j in range(side):
                top, low = i * extent_rows // side, -(-(i + 1) * extent_rows // side)
                left, right = j * extent_cols // side, -(-(j + 1) * extent_cols // side)
                rows.append([number, side, i, j, top, low, left, right, (low - top) * (right - left)])
    padded = (len(rows) + 15) // 16 * 16
    table = np.zeros((padded, 16), np.float32)
    table[:, 0] = -1.0
    table[:, 1] = 1.0
    table[:, 8] = 1.0
    table[: len(rows), :9] = np.array(rows, np.float32)
    return table


def dot(a, b):
    return jnp.dot(a, b, preferred_element_type=f32)


def call(kernel, outs, specs, scratch, flops, moved):
    return pl.pallas_call(
        kernel,
        out_shape=outs,
        in_specs=specs,
        out_specs=jax.tree.map(lambda _: vmem_spec, outs),
        scratch_shapes=scratch,
        compiler_params=params,
        cost_estimate=pl.CostEstimate(flops=flops, bytes_accessed=moved, transcendentals=0),
    )


def wrap(value, count):
    return lax.rem(value + count, count)


def floor_div(value, step):
    return jnp.floor((value + 0.5) / step)


def lateral_kernel(col_count, here_ref, one_ref, two_ref, three_ref, w1_ref, w2_ref, w3_ref, bias_ref, *refs):
    (lat1_ref, lat2_ref), pieces, (wide_buf, one_buf, two_buf, piece_buf) = (
        refs[:2],
        refs[2 : 2 + col_count],
        refs[2 + col_count :],
    )
    channels = w1_ref.shape[1]
    for source, weight, row, buf, out in (
        (one_ref, w1_ref, 5, one_buf, lat1_ref),
        (two_ref, w2_ref, 6, two_buf, lat2_ref),
    ):
        high, wide, depth = source.shape
        value = dot(source[...].reshape(high * wide, depth), weight[...])
        value = jnp.maximum(value + bias_ref[row : row + 1, :], 0.0).reshape(high, wide, channels)
        buf[...] = value
        out[...] = value.astype(bf16)
    high3, whole3, share = three_ref.shape
    wide3 = whole3 // col_count
    col_here = here_ref[1]
    weight = w3_ref[pl.ds(pl.multiple_of(col_here * share, 16), share), :]
    value = dot(three_ref[...].reshape(high3 * whole3, share), weight)
    wide_buf[...] = jnp.zeros_like(wide_buf)
    wide_buf[:, rim : rim + whole3, :] = value.reshape(high3, whole3, channels)
    span = wide3 + 2 * rim
    for shift, piece in enumerate(pieces):
        target = wrap(col_here + shift, col_count)
        for row in range(high3):
            piece_buf[row * span : (row + 1) * span, :] = wide_buf[
                row, pl.ds(pl.multiple_of(target * wide3, 8), span), :
            ]
        start = high3 * span
        for buf in (one_buf, two_buf):
            high, wide = buf.shape[:2]
            first = wide - rim if shift == 1 else 0
            for row in range(high):
                piece_buf[start : start + rim, :] = buf[row, first : first + rim, :]
                start += rim
        piece[...] = piece_buf[...].astype(bf16)


def bins_kernel(row_count, col_count, window_rows, here_ref, table_ref, weight_ref, *refs):
    blocks, pieces, messages = (
        refs[:row_count],
        refs[row_count : row_count + col_count],
        refs[row_count + col_count :],
    )
    table = table_ref[...]
    high, wide, depth = blocks[0].shape
    place = lax.broadcasted_iota(jnp.int32, (1, high * wide), 1).astype(f32)
    place_row = floor_div(place, wide)
    place_col = place - place_row * wide
    in_cols = (place_col >= table[:, 6:7]) & (place_col < table[:, 7:8])
    pooled = None
    for shift, block in enumerate(blocks):
        row = place_row + (wrap(here_ref[0] - shift, row_count) * high).astype(f32)
        inside = in_cols & (row >= table[:, 4:5]) & (row < table[:, 5:6])
        inside = jnp.where(inside, 1.0, 0.0).astype(bf16)
        term = dot(inside, block[...].reshape(high * wide, depth))
        pooled = term if pooled is None else pooled + term
    pooled = (pooled / table[:, 8:9]).astype(bf16)
    bins = None
    for number in range(len(bin_sides)):
        term = jnp.where(table[:, 0:1] == number, dot(pooled, weight_ref[number]), 0.0)
        bins = term if bins is None else bins + term
    bins = bins.astype(bf16)
    cells = bins.shape[0]
    for piece, message in zip(pieces, messages):
        message[0:window_rows, :] = piece[0:window_rows, :]
        message[window_rows : window_rows + cells, :] = bins
        if message.shape[0] > window_rows + cells:
            message[window_rows + cells :, :] = piece[window_rows:, :]


def feature_kernel(row_count, here_ref, weight_ref, *refs):
    blocks, (out_ref, grid_buf) = refs[:row_count], refs[row_count:]
    high, wide, depth = blocks[0].shape
    grid_buf[...] = jnp.zeros_like(grid_buf)
    for shift, block in enumerate(blocks):
        row = wrap(here_ref[0] - shift, row_count) * high + rim + 1
        grid_buf[pl.ds(row, high)] = block[...]
    rows = out_ref.shape[1] // wide
    window = grid_buf[pl.ds(here_ref[0] * high, rows + 2)].reshape((rows + 2) * wide, depth)
    for col_tap in range(3):
        total = dot(window[0 : rows * wide], weight_ref[0, col_tap])
        for row_tap in (1, 2):
            total = total + dot(
                window[row_tap * wide : (row_tap + rows) * wide], weight_ref[row_tap, col_tap]
            )
        out_ref[col_tap] = total


def neck_kernel(
    row_count, col_count, high, window_rows, here_ref, table_ref, turned_ref, weight_ref, bias_ref, taps_ref, *refs
):
    messages, refs = refs[:col_count], refs[col_count:]
    windows, (bins_buf, acc_buf, term_buf) = refs[:col_count], refs[col_count:]
    rows, span, channels = windows[0].shape
    wide = taps_ref.shape[1] // rows
    width4 = span - 2 * rim
    table = table_ref[...]
    cells = table.shape[0]
    bins = messages[0][window_rows : window_rows + cells, :].astype(f32)
    for message in messages[1:]:
        bins = bins + message[window_rows : window_rows + cells, :].astype(f32)
    bias = jnp.zeros((cells, channels), f32)
    for number in range(len(bin_sides)):
        bias = jnp.where(table[:, 0:1] == number, bias_ref[number : number + 1, :], bias)
    share = weight_ref.shape[2]
    first = here_ref[1] * share
    mine = table[:, 0:1] == (first // channels).astype(f32)
    bins_buf[...] = jnp.where(mine, jnp.maximum(bins + bias, 0.0), 0.0)
    if share == channels:
        binned = bins_buf[...]
    else:
        binned = bins_buf[:, pl.ds(pl.multiple_of(lax.rem(first, channels), 128), share)]
    place = lax.broadcasted_iota(jnp.int32, ((rows + 2) * wide, 1), 0).astype(f32)
    place_row = floor_div(place, wide)
    place_col = place - place_row * wide
    place_row = place_row + (here_ref[0] * high - rim - 1).astype(f32)
    grid_rows = float(high * row_count)
    sides = turned_ref[1:2, :]

    def weights(position, extent, index):
        source = (position + 0.5) * sides / extent - 0.5
        source = jnp.minimum(jnp.maximum(source, 0.0), sides - 1.0)
        return jnp.maximum(0.0, 1.0 - jnp.abs(source - index))

    spread = weights(place_row, grid_rows, turned_ref[2:3, :])
    spread = spread * weights(place_col, float(wide), turned_ref[3:4, :])
    spread = jnp.where((place_row >= 0.0) & (place_row < grid_rows), spread, 0.0)
    ppm = jnp.dot(spread, binned, precision=highest, preferred_element_type=f32).astype(bf16)
    size = rows * wide
    for col_tap in range(3):
        total = taps_ref[col_tap]
        for row_tap in range(3):
            total = total + dot(
                ppm[row_tap * wide : row_tap * wide + size], weight_ref[row_tap, col_tap]
            )
        acc_buf[col_tap, 8 : 8 + size, :] = total
    col = place_col[0:size]
    total = (
        acc_buf[1, 8 : 8 + size, :]
        + jnp.where(col > 0.0, acc_buf[0, 7 : 7 + size, :], 0.0)
        + jnp.where(col < wide - 1.0, acc_buf[2, 9 : 9 + size, :], 0.0)
    )
    term_buf[...] = jnp.zeros_like(term_buf)
    term_buf[:, rim : rim + wide, :] = total.reshape(rows, wide, channels)
    for shift, window in enumerate(windows):
        target = wrap(here_ref[1] + shift, col_count)
        window[...] = term_buf[:, pl.ds(pl.multiple_of(target * width4, 8), span), :].astype(bf16)


def rows_kernel(col_count, high3, wide3, here_ref, bias_ref, lat1_ref, lat2_ref, *refs):
    messages, (lat3_ref, low_ref, high_ref, three_buf, pack_buf) = refs[:col_count], refs[col_count:]
    span = wide3 + 2 * rim
    total = messages[0][0 : high3 * span, :].astype(f32)
    for message in messages[1:]:
        total = total + message[0 : high3 * span, :].astype(f32)
    total = jnp.maximum(total + bias_ref[7:8, :], 0.0)
    col_here = here_ref[1]
    place = lax.broadcasted_iota(jnp.int32, (span, 1), 0) + col_here * wide3 - rim
    inside = (place >= 0) & (place < wide3 * col_count)
    for row in range(high3):
        three_buf[row, :span, :] = jnp.where(inside, total[row * span : (row + 1) * span], 0.0)
    lat3_ref[...] = three_buf[:, :span, :].astype(bf16)
    high1, wide1 = lat1_ref.shape[:2]
    high2, wide2 = lat2_ref.shape[:2]
    before, after = messages[1], messages[col_count - 1]
    sides_at = before.shape[0] - rim * (high1 + high2)
    for out, last in ((low_ref, False), (high_ref, True)):
        start, at = 0, sides_at
        for lat, high, wide in ((lat1_ref, high1, wide1), (lat2_ref, high2, wide2)):
            whole = wide + 2 * rim
            first = high - rim if last else 0
            left = before[at + rim * first : at + rim * (first + rim), :].astype(f32)
            right = after[at + rim * first : at + rim * (first + rim), :].astype(f32)
            left = jnp.where(col_here > 0, left, 0.0)
            right = jnp.where(col_here < col_count - 1, right, 0.0)
            for step in range(rim):
                pack_buf[start : start + rim, :] = left[rim * step : rim * (step + 1)]
                pack_buf[start + rim : start + rim + wide, :] = lat[first + step].astype(f32)
                pack_buf[start + rim + wide : start + whole, :] = right[rim * step : rim * (step + 1)]
                start += whole
            at += rim * high
        for step in range(rim):
            row = high3 - rim + step if last else step
            pack_buf[start : start + span, :] = three_buf[row, :span, :]
            start += span
        out[...] = pack_buf[...].astype(bf16)


def stretch_matrix(out_shape, out_first, in_shape, in_first, factor, extent):
    out_rows, out_pitch = out_shape
    in_rows, in_pitch = in_shape
    place = lax.broadcasted_iota(jnp.int32, (1, in_rows * in_pitch), 1).astype(f32)
    place_row = floor_div(place, in_pitch)
    place_col = place - place_row * in_pitch

    def weights(length, first_out, first_in, targets, whole):
        output = first_out + lax.broadcasted_iota(jnp.int32, (length, 1), 0).astype(f32)
        source = (output + 0.5) * (1.0 / factor) - 0.5
        source = jnp.minimum(jnp.maximum(source, 0.0), whole - 1.0)
        inside = jnp.where((output >= 0.0) & (output < whole * factor), 1.0, 0.0)
        return jnp.maximum(0.0, 1.0 - jnp.abs(source - (first_in + targets))) * inside

    down = weights(out_rows, out_first[0], in_first[0], place_row, extent[0])
    across = weights(out_pitch, out_first[1], in_first[1], place_col, extent[1])
    matrix = down[:, None, :] * across[None, :, :]
    return matrix.astype(bf16).reshape(out_rows * out_pitch, in_rows * in_pitch)


def tail_kernel(
    sizes,
    top_count,
    here_ref,
    *refs,
):
    (high1, wide1), (high2, wide2), (high3, wide3), (high4, wide4), (row_count, col_count) = sizes
    top_refs, refs = refs[:top_count], refs[top_count:]
    (
        lat1_ref,
        lat2_ref,
        lat3_ref,
        above_ref,
        below_ref,
        before_ref,
        after_ref,
        bias_ref,
        smooth_hbm,
        join_hbm,
        out_ref,
        top_buf,
        lat1_buf,
        lat2_buf,
        lat3_buf,
        pyr1_buf,
        pyr2_buf,
        pyr3_buf,
        acc_buf,
        sums_buf,
        stack_buf,
        smooth_w,
        join_w,
        sems,
    ) = refs
    smooth_copy = pltpu.make_async_copy(smooth_hbm, smooth_w, sems.at[0])
    join_copy = pltpu.make_async_copy(join_hbm, join_w, sems.at[1])
    smooth_copy.start()
    join_copy.start()
    row_here = here_ref[0].astype(f32)
    col_here = here_ref[1].astype(f32)
    channels = bias_ref.shape[1]

    def firsts(high, wide, border):
        return row_here * high - border, col_here * wide - border

    def extent(high, wide):
        return float(high * row_count), float(wide * col_count)

    side_start = before_ref.shape[0] - rim * (high1 + high2)
    row_start = 0
    for ref, buf, high, wide in (
        (lat1_ref, lat1_buf, high1, wide1),
        (lat2_ref, lat2_buf, high2, wide2),
        (lat3_ref, lat3_buf, high3, wide3 + 2 * rim),
    ):
        buf[...] = jnp.zeros_like(buf)
        whole = wide
        if buf is lat3_buf:
            buf[rim : rim + high, :wide, :] = ref[...].astype(f32)
        else:
            whole = wide + 2 * rim
            buf[rim : rim + high, rim : rim + wide, :] = ref[...].astype(f32)
            for source, col, keep in (
                (before_ref, 0, here_ref[1] > 0),
                (after_ref, rim + wide, here_ref[1] < col_count - 1),
            ):
                sides = source[side_start : side_start + rim * high, :].astype(f32)
                sides = jnp.where(keep, sides, 0.0)
                for row in range(high):
                    buf[rim + row, col : col + rim, :] = sides[rim * row : rim * row + rim]
            side_start += rim * high
        for source, row in ((above_ref, 0), (below_ref, rim + high)):
            both = source[row_start : row_start + rim * whole, :].astype(f32)
            for step in range(rim):
                buf[row + step, :whole, :] = both[step * whole : (step + 1) * whole]
        row_start += rim * whole

    tall4, whole4 = high4 + 2 * rim, wide4 + 2 * rim
    top_sum = top_refs[0][...].astype(f32)
    for ref in top_refs[1:]:
        top_sum = top_sum + ref[...].astype(f32)
    top_buf[...] = jnp.zeros_like(top_buf)
    top_buf[:, :whole4, :] = jnp.maximum(top_sum + bias_ref[4:5, :][None], 0.0)
    pitch4 = top_buf.shape[1]
    top = top_buf[...].astype(bf16).reshape(tall4 * pitch4, channels)

    def pyramid(lat_buf, high, wide, source, source_shape, source_first, source_size):
        rows, pitch = lat_buf.shape[:2]
        matrix = stretch_matrix(
            (rows, pitch), firsts(high, wide, rim), source_shape, source_first, 2, extent(*source_size)
        )
        total = lat_buf[...].reshape(rows * pitch, channels) + dot(matrix, source)
        return total.astype(bf16)

    first4 = firsts(high4, wide4, rim)
    pyr3_buf[...] = pyramid(lat3_buf, high3, wide3, top, (tall4, pitch4), first4, (high4, wide4))
    shape3 = lat3_buf.shape[:2]
    pyr2_buf[...] = pyramid(
        lat2_buf, high2, wide2, pyr3_buf[...], shape3, firsts(high3, wide3, rim), (high3, wide3)
    )
    shape2 = lat2_buf.shape[:2]
    pyr1_buf[...] = pyramid(
        lat1_buf, high1, wide1, pyr2_buf[...], shape2, firsts(high2, wide2, rim), (high2, wide2)
    )
    shape1 = lat1_buf.shape[:2]
    smooth_copy.wait()

    def conv(source, shape, weight_at, rows):
        pitch = shape[1]
        span = rows * pitch
        for col_tap in range(3):
            total = dot(source[0:span, :], weight_at(0, col_tap))
            for row_tap in (1, 2):
                total = total + dot(
                    source[row_tap * pitch : row_tap * pitch + span, :], weight_at(row_tap, col_tap)
                )
            yield col_tap, total.reshape(rows, pitch, channels)

    def smooth(number, source, shape, wide):
        rows, pitch = shape[0] - 2, shape[1]
        for col_tap, total in conv(
            source, shape, lambda i, j: smooth_w[number, i, j], rows
        ):
            acc_buf[col_tap, :rows, :pitch, :] = total
        whole = wide + 2
        total = (
            acc_buf[0, :rows, 0:whole, :]
            + acc_buf[1, :rows, 1 : whole + 1, :]
            + acc_buf[2, :rows, 2 : whole + 2, :]
        )
        return jnp.maximum(total + bias_ref[8 + number : 9 + number, :][None], 0.0)

    def smooth_flat(number, source, shape, wide):
        rows, pitch = shape[0] - 2, shape[1]
        value = smooth(number, source, shape, wide)
        sums_buf[:rows, :pitch, :] = jnp.zeros((rows, pitch, channels), f32)
        sums_buf[:rows, : wide + 2, :] = value
        return sums_buf[:rows, :pitch, :].astype(bf16).reshape(rows * pitch, channels)

    rows1, pitch1 = shape1[0] - 2, shape1[1]
    out_first = firsts(high1, wide1, 1)

    def raise_to_one(source, source_shape, source_first, factor, source_size):
        matrix = stretch_matrix(
            (rows1, pitch1), out_first, source_shape, source_first, factor, extent(*source_size)
        )
        return dot(matrix, source).astype(bf16)

    stack_buf[:, 3 * channels : 4 * channels] = raise_to_one(
        top, (tall4, pitch4), first4, 8, (high4, wide4)
    )
    smooth3 = smooth_flat(2, pyr3_buf, shape3, wide3)
    stack_buf[:, 2 * channels : 3 * channels] = raise_to_one(
        smooth3, (shape3[0] - 2, shape3[1]), firsts(high3, wide3, 1), 4, (high3, wide3)
    )
    smooth2 = smooth_flat(1, pyr2_buf, shape2, wide2)
    stack_buf[:, channels : 2 * channels] = raise_to_one(
        smooth2, (shape2[0] - 2, shape2[1]), firsts(high2, wide2, 1), 2, (high2, wide2)
    )
    value = smooth(0, pyr1_buf, shape1, wide1)
    down = out_first[0] + lax.broadcasted_iota(jnp.int32, (rows1, 1, 1), 0).astype(f32)
    across = out_first[1] + lax.broadcasted_iota(jnp.int32, (1, wide1 + 2, 1), 1).astype(f32)
    tall, broad = extent(high1, wide1)
    inside = (down >= 0.0) & (down < tall) & (across >= 0.0) & (across < broad)
    sums_buf[:rows1, : wide1 + 2, :] = jnp.where(inside, value, 0.0)
    stack_buf[:, 0:channels] = sums_buf[...].astype(bf16).reshape(rows1 * pitch1, channels)
    join_copy.wait()
    shape_join = (rows1, pitch1)
    for col_tap, total in conv(stack_buf, shape_join, lambda i, j: join_w[i, j], high1):
        acc_buf[col_tap, :high1] = total
    total = (
        acc_buf[0, :high1, 0:wide1, :]
        + acc_buf[1, :high1, 1 : wide1 + 1, :]
        + acc_buf[2, :high1, 2 : wide1 + 2, :]
    )
    out_ref[...] = jnp.maximum(total + bias_ref[11:12, :][None], 0.0).astype(bf16)


def pitch_of(width):
    return (width + 15) // 16 * 16


def tail(here, tops, lats, above, below, before, after, biases, smooth_weight, join_weight, sizes):
    (high1, wide1), (high2, wide2), (high3, wide3), (high4, wide4), _ = sizes
    channels = biases.shape[1]

    def window(high, wide):
        return high + 2 * rim, pitch_of(wide + 2 * rim)

    shapes = [window(high, wide) for high, wide in sizes[:4]]
    (rows1, pitch1), (rows2, pitch2), (rows3, pitch3), (rows4, pitch4) = shapes
    vmem = pl.BlockSpec(memory_space=pltpu.VMEM)
    anywhere = pl.BlockSpec(memory_space=pl.ANY)
    return pl.pallas_call(
        functools.partial(tail_kernel, sizes, len(tops)),
        out_shape=jax.ShapeDtypeStruct((high1, wide1, channels), bf16),
        in_specs=[pl.BlockSpec(memory_space=pltpu.SMEM)]
        + [vmem] * (len(tops) + 8)
        + [anywhere] * 2,
        out_specs=vmem,
        scratch_shapes=[
            pltpu.VMEM((rows4, pitch4, channels), f32),
            pltpu.VMEM((rows1, pitch1, channels), f32),
            pltpu.VMEM((rows2, pitch2, channels), f32),
            pltpu.VMEM((rows3, pitch3, channels), f32),
            pltpu.VMEM((rows1 * pitch1, channels), bf16),
            pltpu.VMEM((rows2 * pitch2, channels), bf16),
            pltpu.VMEM((rows3 * pitch3, channels), bf16),
            pltpu.VMEM((3, rows1 - 2, pitch1, channels), f32),
            pltpu.VMEM((rows1 - 2, pitch1, channels), f32),
            pltpu.VMEM(((rows1 - 2) * pitch1, 4 * channels), bf16),
            pltpu.VMEM(smooth_weight.shape, bf16),
            pltpu.VMEM(join_weight.shape, bf16),
            pltpu.SemaphoreType.DMA((2,)),
        ],
        compiler_params=pltpu.CompilerParams(vmem_limit_bytes=44 * 1024 * 1024),
        cost_estimate=pl.CostEstimate(
            flops=10_000_000_000, bytes_accessed=12_000_000, transcendentals=0
        ),
    )(here, *tops, *lats, above, below, before, after, biases, smooth_weight, join_weight)


def local(
    level_one,
    level_two,
    level_three,
    level_four,
    bin_weight,
    neck_feature,
    neck_pooled,
    lateral_one,
    lateral_two,
    lateral_three,
    smooth_weight,
    join_weight,
    biases,
):
    row_count = lax.axis_size("row")
    col_count = lax.axis_size("col")
    here = jnp.stack([lax.axis_index("row"), lax.axis_index("col")]).astype(jnp.int32)
    high1, wide1 = level_one.shape[:2]
    high2, wide2 = level_two.shape[:2]
    high3, wide3 = level_three.shape[0], level_three.shape[1] // col_count
    high4, grid_cols, part_four = level_four.shape
    wide4 = grid_cols // col_count
    channels = bin_weight.shape[2]
    grid_rows = high4 * row_count
    table = cell_table(grid_rows, grid_cols)
    cells = table.shape[0]
    turned = jnp.asarray(np.ascontiguousarray(table.T))
    table = jnp.asarray(table)

    def shape(dims, kind=bf16):
        return jax.ShapeDtypeStruct(dims, kind)

    blocks = [level_four] + [shifted(level_four, "row", shift) for shift in range(1, row_count)]
    window_rows = high3 * (wide3 + 2 * rim)
    side_rows = rim * (high1 + high2)
    lat1, lat2, *pieces = call(
        functools.partial(lateral_kernel, col_count),
        [shape((high1, wide1, channels)), shape((high2, wide2, channels))]
        + [shape((window_rows + side_rows, channels))] * col_count,
        [smem_spec] + [vmem_spec] * 7,
        [
            pltpu.VMEM((high3, level_three.shape[1] + 8, channels), f32),
            pltpu.VMEM((high1, wide1, channels), f32),
            pltpu.VMEM((high2, wide2, channels), f32),
            pltpu.VMEM((window_rows + side_rows, channels), f32),
        ],
        300_000_000,
        2_000_000,
    )(here, level_one, level_two, level_three, lateral_one, lateral_two, lateral_three, biases)
    near = (1, col_count - 1)
    messages = call(
        functools.partial(bins_kernel, row_count, col_count, window_rows),
        [
            shape((window_rows + cells + (side_rows if shift in near else 0), channels))
            for shift in range(col_count)
        ],
        [smem_spec] + [vmem_spec] * (2 + row_count + col_count),
        [],
        100_000_000,
        1_000_000,
    )(here, table, bin_weight, *blocks, *pieces)

    received = [messages[0]] + [
        shifted(messages[shift], "col", shift) for shift in range(1, col_count)
    ]
    rows = high4 + 2 * rim
    taps = call(
        functools.partial(feature_kernel, row_count),
        shape((3, rows * grid_cols, channels), f32),
        [smem_spec] + [vmem_spec] * (1 + row_count),
        [pltpu.VMEM((grid_rows + 2 * rim + 2, grid_cols, part_four), bf16)],
        700_000_000,
        3_000_000,
    )(here, neck_feature, *blocks)
    span4 = wide4 + 2 * rim
    windows = call(
        functools.partial(neck_kernel, row_count, col_count, high4, window_rows),
        [shape((rows, span4, channels))] * col_count,
        [smem_spec] + [vmem_spec] * (5 + col_count),
        [
            pltpu.VMEM((cells, channels), f32),
            pltpu.VMEM((3, rows * grid_cols + 16, channels), f32),
            pltpu.VMEM((rows, grid_cols + 16, channels), f32),
        ],
        300_000_000,
        3_000_000,
    )(here, table, turned, neck_pooled, biases, taps, *received)

    tops = [windows[0]] + [shifted(windows[shift], "col", shift) for shift in range(1, col_count)]
    span3 = wide3 + 2 * rim
    packed = rim * (wide1 + wide2 + wide3 + 6 * rim)
    lat3, low_rows, high_rows = call(
        functools.partial(rows_kernel, col_count, high3, wide3),
        [shape((high3, span3, channels))] + [shape((packed, channels))] * 2,
        [smem_spec] + [vmem_spec] * (3 + col_count),
        [
            pltpu.VMEM((high3, (span3 + 7) // 8 * 8, channels), f32),
            pltpu.VMEM((packed, channels), f32),
        ],
        1_000_000,
        1_000_000,
    )(here, biases, lat1, lat2, *received)
    above, below = edge_swap(low_rows, high_rows, "row")
    sizes = (
        (high1, wide1),
        (high2, wide2),
        (high3, wide3),
        (high4, wide4),
        (row_count, col_count),
    )
    return tail(
        here,
        tops,
        (lat1, lat2, lat3),
        above,
        below,
        received[1],
        received[-1],
        biases,
        smooth_weight,
        join_weight,
        sizes,
    )


def solution(mesh):
    placed = (
        P(("grp", "row"), "col", None),
        P(("grp", "row"), "col", None),
        P(("grp", "row"), None, "col"),
        P(("grp", "row"), None, "col"),
        P(None, "col", None),
        P(None, None, "col", None),
        P(None, None, "col", None),
        P(),
        P(),
        P(),
        P(),
        P(),
        P(),
    )
    return jax.shard_map(
        local, mesh=mesh, in_specs=placed, out_specs=P(("grp", "row"), "col", None), check_vma=False
    )
```

```python
import functools

import jax
import jax.numpy as jnp
import numpy as np
from jax import lax
from jax.experimental import pallas as pl
from jax.experimental.pallas import tpu as pltpu
from jax.sharding import PartitionSpec as P

highest = lax.Precision.HIGHEST
bin_sides = (1, 2, 3, 6)
rim = 2
f32 = jnp.float32
bf16 = jnp.bfloat16
vmem_spec = pl.BlockSpec(memory_space=pltpu.VMEM)
hbm_spec = pl.BlockSpec(memory_space=pltpu.HBM)
smem_spec = pl.BlockSpec(memory_space=pltpu.SMEM)
params = pltpu.CompilerParams(vmem_limit_bytes=24 * 1024 * 1024)


def shifted(value, axis, shift):
    count = lax.axis_size(axis)
    return lax.ppermute(value, axis, [(i, (i + shift) % count) for i in range(count)])


def edge_swap(low_out, high_out, axis):
    count = lax.axis_size(axis)
    forward = [(i, i + 1) for i in range(count - 1)]
    backward = [(target, source) for source, target in forward]
    return lax.ppermute(high_out, axis, forward), lax.ppermute(low_out, axis, backward)


def cell_table(extent_rows, extent_cols):
    rows = []
    for number, side in enumerate(bin_sides):
        for i in range(side):
            for j in range(side):
                top, low = i * extent_rows // side, -(-(i + 1) * extent_rows // side)
                left, right = j * extent_cols // side, -(-(j + 1) * extent_cols // side)
                rows.append([number, side, i, j, top, low, left, right, (low - top) * (right - left)])
    padded = (len(rows) + 15) // 16 * 16
    table = np.zeros((padded, 16), np.float32)
    table[:, 0] = -1.0
    table[:, 1] = 1.0
    table[:, 8] = 1.0
    table[: len(rows), :9] = np.array(rows, np.float32)
    return table


def dot(a, b):
    return jnp.dot(a, b, preferred_element_type=f32)


def in_hbm(value):
    return pltpu.with_memory_space_constraint(value, pltpu.HBM)


def call(kernel, outs, specs, scratch, flops, moved):
    return pl.pallas_call(
        kernel,
        out_shape=outs,
        in_specs=specs,
        out_specs=jax.tree.map(lambda _: vmem_spec, outs),
        scratch_shapes=scratch,
        compiler_params=params,
        cost_estimate=pl.CostEstimate(flops=flops, bytes_accessed=moved, transcendentals=0),
    )


def wrap(value, count):
    return lax.rem(value + count, count)


def floor_div(value, step):
    return jnp.floor((value + 0.5) / step)


def lateral_kernel(col_count, kept_count, here_ref, *refs):
    sources, refs = refs[: 6 + kept_count], refs[6 + kept_count :]
    (lat1_ref, lat2_ref), refs = refs[:2], refs[2:]
    pieces, refs = refs[:col_count], refs[col_count:]
    kept, refs = refs[:kept_count], refs[kept_count:]
    fetched, (wide_buf, one_buf, two_buf, piece_buf, sems) = refs[:6], refs[6:]
    copies = [
        pltpu.make_async_copy(source, target, sems.at[number])
        for number, (source, target) in enumerate(zip(sources, (*fetched, *kept)))
    ]
    for copy in copies:
        copy.start()
    one_ref, w1_ref, two_ref, w2_ref, three_ref, w3_ref = fetched
    bias_ref = kept[0]
    copies[6].wait()
    channels = w1_ref.shape[1]
    for number, (source, weight, row, buf, out) in enumerate(
        (
            (one_ref, w1_ref, 5, one_buf, lat1_ref),
            (two_ref, w2_ref, 6, two_buf, lat2_ref),
        )
    ):
        copies[2 * number].wait()
        copies[2 * number + 1].wait()
        high, wide, depth = source.shape
        value = dot(source[...].reshape(high * wide, depth), weight[...])
        value = jnp.maximum(value + bias_ref[row : row + 1, :], 0.0).reshape(high, wide, channels)
        buf[...] = value
        out[...] = value.astype(bf16)
    high3, whole3, share = three_ref.shape
    wide3 = whole3 // col_count
    col_here = here_ref[1]
    copies[4].wait()
    copies[5].wait()
    weight = w3_ref[pl.ds(pl.multiple_of(col_here * share, 16), share), :]
    value = dot(three_ref[...].reshape(high3 * whole3, share), weight)
    wide_buf[...] = jnp.zeros_like(wide_buf)
    wide_buf[:, rim : rim + whole3, :] = value.reshape(high3, whole3, channels)
    span = wide3 + 2 * rim
    for shift, piece in enumerate(pieces):
        target = wrap(col_here + shift, col_count)
        for row in range(high3):
            piece_buf[row * span : (row + 1) * span, :] = wide_buf[
                row, pl.ds(pl.multiple_of(target * wide3, 8), span), :
            ]
        start = high3 * span
        for buf in (one_buf, two_buf):
            high, wide = buf.shape[:2]
            first = wide - rim if shift == 1 else 0
            for row in range(high):
                piece_buf[start : start + rim, :] = buf[row, first : first + rim, :]
                start += rim
        piece[...] = piece_buf[...].astype(bf16)
    for copy in copies[7:]:
        copy.wait()


def bins_kernel(row_count, col_count, window_rows, here_ref, table_ref, weight_ref, *refs):
    blocks, pieces, messages = (
        refs[:row_count],
        refs[row_count : row_count + col_count],
        refs[row_count + col_count :],
    )
    table = table_ref[...]
    high, wide, depth = blocks[0].shape
    place = lax.broadcasted_iota(jnp.int32, (1, high * wide), 1).astype(f32)
    place_row = floor_div(place, wide)
    place_col = place - place_row * wide
    in_cols = (place_col >= table[:, 6:7]) & (place_col < table[:, 7:8])
    pooled = None
    for shift, block in enumerate(blocks):
        row = place_row + (wrap(here_ref[0] - shift, row_count) * high).astype(f32)
        inside = in_cols & (row >= table[:, 4:5]) & (row < table[:, 5:6])
        inside = jnp.where(inside, 1.0, 0.0).astype(bf16)
        term = dot(inside, block[...].reshape(high * wide, depth))
        pooled = term if pooled is None else pooled + term
    pooled = (pooled / table[:, 8:9]).astype(bf16)
    bins = None
    for number in range(len(bin_sides)):
        term = jnp.where(table[:, 0:1] == number, dot(pooled, weight_ref[number]), 0.0)
        bins = term if bins is None else bins + term
    bins = bins.astype(bf16)
    cells = bins.shape[0]
    for piece, message in zip(pieces, messages):
        message[0:window_rows, :] = piece[0:window_rows, :]
        message[window_rows : window_rows + cells, :] = bins
        if message.shape[0] > window_rows + cells:
            message[window_rows + cells :, :] = piece[window_rows:, :]


def feature_kernel(row_count, here_ref, weight_ref, *refs):
    blocks, (out_ref, grid_buf) = refs[:row_count], refs[row_count:]
    high, wide, depth = blocks[0].shape
    grid_buf[...] = jnp.zeros_like(grid_buf)
    for shift, block in enumerate(blocks):
        row = wrap(here_ref[0] - shift, row_count) * high + rim + 1
        grid_buf[pl.ds(row, high)] = block[...]
    rows = out_ref.shape[1] // wide
    window = grid_buf[pl.ds(here_ref[0] * high, rows + 2)].reshape((rows + 2) * wide, depth)
    for col_tap in range(3):
        total = dot(window[0 : rows * wide], weight_ref[0, col_tap])
        for row_tap in (1, 2):
            total = total + dot(
                window[row_tap * wide : (row_tap + rows) * wide], weight_ref[row_tap, col_tap]
            )
        out_ref[col_tap] = total


def neck_kernel(
    row_count, col_count, high, window_rows, here_ref, table_ref, turned_ref, weight_ref, bias_ref, taps_ref, *refs
):
    messages, refs = refs[:col_count], refs[col_count:]
    windows, (bins_buf, acc_buf, term_buf) = refs[:col_count], refs[col_count:]
    rows, span, channels = windows[0].shape
    wide = taps_ref.shape[1] // rows
    width4 = span - 2 * rim
    table = table_ref[...]
    cells = table.shape[0]
    bins = messages[0][window_rows : window_rows + cells, :].astype(f32)
    for message in messages[1:]:
        bins = bins + message[window_rows : window_rows + cells, :].astype(f32)
    bias = jnp.zeros((cells, channels), f32)
    for number in range(len(bin_sides)):
        bias = jnp.where(table[:, 0:1] == number, bias_ref[number : number + 1, :], bias)
    share = weight_ref.shape[2]
    first = here_ref[1] * share
    mine = table[:, 0:1] == (first // channels).astype(f32)
    bins_buf[...] = jnp.where(mine, jnp.maximum(bins + bias, 0.0), 0.0)
    if share == channels:
        binned = bins_buf[...]
    else:
        binned = bins_buf[:, pl.ds(pl.multiple_of(lax.rem(first, channels), 128), share)]
    place = lax.broadcasted_iota(jnp.int32, ((rows + 2) * wide, 1), 0).astype(f32)
    place_row = floor_div(place, wide)
    place_col = place - place_row * wide
    place_row = place_row + (here_ref[0] * high - rim - 1).astype(f32)
    grid_rows = float(high * row_count)
    sides = turned_ref[1:2, :]

    def weights(position, extent, index):
        source = (position + 0.5) * sides / extent - 0.5
        source = jnp.minimum(jnp.maximum(source, 0.0), sides - 1.0)
        return jnp.maximum(0.0, 1.0 - jnp.abs(source - index))

    spread = weights(place_row, grid_rows, turned_ref[2:3, :])
    spread = spread * weights(place_col, float(wide), turned_ref[3:4, :])
    spread = jnp.where((place_row >= 0.0) & (place_row < grid_rows), spread, 0.0)
    ppm = jnp.dot(spread, binned, precision=highest, preferred_element_type=f32).astype(bf16)
    size = rows * wide
    for col_tap in range(3):
        total = taps_ref[col_tap]
        for row_tap in range(3):
            total = total + dot(
                ppm[row_tap * wide : row_tap * wide + size], weight_ref[row_tap, col_tap]
            )
        acc_buf[col_tap, 8 : 8 + size, :] = total
    col = place_col[0:size]
    total = (
        acc_buf[1, 8 : 8 + size, :]
        + jnp.where(col > 0.0, acc_buf[0, 7 : 7 + size, :], 0.0)
        + jnp.where(col < wide - 1.0, acc_buf[2, 9 : 9 + size, :], 0.0)
    )
    term_buf[...] = jnp.zeros_like(term_buf)
    term_buf[:, rim : rim + wide, :] = total.reshape(rows, wide, channels)
    for shift, window in enumerate(windows):
        target = wrap(here_ref[1] + shift, col_count)
        window[...] = term_buf[:, pl.ds(pl.multiple_of(target * width4, 8), span), :].astype(bf16)


def rows_kernel(col_count, high3, wide3, here_ref, bias_ref, lat1_ref, lat2_ref, *refs):
    messages, (lat3_ref, low_ref, high_ref, three_buf, pack_buf) = refs[:col_count], refs[col_count:]
    span = wide3 + 2 * rim
    total = messages[0][0 : high3 * span, :].astype(f32)
    for message in messages[1:]:
        total = total + message[0 : high3 * span, :].astype(f32)
    total = jnp.maximum(total + bias_ref[7:8, :], 0.0)
    col_here = here_ref[1]
    place = lax.broadcasted_iota(jnp.int32, (span, 1), 0) + col_here * wide3 - rim
    inside = (place >= 0) & (place < wide3 * col_count)
    for row in range(high3):
        three_buf[row, :span, :] = jnp.where(inside, total[row * span : (row + 1) * span], 0.0)
    lat3_ref[...] = three_buf[:, :span, :].astype(bf16)
    high1, wide1 = lat1_ref.shape[:2]
    high2, wide2 = lat2_ref.shape[:2]
    before, after = messages[1], messages[col_count - 1]
    sides_at = before.shape[0] - rim * (high1 + high2)
    for out, last in ((low_ref, False), (high_ref, True)):
        start, at = 0, sides_at
        for lat, high, wide in ((lat1_ref, high1, wide1), (lat2_ref, high2, wide2)):
            whole = wide + 2 * rim
            first = high - rim if last else 0
            left = before[at + rim * first : at + rim * (first + rim), :].astype(f32)
            right = after[at + rim * first : at + rim * (first + rim), :].astype(f32)
            left = jnp.where(col_here > 0, left, 0.0)
            right = jnp.where(col_here < col_count - 1, right, 0.0)
            for step in range(rim):
                pack_buf[start : start + rim, :] = left[rim * step : rim * (step + 1)]
                pack_buf[start + rim : start + rim + wide, :] = lat[first + step].astype(f32)
                pack_buf[start + rim + wide : start + whole, :] = right[rim * step : rim * (step + 1)]
                start += whole
            at += rim * high
        for step in range(rim):
            row = high3 - rim + step if last else step
            pack_buf[start : start + span, :] = three_buf[row, :span, :]
            start += span
        out[...] = pack_buf[...].astype(bf16)


def stretch_matrix(out_shape, out_first, in_shape, in_first, factor, extent):
    out_rows, out_pitch = out_shape
    in_rows, in_pitch = in_shape
    place = lax.broadcasted_iota(jnp.int32, (1, in_rows * in_pitch), 1).astype(f32)
    place_row = floor_div(place, in_pitch)
    place_col = place - place_row * in_pitch

    def weights(length, first_out, first_in, targets, whole):
        output = first_out + lax.broadcasted_iota(jnp.int32, (length, 1), 0).astype(f32)
        source = (output + 0.5) * (1.0 / factor) - 0.5
        source = jnp.minimum(jnp.maximum(source, 0.0), whole - 1.0)
        inside = jnp.where((output >= 0.0) & (output < whole * factor), 1.0, 0.0)
        return jnp.maximum(0.0, 1.0 - jnp.abs(source - (first_in + targets))) * inside

    down = weights(out_rows, out_first[0], in_first[0], place_row, extent[0])
    across = weights(out_pitch, out_first[1], in_first[1], place_col, extent[1])
    matrix = down[:, None, :] * across[None, :, :]
    return matrix.astype(bf16).reshape(out_rows * out_pitch, in_rows * in_pitch)


def tail_kernel(
    sizes,
    top_count,
    here_ref,
    *refs,
):
    (high1, wide1), (high2, wide2), (high3, wide3), (high4, wide4), (row_count, col_count) = sizes
    top_refs, refs = refs[:top_count], refs[top_count:]
    (
        lat1_ref,
        lat2_ref,
        lat3_ref,
        above_ref,
        below_ref,
        before_ref,
        after_ref,
        bias_ref,
        smooth_hbm,
        join_hbm,
        out_ref,
        top_buf,
        lat1_buf,
        lat2_buf,
        lat3_buf,
        pyr1_buf,
        pyr2_buf,
        pyr3_buf,
        acc_buf,
        sums_buf,
        stack_buf,
        smooth_w,
        join_w,
        sems,
    ) = refs
    smooth_copy = pltpu.make_async_copy(smooth_hbm, smooth_w, sems.at[0])
    join_copy = pltpu.make_async_copy(join_hbm, join_w, sems.at[1])
    smooth_copy.start()
    join_copy.start()
    row_here = here_ref[0].astype(f32)
    col_here = here_ref[1].astype(f32)
    channels = bias_ref.shape[1]

    def firsts(high, wide, border):
        return row_here * high - border, col_here * wide - border

    def extent(high, wide):
        return float(high * row_count), float(wide * col_count)

    side_start = before_ref.shape[0] - rim * (high1 + high2)
    row_start = 0
    for ref, buf, high, wide in (
        (lat1_ref, lat1_buf, high1, wide1),
        (lat2_ref, lat2_buf, high2, wide2),
        (lat3_ref, lat3_buf, high3, wide3 + 2 * rim),
    ):
        buf[...] = jnp.zeros_like(buf)
        whole = wide
        if buf is lat3_buf:
            buf[rim : rim + high, :wide, :] = ref[...].astype(f32)
        else:
            whole = wide + 2 * rim
            buf[rim : rim + high, rim : rim + wide, :] = ref[...].astype(f32)
            for source, col, keep in (
                (before_ref, 0, here_ref[1] > 0),
                (after_ref, rim + wide, here_ref[1] < col_count - 1),
            ):
                sides = source[side_start : side_start + rim * high, :].astype(f32)
                sides = jnp.where(keep, sides, 0.0)
                for row in range(high):
                    buf[rim + row, col : col + rim, :] = sides[rim * row : rim * row + rim]
            side_start += rim * high
        for source, row in ((above_ref, 0), (below_ref, rim + high)):
            both = source[row_start : row_start + rim * whole, :].astype(f32)
            for step in range(rim):
                buf[row + step, :whole, :] = both[step * whole : (step + 1) * whole]
        row_start += rim * whole

    tall4, whole4 = high4 + 2 * rim, wide4 + 2 * rim
    top_sum = top_refs[0][...].astype(f32)
    for ref in top_refs[1:]:
        top_sum = top_sum + ref[...].astype(f32)
    top_buf[...] = jnp.zeros_like(top_buf)
    top_buf[:, :whole4, :] = jnp.maximum(top_sum + bias_ref[4:5, :][None], 0.0)
    pitch4 = top_buf.shape[1]
    top = top_buf[...].astype(bf16).reshape(tall4 * pitch4, channels)

    def pyramid(lat_buf, high, wide, source, source_shape, source_first, source_size):
        rows, pitch = lat_buf.shape[:2]
        matrix = stretch_matrix(
            (rows, pitch), firsts(high, wide, rim), source_shape, source_first, 2, extent(*source_size)
        )
        total = lat_buf[...].reshape(rows * pitch, channels) + dot(matrix, source)
        return total.astype(bf16)

    first4 = firsts(high4, wide4, rim)
    pyr3_buf[...] = pyramid(lat3_buf, high3, wide3, top, (tall4, pitch4), first4, (high4, wide4))
    shape3 = lat3_buf.shape[:2]
    pyr2_buf[...] = pyramid(
        lat2_buf, high2, wide2, pyr3_buf[...], shape3, firsts(high3, wide3, rim), (high3, wide3)
    )
    shape2 = lat2_buf.shape[:2]
    pyr1_buf[...] = pyramid(
        lat1_buf, high1, wide1, pyr2_buf[...], shape2, firsts(high2, wide2, rim), (high2, wide2)
    )
    shape1 = lat1_buf.shape[:2]
    smooth_copy.wait()

    def conv(source, shape, weight_at, rows):
        pitch = shape[1]
        span = rows * pitch
        for col_tap in range(3):
            total = dot(source[0:span, :], weight_at(0, col_tap))
            for row_tap in (1, 2):
                total = total + dot(
                    source[row_tap * pitch : row_tap * pitch + span, :], weight_at(row_tap, col_tap)
                )
            yield col_tap, total.reshape(rows, pitch, channels)

    def smooth(number, source, shape, wide):
        rows, pitch = shape[0] - 2, shape[1]
        for col_tap, total in conv(
            source, shape, lambda i, j: smooth_w[number, i, j], rows
        ):
            acc_buf[col_tap, :rows, :pitch, :] = total
        whole = wide + 2
        total = (
            acc_buf[0, :rows, 0:whole, :]
            + acc_buf[1, :rows, 1 : whole + 1, :]
            + acc_buf[2, :rows, 2 : whole + 2, :]
        )
        return jnp.maximum(total + bias_ref[8 + number : 9 + number, :][None], 0.0)

    def smooth_flat(number, source, shape, wide):
        rows, pitch = shape[0] - 2, shape[1]
        value = smooth(number, source, shape, wide)
        sums_buf[:rows, :pitch, :] = jnp.zeros((rows, pitch, channels), f32)
        sums_buf[:rows, : wide + 2, :] = value
        return sums_buf[:rows, :pitch, :].astype(bf16).reshape(rows * pitch, channels)

    rows1, pitch1 = shape1[0] - 2, shape1[1]
    out_first = firsts(high1, wide1, 1)

    def raise_to_one(source, source_shape, source_first, factor, source_size):
        matrix = stretch_matrix(
            (rows1, pitch1), out_first, source_shape, source_first, factor, extent(*source_size)
        )
        return dot(matrix, source).astype(bf16)

    stack_buf[:, 3 * channels : 4 * channels] = raise_to_one(
        top, (tall4, pitch4), first4, 8, (high4, wide4)
    )
    smooth3 = smooth_flat(2, pyr3_buf, shape3, wide3)
    stack_buf[:, 2 * channels : 3 * channels] = raise_to_one(
        smooth3, (shape3[0] - 2, shape3[1]), firsts(high3, wide3, 1), 4, (high3, wide3)
    )
    smooth2 = smooth_flat(1, pyr2_buf, shape2, wide2)
    stack_buf[:, channels : 2 * channels] = raise_to_one(
        smooth2, (shape2[0] - 2, shape2[1]), firsts(high2, wide2, 1), 2, (high2, wide2)
    )
    value = smooth(0, pyr1_buf, shape1, wide1)
    down = out_first[0] + lax.broadcasted_iota(jnp.int32, (rows1, 1, 1), 0).astype(f32)
    across = out_first[1] + lax.broadcasted_iota(jnp.int32, (1, wide1 + 2, 1), 1).astype(f32)
    tall, broad = extent(high1, wide1)
    inside = (down >= 0.0) & (down < tall) & (across >= 0.0) & (across < broad)
    sums_buf[:rows1, : wide1 + 2, :] = jnp.where(inside, value, 0.0)
    stack_buf[:, 0:channels] = sums_buf[...].astype(bf16).reshape(rows1 * pitch1, channels)
    join_copy.wait()
    shape_join = (rows1, pitch1)
    for col_tap, total in conv(stack_buf, shape_join, lambda i, j: join_w[i, j], high1):
        acc_buf[col_tap, :high1] = total
    total = (
        acc_buf[0, :high1, 0:wide1, :]
        + acc_buf[1, :high1, 1 : wide1 + 1, :]
        + acc_buf[2, :high1, 2 : wide1 + 2, :]
    )
    out_ref[...] = jnp.maximum(total + bias_ref[11:12, :][None], 0.0).astype(bf16)


def pitch_of(width):
    return (width + 15) // 16 * 16


def tail(here, tops, lats, above, below, before, after, biases, smooth_weight, join_weight, sizes):
    (high1, wide1), (high2, wide2), (high3, wide3), (high4, wide4), _ = sizes
    channels = biases.shape[1]

    def window(high, wide):
        return high + 2 * rim, pitch_of(wide + 2 * rim)

    shapes = [window(high, wide) for high, wide in sizes[:4]]
    (rows1, pitch1), (rows2, pitch2), (rows3, pitch3), (rows4, pitch4) = shapes
    return pl.pallas_call(
        functools.partial(tail_kernel, sizes, len(tops)),
        out_shape=jax.ShapeDtypeStruct((high1, wide1, channels), bf16),
        in_specs=[smem_spec]
        + [vmem_spec] * (len(tops) + 8)
        + [hbm_spec] * 2,
        out_specs=vmem_spec,
        scratch_shapes=[
            pltpu.VMEM((rows4, pitch4, channels), f32),
            pltpu.VMEM((rows1, pitch1, channels), f32),
            pltpu.VMEM((rows2, pitch2, channels), f32),
            pltpu.VMEM((rows3, pitch3, channels), f32),
            pltpu.VMEM((rows1 * pitch1, channels), bf16),
            pltpu.VMEM((rows2 * pitch2, channels), bf16),
            pltpu.VMEM((rows3 * pitch3, channels), bf16),
            pltpu.VMEM((3, rows1 - 2, pitch1, channels), f32),
            pltpu.VMEM((rows1 - 2, pitch1, channels), f32),
            pltpu.VMEM(((rows1 - 2) * pitch1, 4 * channels), bf16),
            pltpu.VMEM(smooth_weight.shape, bf16),
            pltpu.VMEM(join_weight.shape, bf16),
            pltpu.SemaphoreType.DMA((2,)),
        ],
        compiler_params=pltpu.CompilerParams(vmem_limit_bytes=44 * 1024 * 1024),
        cost_estimate=pl.CostEstimate(
            flops=10_000_000_000, bytes_accessed=12_000_000, transcendentals=0
        ),
    )(
        here,
        *tops,
        *lats,
        above,
        below,
        before,
        after,
        biases,
        in_hbm(smooth_weight),
        in_hbm(join_weight),
    )


def local(
    level_one,
    level_two,
    level_three,
    level_four,
    bin_weight,
    neck_feature,
    neck_pooled,
    lateral_one,
    lateral_two,
    lateral_three,
    smooth_weight,
    join_weight,
    biases,
):
    row_count = lax.axis_size("row")
    col_count = lax.axis_size("col")
    here = jnp.stack([lax.axis_index("row"), lax.axis_index("col")]).astype(jnp.int32)
    high1, wide1 = level_one.shape[:2]
    high2, wide2 = level_two.shape[:2]
    high3, wide3 = level_three.shape[0], level_three.shape[1] // col_count
    high4, grid_cols, part_four = level_four.shape
    wide4 = grid_cols // col_count
    channels = bin_weight.shape[2]
    grid_rows = high4 * row_count
    table = cell_table(grid_rows, grid_cols)
    cells = table.shape[0]
    turned = jnp.asarray(np.ascontiguousarray(table.T))
    table = jnp.asarray(table)

    def shape(dims, kind=bf16):
        return jax.ShapeDtypeStruct(dims, kind)

    others = [shifted(level_four, "row", shift) for shift in range(1, row_count)]
    window_rows = high3 * (wide3 + 2 * rim)
    side_rows = rim * (high1 + high2)
    used = (level_one, lateral_one, level_two, lateral_two, level_three, lateral_three)
    kept = (biases, level_four, table, bin_weight, turned, neck_feature, neck_pooled)
    lat1, lat2, *rest = call(
        functools.partial(lateral_kernel, col_count, len(kept)),
        [shape((high1, wide1, channels)), shape((high2, wide2, channels))]
        + [shape((window_rows + side_rows, channels))] * col_count
        + [shape(value.shape, value.dtype) for value in kept],
        [smem_spec] + [hbm_spec] * (len(used) + len(kept)),
        [pltpu.VMEM(value.shape, value.dtype) for value in used]
        + [
            pltpu.VMEM((high3, level_three.shape[1] + 8, channels), f32),
            pltpu.VMEM((high1, wide1, channels), f32),
            pltpu.VMEM((high2, wide2, channels), f32),
            pltpu.VMEM((window_rows + side_rows, channels), f32),
            pltpu.SemaphoreType.DMA((len(used) + len(kept),)),
        ],
        300_000_000,
        8_000_000,
    )(here, *(in_hbm(value) for value in (*used, *kept)))
    pieces = rest[:col_count]
    bias_table, level_four, table, bin_weight, turned, neck_feature, neck_pooled = rest[col_count:]
    blocks = [level_four] + others
    near = (1, col_count - 1)
    messages = call(
        functools.partial(bins_kernel, row_count, col_count, window_rows),
        [
            shape((window_rows + cells + (side_rows if shift in near else 0), channels))
            for shift in range(col_count)
        ],
        [smem_spec] + [vmem_spec] * (2 + row_count + col_count),
        [],
        100_000_000,
        1_000_000,
    )(here, table, bin_weight, *blocks, *pieces)

    received = [messages[0]] + [
        shifted(messages[shift], "col", shift) for shift in range(1, col_count)
    ]
    rows = high4 + 2 * rim
    taps = call(
        functools.partial(feature_kernel, row_count),
        shape((3, rows * grid_cols, channels), f32),
        [smem_spec] + [vmem_spec] * (1 + row_count),
        [pltpu.VMEM((grid_rows + 2 * rim + 2, grid_cols, part_four), bf16)],
        700_000_000,
        3_000_000,
    )(here, neck_feature, *blocks)
    span4 = wide4 + 2 * rim
    windows = call(
        functools.partial(neck_kernel, row_count, col_count, high4, window_rows),
        [shape((rows, span4, channels))] * col_count,
        [smem_spec] + [vmem_spec] * (5 + col_count),
        [
            pltpu.VMEM((cells, channels), f32),
            pltpu.VMEM((3, rows * grid_cols + 16, channels), f32),
            pltpu.VMEM((rows, grid_cols + 16, channels), f32),
        ],
        300_000_000,
        3_000_000,
    )(here, table, turned, neck_pooled, bias_table, taps, *received)

    tops = [windows[0]] + [shifted(windows[shift], "col", shift) for shift in range(1, col_count)]
    span3 = wide3 + 2 * rim
    packed = rim * (wide1 + wide2 + wide3 + 6 * rim)
    lat3, low_rows, high_rows = call(
        functools.partial(rows_kernel, col_count, high3, wide3),
        [shape((high3, span3, channels))] + [shape((packed, channels))] * 2,
        [smem_spec] + [vmem_spec] * (3 + col_count),
        [
            pltpu.VMEM((high3, (span3 + 7) // 8 * 8, channels), f32),
            pltpu.VMEM((packed, channels), f32),
        ],
        1_000_000,
        1_000_000,
    )(here, bias_table, lat1, lat2, *received)
    above, below = edge_swap(low_rows, high_rows, "row")
    sizes = (
        (high1, wide1),
        (high2, wide2),
        (high3, wide3),
        (high4, wide4),
        (row_count, col_count),
    )
    return tail(
        here,
        tops,
        (lat1, lat2, lat3),
        above,
        below,
        received[1],
        received[-1],
        bias_table,
        smooth_weight,
        join_weight,
        sizes,
    )


def solution(mesh):
    placed = (
        P(("grp", "row"), "col", None),
        P(("grp", "row"), "col", None),
        P(("grp", "row"), None, "col"),
        P(("grp", "row"), None, "col"),
        P(None, "col", None),
        P(None, None, "col", None),
        P(None, None, "col", None),
        P(),
        P(),
        P(),
        P(),
        P(),
        P(),
    )
    return jax.shard_map(
        local, mesh=mesh, in_specs=placed, out_specs=P(("grp", "row"), "col", None), check_vma=False
    )
```

```python
import functools

import jax
import jax.numpy as jnp
import numpy as np
from jax import lax
from jax.experimental import pallas as pl
from jax.experimental.pallas import tpu as pltpu
from jax.sharding import PartitionSpec as P

highest = lax.Precision.HIGHEST
bin_sides = (1, 2, 3, 6)
rim = 2
f32 = jnp.float32
bf16 = jnp.bfloat16
vmem_spec = pl.BlockSpec(memory_space=pltpu.VMEM)
hbm_spec = pl.BlockSpec(memory_space=pltpu.HBM)
smem_spec = pl.BlockSpec(memory_space=pltpu.SMEM)
params = pltpu.CompilerParams(vmem_limit_bytes=30 * 1024 * 1024)


def shifted(value, axis, shift):
    count = lax.axis_size(axis)
    return lax.ppermute(value, axis, [(i, (i + shift) % count) for i in range(count)])


def edge_swap(low_out, high_out, axis):
    count = lax.axis_size(axis)
    forward = [(i, i + 1) for i in range(count - 1)]
    backward = [(target, source) for source, target in forward]
    return lax.ppermute(high_out, axis, forward), lax.ppermute(low_out, axis, backward)


def cell_table(extent_rows, extent_cols):
    rows = []
    for number, side in enumerate(bin_sides):
        for i in range(side):
            for j in range(side):
                top, low = i * extent_rows // side, -(-(i + 1) * extent_rows // side)
                left, right = j * extent_cols // side, -(-(j + 1) * extent_cols // side)
                rows.append([number, side, i, j, top, low, left, right, (low - top) * (right - left)])
    padded = (len(rows) + 15) // 16 * 16
    table = np.zeros((padded, 16), np.float32)
    table[:, 0] = -1.0
    table[:, 1] = 1.0
    table[:, 8] = 1.0
    table[: len(rows), :9] = np.array(rows, np.float32)
    return table


def dot(a, b):
    return jnp.dot(a, b, preferred_element_type=f32)


def in_hbm(value):
    return pltpu.with_memory_space_constraint(value, pltpu.HBM)


def call(kernel, outs, specs, scratch, flops, moved):
    return pl.pallas_call(
        kernel,
        out_shape=outs,
        in_specs=specs,
        out_specs=jax.tree.map(lambda _: vmem_spec, outs),
        scratch_shapes=scratch,
        compiler_params=params,
        cost_estimate=pl.CostEstimate(flops=flops, bytes_accessed=moved, transcendentals=0),
    )


def wrap(value, count):
    return lax.rem(value + count, count)


def floor_div(value, step):
    return jnp.floor((value + 0.5) / step)


def stretch_matrix(here, out_shape, out_border, in_shape, in_border, factor, out_size, in_size, counts, lanes, taps=1):
    out_rows, out_pitch = out_shape
    lane = lax.broadcasted_iota(jnp.int32, (1, lanes * taps * taps), 1).astype(f32)
    tap = floor_div(lane, lanes)
    place = lane - tap * lanes
    row_tap = floor_div(tap, taps)
    col_tap = tap - row_tap * taps
    place_row = floor_div(place, in_shape[1])
    place_col = place - place_row * in_shape[1]

    def weights(axis, length, targets, tap_here):
        whole = float(in_size[axis] * counts[axis])
        first_out = (here[axis] * out_size[axis] - out_border).astype(f32) - (taps // 2)
        first_in = (here[axis] * in_size[axis] - in_border).astype(f32)
        output = first_out + tap_here + lax.broadcasted_iota(jnp.int32, (length, 1), 0).astype(f32)
        source = (output + 0.5) * (1.0 / factor) - 0.5
        source = jnp.minimum(jnp.maximum(source, 0.0), whole - 1.0)
        inside = jnp.where((output >= 0.0) & (output < whole * factor), 1.0, 0.0)
        return jnp.maximum(0.0, 1.0 - jnp.abs(source - (first_in + targets))) * inside

    down = weights(0, out_rows, place_row, row_tap)
    across = weights(1, out_pitch, place_col, col_tap)
    matrix = down[:, None, :] * across[None, :, :]
    return matrix.astype(bf16).reshape(out_rows * out_pitch, -1)


def pitch_of(width):
    return (width + 15) // 16 * 16


def window_shape(size, border):
    return size[0] + 2 * border, pitch_of(size[1] + 2 * border)


def compact_shape(size, border):
    return size[0] + 2 * border, size[1] + 2 * border


def stretches(sizes):
    one, two, three, four, counts = sizes

    def matrix(out, out_border, source, in_border, compact=False):
        factor = out[0] // source[0]
        if compact:
            shape = compact_shape(source, in_border)
            return (out, out_border, shape, in_border, factor, out, source, counts, pitch_of(shape[0] * shape[1]), 3)
        shape = window_shape(source, in_border)
        return (window_shape(out, out_border), out_border, shape, in_border, factor, out, source, counts, shape[0] * shape[1], 1)

    return (
        matrix(three, rim, four, rim),
        matrix(two, rim, three, rim),
        matrix(one, rim, two, rim),
        matrix(one, 1, two, 1),
        matrix(one, 0, three, 1, True),
        matrix(one, 0, four, 1, True),
    )


def lateral_kernel(col_count, kept_count, here_ref, *refs):
    sources, refs = refs[: 6 + kept_count], refs[6 + kept_count :]
    (lat1_ref, lat2_ref), refs = refs[:2], refs[2:]
    pieces, refs = refs[:col_count], refs[col_count:]
    kept, refs = refs[:kept_count], refs[kept_count:]
    fetched, (wide_buf, one_buf, two_buf, piece_buf, sems) = refs[:6], refs[6:]
    copies = [
        pltpu.make_async_copy(source, target, sems.at[number])
        for number, (source, target) in enumerate(zip(sources, (*fetched, *kept)))
    ]
    for copy in copies:
        copy.start()
    one_ref, w1_ref, two_ref, w2_ref, three_ref, w3_ref = fetched
    bias_ref = kept[0]
    copies[6].wait()
    channels = w1_ref.shape[1]
    for number, (source, weight, row, buf, out) in enumerate(
        (
            (one_ref, w1_ref, 5, one_buf, lat1_ref),
            (two_ref, w2_ref, 6, two_buf, lat2_ref),
        )
    ):
        copies[2 * number].wait()
        copies[2 * number + 1].wait()
        high, wide, depth = source.shape
        value = dot(source[...].reshape(high * wide, depth), weight[...])
        value = jnp.maximum(value + bias_ref[row : row + 1, :], 0.0).reshape(high, wide, channels)
        buf[...] = value
        out[...] = value.astype(bf16)
    high3, whole3, share = three_ref.shape
    wide3 = whole3 // col_count
    col_here = here_ref[1]
    copies[4].wait()
    copies[5].wait()
    weight = w3_ref[pl.ds(pl.multiple_of(col_here * share, 16), share), :]
    value = dot(three_ref[...].reshape(high3 * whole3, share), weight)
    wide_buf[...] = jnp.zeros_like(wide_buf)
    wide_buf[:, rim : rim + whole3, :] = value.reshape(high3, whole3, channels)
    span = wide3 + 2 * rim
    for shift, piece in enumerate(pieces):
        target = wrap(col_here + shift, col_count)
        for row in range(high3):
            piece_buf[row * span : (row + 1) * span, :] = wide_buf[
                row, pl.ds(pl.multiple_of(target * wide3, 8), span), :
            ]
        start = high3 * span
        for buf in (one_buf, two_buf):
            high, wide = buf.shape[:2]
            first = wide - rim if shift == 1 else 0
            for row in range(high):
                piece_buf[start : start + rim, :] = buf[row, first : first + rim, :]
                start += rim
        piece[...] = piece_buf[...].astype(bf16)
    for copy in copies[7:]:
        copy.wait()


def bins_kernel(row_count, col_count, window_rows, here_ref, table_ref, weight_ref, *refs):
    blocks, pieces, messages = (
        refs[:row_count],
        refs[row_count : row_count + col_count],
        refs[row_count + col_count :],
    )
    table = table_ref[...]
    high, wide, depth = blocks[0].shape
    place = lax.broadcasted_iota(jnp.int32, (1, high * wide), 1).astype(f32)
    place_row = floor_div(place, wide)
    place_col = place - place_row * wide
    in_cols = (place_col >= table[:, 6:7]) & (place_col < table[:, 7:8])
    pooled = None
    for shift, block in enumerate(blocks):
        row = place_row + (wrap(here_ref[0] - shift, row_count) * high).astype(f32)
        inside = in_cols & (row >= table[:, 4:5]) & (row < table[:, 5:6])
        inside = jnp.where(inside, 1.0, 0.0).astype(bf16)
        term = dot(inside, block[...].reshape(high * wide, depth))
        pooled = term if pooled is None else pooled + term
    pooled = (pooled / table[:, 8:9]).astype(bf16)
    bins = None
    for number in range(len(bin_sides)):
        term = jnp.where(table[:, 0:1] == number, dot(pooled, weight_ref[number]), 0.0)
        bins = term if bins is None else bins + term
    bins = bins.astype(bf16)
    cells = bins.shape[0]
    for piece, message in zip(pieces, messages):
        message[0:window_rows, :] = piece[0:window_rows, :]
        message[window_rows : window_rows + cells, :] = bins
        if message.shape[0] > window_rows + cells:
            message[window_rows + cells :, :] = piece[window_rows:, :]


def feature_kernel(row_count, plans, here_ref, weight_hbm, *refs):
    blocks, refs = refs[:row_count], refs[row_count:]
    late, refs = refs[:3], refs[3:]
    out_ref, kept, matrices = refs[0], refs[1:4], refs[4 : 4 + len(plans)]
    weight_ref, grid_buf, sems = refs[4 + len(plans) :]
    copies = [
        pltpu.make_async_copy(source, target, sems.at[number])
        for number, (source, target) in enumerate(zip((weight_hbm, *late), (weight_ref, *kept)))
    ]
    for copy in copies:
        copy.start()
    here = (here_ref[0], here_ref[1])
    for plan, matrix in zip(plans, matrices):
        matrix[...] = stretch_matrix(here, *plan)
    high, wide, depth = blocks[0].shape
    grid_buf[...] = jnp.zeros_like(grid_buf)
    for shift, block in enumerate(blocks):
        row = wrap(here_ref[0] - shift, row_count) * high + rim + 1
        grid_buf[pl.ds(row, high)] = block[...]
    rows = out_ref.shape[1] // wide
    window = grid_buf[pl.ds(here_ref[0] * high, rows + 2)].reshape((rows + 2) * wide, depth)
    copies[0].wait()
    for col_tap in range(3):
        total = dot(window[0 : rows * wide], weight_ref[0, col_tap])
        for row_tap in (1, 2):
            total = total + dot(
                window[row_tap * wide : (row_tap + rows) * wide], weight_ref[row_tap, col_tap]
            )
        out_ref[col_tap] = total
    for copy in copies[1:]:
        copy.wait()


def neck_kernel(
    row_count, col_count, high, window_rows, here_ref, table_ref, turned_ref, weight_ref, bias_ref, taps_ref, *refs
):
    messages, refs = refs[:col_count], refs[col_count:]
    windows, (bins_buf, acc_buf, term_buf) = refs[:col_count], refs[col_count:]
    rows, span, channels = windows[0].shape
    wide = taps_ref.shape[1] // rows
    width4 = span - 2 * rim
    table = table_ref[...]
    cells = table.shape[0]
    bins = messages[0][window_rows : window_rows + cells, :].astype(f32)
    for message in messages[1:]:
        bins = bins + message[window_rows : window_rows + cells, :].astype(f32)
    bias = jnp.zeros((cells, channels), f32)
    for number in range(len(bin_sides)):
        bias = jnp.where(table[:, 0:1] == number, bias_ref[number : number + 1, :], bias)
    share = weight_ref.shape[2]
    first = here_ref[1] * share
    mine = table[:, 0:1] == (first // channels).astype(f32)
    bins_buf[...] = jnp.where(mine, jnp.maximum(bins + bias, 0.0), 0.0)
    if share == channels:
        binned = bins_buf[...]
    else:
        binned = bins_buf[:, pl.ds(pl.multiple_of(lax.rem(first, channels), 128), share)]
    place = lax.broadcasted_iota(jnp.int32, ((rows + 2) * wide, 1), 0).astype(f32)
    place_row = floor_div(place, wide)
    place_col = place - place_row * wide
    place_row = place_row + (here_ref[0] * high - rim - 1).astype(f32)
    grid_rows = float(high * row_count)
    sides = turned_ref[1:2, :]

    def weights(position, extent, index):
        source = (position + 0.5) * sides / extent - 0.5
        source = jnp.minimum(jnp.maximum(source, 0.0), sides - 1.0)
        return jnp.maximum(0.0, 1.0 - jnp.abs(source - index))

    spread = weights(place_row, grid_rows, turned_ref[2:3, :])
    spread = spread * weights(place_col, float(wide), turned_ref[3:4, :])
    spread = jnp.where((place_row >= 0.0) & (place_row < grid_rows), spread, 0.0)
    ppm = jnp.dot(spread, binned, precision=highest, preferred_element_type=f32).astype(bf16)
    size = rows * wide
    for col_tap in range(3):
        total = taps_ref[col_tap]
        for row_tap in range(3):
            total = total + dot(
                ppm[row_tap * wide : row_tap * wide + size], weight_ref[row_tap, col_tap]
            )
        acc_buf[col_tap, 8 : 8 + size, :] = total
    col = place_col[0:size]
    total = (
        acc_buf[1, 8 : 8 + size, :]
        + jnp.where(col > 0.0, acc_buf[0, 7 : 7 + size, :], 0.0)
        + jnp.where(col < wide - 1.0, acc_buf[2, 9 : 9 + size, :], 0.0)
    )
    term_buf[...] = jnp.zeros_like(term_buf)
    term_buf[:, rim : rim + wide, :] = total.reshape(rows, wide, channels)
    for shift, window in enumerate(windows):
        target = wrap(here_ref[1] + shift, col_count)
        window[...] = term_buf[:, pl.ds(pl.multiple_of(target * width4, 8), span), :].astype(bf16)


def rows_kernel(col_count, high3, wide3, here_ref, bias_ref, lat1_ref, lat2_ref, *refs):
    messages, (lat3_ref, low_ref, high_ref, three_buf, pack_buf) = refs[:col_count], refs[col_count:]
    span = wide3 + 2 * rim
    total = messages[0][0 : high3 * span, :].astype(f32)
    for message in messages[1:]:
        total = total + message[0 : high3 * span, :].astype(f32)
    total = jnp.maximum(total + bias_ref[7:8, :], 0.0)
    col_here = here_ref[1]
    place = lax.broadcasted_iota(jnp.int32, (span, 1), 0) + col_here * wide3 - rim
    inside = (place >= 0) & (place < wide3 * col_count)
    for row in range(high3):
        three_buf[row, :span, :] = jnp.where(inside, total[row * span : (row + 1) * span], 0.0)
    lat3_ref[...] = three_buf[:, :span, :].astype(bf16)
    high1, wide1 = lat1_ref.shape[:2]
    high2, wide2 = lat2_ref.shape[:2]
    before, after = messages[1], messages[col_count - 1]
    sides_at = before.shape[0] - rim * (high1 + high2)
    for out, last in ((low_ref, False), (high_ref, True)):
        start, at = 0, sides_at
        for lat, high, wide in ((lat1_ref, high1, wide1), (lat2_ref, high2, wide2)):
            whole = wide + 2 * rim
            first = high - rim if last else 0
            left = before[at + rim * first : at + rim * (first + rim), :].astype(f32)
            right = after[at + rim * first : at + rim * (first + rim), :].astype(f32)
            left = jnp.where(col_here > 0, left, 0.0)
            right = jnp.where(col_here < col_count - 1, right, 0.0)
            for step in range(rim):
                pack_buf[start : start + rim, :] = left[rim * step : rim * (step + 1)]
                pack_buf[start + rim : start + rim + wide, :] = lat[first + step].astype(f32)
                pack_buf[start + rim + wide : start + whole, :] = right[rim * step : rim * (step + 1)]
                start += whole
            at += rim * high
        for step in range(rim):
            row = high3 - rim + step if last else step
            pack_buf[start : start + span, :] = three_buf[row, :span, :]
            start += span
        out[...] = pack_buf[...].astype(bf16)


def tail_kernel(
    sizes,
    top_count,
    here_ref,
    *refs,
):
    (high1, wide1), (high2, wide2), (high3, wide3), (high4, wide4), (row_count, col_count) = sizes
    top_refs, refs = refs[:top_count], refs[top_count:]
    (
        lat1_ref,
        lat2_ref,
        lat3_ref,
        above_ref,
        below_ref,
        before_ref,
        after_ref,
        bias_ref,
        smooth_w,
        join_w,
        up3_ref,
        up2_ref,
        up1_ref,
        raise2_ref,
        spread3_ref,
        spread4_ref,
        out_ref,
        top_buf,
        lat1_buf,
        lat2_buf,
        lat3_buf,
        pyr1_buf,
        pyr2_buf,
        pyr3_buf,
        acc_buf,
        sums_buf,
        stack_buf,
        small3_buf,
        small4_buf,
        terms3_buf,
        terms4_buf,
    ) = refs
    channels = bias_ref.shape[1]

    side_start = before_ref.shape[0] - rim * (high1 + high2)
    row_start = 0
    for ref, buf, high, wide in (
        (lat1_ref, lat1_buf, high1, wide1),
        (lat2_ref, lat2_buf, high2, wide2),
        (lat3_ref, lat3_buf, high3, wide3 + 2 * rim),
    ):
        buf[...] = jnp.zeros_like(buf)
        whole = wide
        if buf is lat3_buf:
            buf[rim : rim + high, :wide, :] = ref[...].astype(f32)
        else:
            whole = wide + 2 * rim
            buf[rim : rim + high, rim : rim + wide, :] = ref[...].astype(f32)
            for source, col, keep in (
                (before_ref, 0, here_ref[1] > 0),
                (after_ref, rim + wide, here_ref[1] < col_count - 1),
            ):
                sides = source[side_start : side_start + rim * high, :].astype(f32)
                sides = jnp.where(keep, sides, 0.0)
                for row in range(high):
                    buf[rim + row, col : col + rim, :] = sides[rim * row : rim * row + rim]
            side_start += rim * high
        for source, row in ((above_ref, 0), (below_ref, rim + high)):
            both = source[row_start : row_start + rim * whole, :].astype(f32)
            for step in range(rim):
                buf[row + step, :whole, :] = both[step * whole : (step + 1) * whole]
        row_start += rim * whole

    tall4, whole4 = high4 + 2 * rim, wide4 + 2 * rim
    top_sum = top_refs[0][...].astype(f32)
    for ref in top_refs[1:]:
        top_sum = top_sum + ref[...].astype(f32)
    top_buf[...] = jnp.zeros_like(top_buf)
    top_buf[:, :whole4, :] = jnp.maximum(top_sum + bias_ref[4:5, :][None], 0.0)
    pitch4 = top_buf.shape[1]
    top = top_buf[...].astype(bf16).reshape(tall4 * pitch4, channels)

    shape1, shape2, shape3 = lat1_buf.shape[:2], lat2_buf.shape[:2], lat3_buf.shape[:2]
    for lat_buf, matrix, source, out in (
        (lat3_buf, up3_ref, None, pyr3_buf),
        (lat2_buf, up2_ref, pyr3_buf, pyr2_buf),
        (lat1_buf, up1_ref, pyr2_buf, pyr1_buf),
    ):
        source = top if source is None else source[...]
        total = lat_buf[...].reshape(-1, channels) + dot(matrix[...], source)
        out[...] = total.astype(bf16)

    def conv(source, shape, weight_at, rows):
        pitch = shape[1]
        span = rows * pitch
        stacked = jnp.concatenate(
            [source[row_tap * pitch : row_tap * pitch + span, :] for row_tap in range(3)], axis=1
        )
        for col_tap in range(3):
            weight = weight_at(col_tap)
            total = dot(stacked, weight.reshape(-1, channels))
            acc_buf[col_tap, :rows, :pitch, :] = total.reshape(rows, pitch, channels)

    def taps_total(rows, whole):
        total = acc_buf[0, :rows, 0:whole, :]
        for col_tap in (1, 2):
            total = total + acc_buf[col_tap, :rows, col_tap : whole + col_tap, :]
        return total

    def smooth(number, source, shape, wide):
        rows = shape[0] - 2
        conv(source, shape, lambda j: smooth_w[number, :, j], rows)
        total = taps_total(rows, wide + 2)
        return jnp.maximum(total + bias_ref[8 + number : 9 + number, :][None], 0.0)

    def tap_terms(source, first, buf):
        lanes = source.shape[0]
        small = source[...].astype(bf16)
        for tap in range(9):
            weight = join_w[tap // 3, tap % 3, first : first + channels, :]
            buf[tap * lanes : (tap + 1) * lanes, :] = dot(small, weight).astype(bf16)

    tall, broad = compact_shape((high4, wide4), 1)
    small4_buf[...] = jnp.zeros_like(small4_buf)
    for row in range(tall):
        small4_buf[row * broad : (row + 1) * broad, :] = top_buf[row + rim - 1, rim - 1 : rim - 1 + broad, :]
    tap_terms(small4_buf, 3 * channels, terms4_buf)
    value = smooth(2, pyr3_buf, shape3, wide3)
    tall, broad = compact_shape((high3, wide3), 1)
    small3_buf[...] = jnp.zeros_like(small3_buf)
    for row in range(tall):
        small3_buf[row * broad : (row + 1) * broad, :] = value[row]
    tap_terms(small3_buf, 2 * channels, terms3_buf)

    rows2, pitch2 = window_shape((high2, wide2), 1)
    value = smooth(1, pyr2_buf, shape2, wide2)
    sums_buf[:rows2, :pitch2, :] = jnp.zeros((rows2, pitch2, channels), f32)
    sums_buf[:rows2, : wide2 + 2, :] = value
    smooth2 = sums_buf[:rows2, :pitch2, :].astype(bf16).reshape(rows2 * pitch2, channels)
    stack_buf[:, channels : 2 * channels] = dot(raise2_ref[...], smooth2).astype(bf16)

    rows1, pitch1 = window_shape((high1, wide1), 1)
    value = smooth(0, pyr1_buf, shape1, wide1)
    down = here_ref[0] * high1 - 1 + lax.broadcasted_iota(jnp.int32, (rows1, 1, 1), 0)
    across = here_ref[1] * wide1 - 1 + lax.broadcasted_iota(jnp.int32, (1, wide1 + 2, 1), 1)
    inside = (down >= 0) & (down < high1 * row_count) & (across >= 0) & (across < wide1 * col_count)
    sums_buf[:rows1, : wide1 + 2, :] = jnp.where(inside, value, 0.0)
    stack_buf[:, 0:channels] = sums_buf[...].astype(bf16).reshape(rows1 * pitch1, channels)
    conv(stack_buf, (rows1, pitch1), lambda j: join_w[:, j, 0 : 2 * channels], high1)
    total = taps_total(high1, wide1)
    spread = dot(spread3_ref[...], terms3_buf[...]) + dot(spread4_ref[...], terms4_buf[...])
    total = total + spread.reshape(high1, wide1, channels)
    out_ref[...] = jnp.maximum(total + bias_ref[11:12, :][None], 0.0).astype(bf16)


def tail(here, tops, lats, above, below, before, after, biases, weights, matrices, sizes):
    one, _, _, _, _ = sizes
    channels = biases.shape[1]
    shapes = [window_shape(size, rim) for size in sizes[:4]]
    (rows1, pitch1), (rows2, pitch2), (rows3, pitch3), (rows4, pitch4) = shapes
    small3, small4 = (matrix.shape[1] // 9 for matrix in matrices[-2:])
    inputs = (*tops, *lats, above, below, before, after, biases, *weights, *matrices)
    return pl.pallas_call(
        functools.partial(tail_kernel, sizes, len(tops)),
        out_shape=jax.ShapeDtypeStruct((*one, channels), bf16),
        in_specs=[smem_spec] + [vmem_spec] * len(inputs),
        out_specs=vmem_spec,
        scratch_shapes=[
            pltpu.VMEM((rows4, pitch4, channels), f32),
            pltpu.VMEM((rows1, pitch1, channels), f32),
            pltpu.VMEM((rows2, pitch2, channels), f32),
            pltpu.VMEM((rows3, pitch3, channels), f32),
            pltpu.VMEM((rows1 * pitch1, channels), bf16),
            pltpu.VMEM((rows2 * pitch2, channels), bf16),
            pltpu.VMEM((rows3 * pitch3, channels), bf16),
            pltpu.VMEM((3, rows1 - 2, pitch1, channels), f32),
            pltpu.VMEM((rows1 - 2, pitch1, channels), f32),
            pltpu.VMEM(((rows1 - 2) * pitch1, 2 * channels), bf16),
            pltpu.VMEM((small3, channels), f32),
            pltpu.VMEM((small4, channels), f32),
            pltpu.VMEM((9 * small3, channels), bf16),
            pltpu.VMEM((9 * small4, channels), bf16),
        ],
        compiler_params=pltpu.CompilerParams(vmem_limit_bytes=32 * 1024 * 1024),
        cost_estimate=pl.CostEstimate(
            flops=10_000_000_000, bytes_accessed=12_000_000, transcendentals=0
        ),
    )(here, *inputs)


def local(
    level_one,
    level_two,
    level_three,
    level_four,
    bin_weight,
    neck_feature,
    neck_pooled,
    lateral_one,
    lateral_two,
    lateral_three,
    smooth_weight,
    join_weight,
    biases,
):
    row_count = lax.axis_size("row")
    col_count = lax.axis_size("col")
    here = jnp.stack([lax.axis_index("row"), lax.axis_index("col")]).astype(jnp.int32)
    high1, wide1 = level_one.shape[:2]
    high2, wide2 = level_two.shape[:2]
    high3, wide3 = level_three.shape[0], level_three.shape[1] // col_count
    high4, grid_cols, part_four = level_four.shape
    wide4 = grid_cols // col_count
    channels = bin_weight.shape[2]
    grid_rows = high4 * row_count
    table = cell_table(grid_rows, grid_cols)
    cells = table.shape[0]
    turned = jnp.asarray(np.ascontiguousarray(table.T))
    table = jnp.asarray(table)

    def shape(dims, kind=bf16):
        return jax.ShapeDtypeStruct(dims, kind)

    others = [shifted(level_four, "row", shift) for shift in range(1, row_count)]
    window_rows = high3 * (wide3 + 2 * rim)
    side_rows = rim * (high1 + high2)
    used = (level_one, lateral_one, level_two, lateral_two, level_three, lateral_three)
    kept = (biases, level_four, table, bin_weight, turned)
    lat1, lat2, *rest = call(
        functools.partial(lateral_kernel, col_count, len(kept)),
        [shape((high1, wide1, channels)), shape((high2, wide2, channels))]
        + [shape((window_rows + side_rows, channels))] * col_count
        + [shape(value.shape, value.dtype) for value in kept],
        [smem_spec] + [hbm_spec] * (len(used) + len(kept)),
        [pltpu.VMEM(value.shape, value.dtype) for value in used]
        + [
            pltpu.VMEM((high3, level_three.shape[1] + 8, channels), f32),
            pltpu.VMEM((high1, wide1, channels), f32),
            pltpu.VMEM((high2, wide2, channels), f32),
            pltpu.VMEM((window_rows + side_rows, channels), f32),
            pltpu.SemaphoreType.DMA((len(used) + len(kept),)),
        ],
        300_000_000,
        4_000_000,
    )(here, *(in_hbm(value) for value in (*used, *kept)))
    pieces = rest[:col_count]
    bias_table, level_four, table, bin_weight, turned = rest[col_count:]
    blocks = [level_four] + others
    near = (1, col_count - 1)
    messages = call(
        functools.partial(bins_kernel, row_count, col_count, window_rows),
        [
            shape((window_rows + cells + (side_rows if shift in near else 0), channels))
            for shift in range(col_count)
        ],
        [smem_spec] + [vmem_spec] * (2 + row_count + col_count),
        [],
        100_000_000,
        1_000_000,
    )(here, table, bin_weight, *blocks, *pieces)

    received = [messages[0]] + [
        shifted(messages[shift], "col", shift) for shift in range(1, col_count)
    ]
    rows = high4 + 2 * rim
    sizes = (
        (high1, wide1),
        (high2, wide2),
        (high3, wide3),
        (high4, wide4),
        (row_count, col_count),
    )
    plans = stretches(sizes)
    late = (neck_pooled, smooth_weight, join_weight)
    taps, neck_pooled, smooth_weight, join_weight, *matrices = call(
        functools.partial(feature_kernel, row_count, plans),
        [shape((3, rows * grid_cols, channels), f32)]
        + [shape(value.shape) for value in late]
        + [shape((plan[0][0] * plan[0][1], plan[8] * plan[9] ** 2)) for plan in plans],
        [smem_spec, hbm_spec] + [vmem_spec] * row_count + [hbm_spec] * len(late),
        [
            pltpu.VMEM(neck_feature.shape, bf16),
            pltpu.VMEM((grid_rows + 2 * rim + 2, grid_cols, part_four), bf16),
            pltpu.SemaphoreType.DMA((1 + len(late),)),
        ],
        700_000_000,
        12_000_000,
    )(here, in_hbm(neck_feature), *blocks, *(in_hbm(value) for value in late))
    span4 = wide4 + 2 * rim
    windows = call(
        functools.partial(neck_kernel, row_count, col_count, high4, window_rows),
        [shape((rows, span4, channels))] * col_count,
        [smem_spec] + [vmem_spec] * (5 + col_count),
        [
            pltpu.VMEM((cells, channels), f32),
            pltpu.VMEM((3, rows * grid_cols + 16, channels), f32),
            pltpu.VMEM((rows, grid_cols + 16, channels), f32),
        ],
        300_000_000,
        3_000_000,
    )(here, table, turned, neck_pooled, bias_table, taps, *received)

    tops = [windows[0]] + [shifted(windows[shift], "col", shift) for shift in range(1, col_count)]
    span3 = wide3 + 2 * rim
    packed = rim * (wide1 + wide2 + wide3 + 6 * rim)
    lat3, low_rows, high_rows = call(
        functools.partial(rows_kernel, col_count, high3, wide3),
        [shape((high3, span3, channels))] + [shape((packed, channels))] * 2,
        [smem_spec] + [vmem_spec] * (3 + col_count),
        [
            pltpu.VMEM((high3, (span3 + 7) // 8 * 8, channels), f32),
            pltpu.VMEM((packed, channels), f32),
        ],
        1_000_000,
        1_000_000,
    )(here, bias_table, lat1, lat2, *received)
    above, below = edge_swap(low_rows, high_rows, "row")
    return tail(
        here,
        tops,
        (lat1, lat2, lat3),
        above,
        below,
        received[1],
        received[-1],
        bias_table,
        (smooth_weight, join_weight),
        matrices,
        sizes,
    )


def solution(mesh):
    placed = (
        P(("grp", "row"), "col", None),
        P(("grp", "row"), "col", None),
        P(("grp", "row"), None, "col"),
        P(("grp", "row"), None, "col"),
        P(None, "col", None),
        P(None, None, "col", None),
        P(None, None, "col", None),
        P(),
        P(),
        P(),
        P(),
        P(),
        P(),
    )
    return jax.shard_map(
        local, mesh=mesh, in_specs=placed, out_specs=P(("grp", "row"), "col", None), check_vma=False
    )
```

```python
import functools

import jax
import jax.numpy as jnp
import numpy as np
from jax import lax
from jax.experimental import pallas as pl
from jax.experimental.pallas import tpu as pltpu
from jax.sharding import PartitionSpec as P

highest = lax.Precision.HIGHEST
bin_sides = (1, 2, 3, 6)
rim = 2
cuts2 = 2
f32 = jnp.float32
bf16 = jnp.bfloat16
vmem_spec = pl.BlockSpec(memory_space=pltpu.VMEM)
hbm_spec = pl.BlockSpec(memory_space=pltpu.HBM)
smem_spec = pl.BlockSpec(memory_space=pltpu.SMEM)
params = pltpu.CompilerParams(vmem_limit_bytes=30 * 1024 * 1024)


def shifted(value, axis, shift):
    count = lax.axis_size(axis)
    return lax.ppermute(value, axis, [(i, (i + shift) % count) for i in range(count)])


def pair_swap(first, second, axis):
    count = lax.axis_size(axis)

    def pairs(start):
        return [
            edge
            for i in range(start, count - 1, 2)
            for edge in ((i, i + 1), (i + 1, i))
        ]

    return lax.ppermute(first, axis, pairs(0)), lax.ppermute(second, axis, pairs(1))


def cell_table(extent_rows, extent_cols):
    rows = []
    for number, side in enumerate(bin_sides):
        for i in range(side):
            for j in range(side):
                top, low = i * extent_rows // side, -(-(i + 1) * extent_rows // side)
                left, right = j * extent_cols // side, -(-(j + 1) * extent_cols // side)
                rows.append([number, side, i, j, top, low, left, right, (low - top) * (right - left)])
    padded = (len(rows) + 15) // 16 * 16
    table = np.zeros((padded, 16), np.float32)
    table[:, 0] = -1.0
    table[:, 1] = 1.0
    table[:, 8] = 1.0
    table[: len(rows), :9] = np.array(rows, np.float32)
    return table


def dot(a, b):
    return jnp.dot(a, b, preferred_element_type=f32)


def in_hbm(value):
    return pltpu.with_memory_space_constraint(value, pltpu.HBM)


def call(kernel, outs, specs, scratch, flops, moved):
    return pl.pallas_call(
        kernel,
        out_shape=outs,
        in_specs=specs,
        out_specs=jax.tree.map(lambda _: vmem_spec, outs),
        scratch_shapes=scratch,
        compiler_params=params,
        cost_estimate=pl.CostEstimate(flops=flops, bytes_accessed=moved, transcendentals=0),
    )


def wrap(value, count):
    return lax.rem(value + count, count)


def floor_div(value, step):
    return jnp.floor((value + 0.5) / step)


def stretch_matrix(here, out_shape, out_border, in_shape, in_border, factor, out_size, in_size, counts, lanes, taps=1):
    out_rows, out_pitch = out_shape
    lane = lax.broadcasted_iota(jnp.int32, (1, lanes * taps * taps), 1).astype(f32)
    tap = floor_div(lane, lanes)
    place = lane - tap * lanes
    row_tap = floor_div(tap, taps)
    col_tap = tap - row_tap * taps
    place_row = floor_div(place, in_shape[1])
    place_col = place - place_row * in_shape[1]

    def weights(axis, length, targets, tap_here):
        whole = float(in_size[axis] * counts[axis])
        first_out = (here[axis] * out_size[axis] - out_border[axis]).astype(f32) - (taps // 2)
        first_in = (here[axis] * in_size[axis] - in_border[axis]).astype(f32)
        output = first_out + tap_here + lax.broadcasted_iota(jnp.int32, (length, 1), 0).astype(f32)
        source = (output + 0.5) * (1.0 / factor) - 0.5
        source = jnp.minimum(jnp.maximum(source, 0.0), whole - 1.0)
        inside = jnp.where((output >= 0.0) & (output < whole * factor), 1.0, 0.0)
        return jnp.maximum(0.0, 1.0 - jnp.abs(source - (first_in + targets))) * inside

    down = weights(0, out_rows, place_row, row_tap)
    across = weights(1, out_pitch, place_col, col_tap)
    matrix = down[:, None, :] * across[None, :, :]
    return matrix.astype(bf16).reshape(out_rows * out_pitch, -1)


def pitch_of(width):
    return (width + 15) // 16 * 16


def window_shape(size, border):
    return size[0] + 2 * border, pitch_of(size[1] + 2 * border)


def compact_shape(size, border):
    return size[0] + 2 * border, size[1] + 2 * border


def stretches(sizes):
    one, two, three, four, counts = sizes

    def pyramid(out, source):
        shape = window_shape(source, rim)
        borders = (rim, rim)
        factor = out[0] // source[0]
        return (
            window_shape(out, rim), borders, shape, borders, factor, out, source, counts, shape[0] * shape[1]
        )

    def join(source, cuts, part):
        tile = (one[0] // cuts, one[1] // cuts)
        small = (source[0] // cuts, source[1] // cuts)
        shape = compact_shape(small, 1)
        out_border = (-part[0] * tile[0], -part[1] * tile[1])
        in_border = (1 - part[0] * small[0], 1 - part[1] * small[1])
        factor = one[0] // source[0]
        lanes = pitch_of(shape[0] * shape[1])
        return tile, out_border, shape, in_border, factor, one, source, counts, lanes, 3

    parts = [(i, j) for i in range(cuts2) for j in range(cuts2)]
    return (
        (pyramid(three, four), pyramid(two, three), pyramid(one, two), join(three, 1, (0, 0))),
        (join(four, 1, (0, 0)), *(join(two, cuts2, part) for part in parts)),
    )


def matrix_shape(plan):
    return plan[0][0] * plan[0][1], plan[8] * (plan[9] if len(plan) > 9 else 1) ** 2


def lateral_kernel(col_count, kept_count, here_ref, *refs):
    sources, refs = refs[: 6 + kept_count], refs[6 + kept_count :]
    (lat1_ref, lat2_ref), refs = refs[:2], refs[2:]
    pieces, refs = refs[:col_count], refs[col_count:]
    kept, refs = refs[:kept_count], refs[kept_count:]
    fetched, (wide_buf, one_buf, two_buf, piece_buf, sems) = refs[:6], refs[6:]
    copies = [
        pltpu.make_async_copy(source, target, sems.at[number])
        for number, (source, target) in enumerate(zip(sources, (*fetched, *kept)))
    ]
    for copy in copies:
        copy.start()
    one_ref, w1_ref, two_ref, w2_ref, three_ref, w3_ref = fetched
    bias_ref = kept[0]
    copies[6].wait()
    channels = w1_ref.shape[1]
    for number, (source, weight, row, buf, out) in enumerate(
        (
            (one_ref, w1_ref, 5, one_buf, lat1_ref),
            (two_ref, w2_ref, 6, two_buf, lat2_ref),
        )
    ):
        copies[2 * number].wait()
        copies[2 * number + 1].wait()
        high, wide, depth = source.shape
        value = dot(source[...].reshape(high * wide, depth), weight[...])
        value = jnp.maximum(value + bias_ref[row : row + 1, :], 0.0).reshape(high, wide, channels)
        buf[...] = value
        out[...] = value.astype(bf16)
    high3, whole3, share = three_ref.shape
    wide3 = whole3 // col_count
    col_here = here_ref[1]
    copies[4].wait()
    copies[5].wait()
    weight = w3_ref[pl.ds(pl.multiple_of(col_here * share, 16), share), :]
    value = dot(three_ref[...].reshape(high3 * whole3, share), weight)
    wide_buf[...] = jnp.zeros_like(wide_buf)
    wide_buf[:, rim : rim + whole3, :] = value.reshape(high3, whole3, channels)
    span = wide3 + 2 * rim
    for shift, piece in enumerate(pieces):
        target = wrap(col_here + shift, col_count)
        for row in range(high3):
            piece_buf[row * span : (row + 1) * span, :] = wide_buf[
                row, pl.ds(pl.multiple_of(target * wide3, 8), span), :
            ]
        start = high3 * span
        for buf in (one_buf, two_buf):
            high, wide = buf.shape[:2]
            first = wide - rim if shift == 1 else 0
            for row in range(high):
                piece_buf[start : start + rim, :] = buf[row, first : first + rim, :]
                start += rim
        piece[...] = piece_buf[...].astype(bf16)
    for copy in copies[7:]:
        copy.wait()


def bins_kernel(row_count, col_count, window_rows, here_ref, table_ref, weight_ref, *refs):
    blocks, pieces, messages = (
        refs[:row_count],
        refs[row_count : row_count + col_count],
        refs[row_count + col_count :],
    )
    table = table_ref[...]
    high, wide, depth = blocks[0].shape
    place = lax.broadcasted_iota(jnp.int32, (1, high * wide), 1).astype(f32)
    place_row = floor_div(place, wide)
    place_col = place - place_row * wide
    in_cols = (place_col >= table[:, 6:7]) & (place_col < table[:, 7:8])
    pooled = None
    for shift, block in enumerate(blocks):
        row = place_row + (wrap(here_ref[0] - shift, row_count) * high).astype(f32)
        inside = in_cols & (row >= table[:, 4:5]) & (row < table[:, 5:6])
        inside = jnp.where(inside, 1.0, 0.0).astype(bf16)
        term = dot(inside, block[...].reshape(high * wide, depth))
        pooled = term if pooled is None else pooled + term
    pooled = (pooled / table[:, 8:9]).astype(bf16)
    bins = None
    for number in range(len(bin_sides)):
        term = jnp.where(table[:, 0:1] == number, dot(pooled, weight_ref[number]), 0.0)
        bins = term if bins is None else bins + term
    bins = bins.astype(bf16)
    cells = bins.shape[0]
    for piece, message in zip(pieces, messages):
        message[0:window_rows, :] = piece[0:window_rows, :]
        message[window_rows : window_rows + cells, :] = bins
        if message.shape[0] > window_rows + cells:
            message[window_rows + cells :, :] = piece[window_rows:, :]


def feature_kernel(row_count, plans, here_ref, weight_hbm, *refs):
    blocks, refs = refs[:row_count], refs[row_count:]
    late, refs = refs[:3], refs[3:]
    out_ref, kept, matrices = refs[0], refs[1:4], refs[4 : 4 + len(plans)]
    weight_ref, grid_buf, sems = refs[4 + len(plans) :]
    copies = [
        pltpu.make_async_copy(source, target, sems.at[number])
        for number, (source, target) in enumerate(zip((weight_hbm, *late), (weight_ref, *kept)))
    ]
    for copy in copies:
        copy.start()
    here = (here_ref[0], here_ref[1])
    for plan, matrix in zip(plans, matrices):
        matrix[...] = stretch_matrix(here, *plan)
    high, wide, depth = blocks[0].shape
    grid_buf[...] = jnp.zeros_like(grid_buf)
    for shift, block in enumerate(blocks):
        row = wrap(here_ref[0] - shift, row_count) * high + rim + 1
        grid_buf[pl.ds(row, high)] = block[...]
    rows = out_ref.shape[1] // wide
    window = grid_buf[pl.ds(here_ref[0] * high, rows + 2)].reshape((rows + 2) * wide, depth)
    copies[0].wait()
    for col_tap in range(3):
        total = dot(window[0 : rows * wide], weight_ref[0, col_tap])
        for row_tap in (1, 2):
            total = total + dot(
                window[row_tap * wide : (row_tap + rows) * wide], weight_ref[row_tap, col_tap]
            )
        out_ref[col_tap] = total
    for copy in copies[1:]:
        copy.wait()


def neck_kernel(
    row_count, col_count, high, window_rows, here_ref, table_ref, turned_ref, weight_ref, bias_ref, taps_ref, *refs
):
    messages, refs = refs[:col_count], refs[col_count:]
    windows, (bins_buf, acc_buf, term_buf) = refs[:col_count], refs[col_count:]
    rows, span, channels = windows[0].shape
    wide = taps_ref.shape[1] // rows
    width4 = span - 2 * rim
    table = table_ref[...]
    cells = table.shape[0]
    bins = messages[0][window_rows : window_rows + cells, :].astype(f32)
    for message in messages[1:]:
        bins = bins + message[window_rows : window_rows + cells, :].astype(f32)
    bias = jnp.zeros((cells, channels), f32)
    for number in range(len(bin_sides)):
        bias = jnp.where(table[:, 0:1] == number, bias_ref[number : number + 1, :], bias)
    share = weight_ref.shape[2]
    first = here_ref[1] * share
    mine = table[:, 0:1] == (first // channels).astype(f32)
    bins_buf[...] = jnp.where(mine, jnp.maximum(bins + bias, 0.0), 0.0)
    if share == channels:
        binned = bins_buf[...]
    else:
        binned = bins_buf[:, pl.ds(pl.multiple_of(lax.rem(first, channels), 128), share)]
    place = lax.broadcasted_iota(jnp.int32, ((rows + 2) * wide, 1), 0).astype(f32)
    place_row = floor_div(place, wide)
    place_col = place - place_row * wide
    place_row = place_row + (here_ref[0] * high - rim - 1).astype(f32)
    grid_rows = float(high * row_count)
    sides = turned_ref[1:2, :]

    def weights(position, extent, index):
        source = (position + 0.5) * sides / extent - 0.5
        source = jnp.minimum(jnp.maximum(source, 0.0), sides - 1.0)
        return jnp.maximum(0.0, 1.0 - jnp.abs(source - index))

    spread = weights(place_row, grid_rows, turned_ref[2:3, :])
    spread = spread * weights(place_col, float(wide), turned_ref[3:4, :])
    spread = jnp.where((place_row >= 0.0) & (place_row < grid_rows), spread, 0.0)
    ppm = jnp.dot(spread, binned, precision=highest, preferred_element_type=f32).astype(bf16)
    size = rows * wide
    for col_tap in range(3):
        total = taps_ref[col_tap]
        for row_tap in range(3):
            total = total + dot(
                ppm[row_tap * wide : row_tap * wide + size], weight_ref[row_tap, col_tap]
            )
        acc_buf[col_tap, 8 : 8 + size, :] = total
    col = place_col[0:size]
    total = (
        acc_buf[1, 8 : 8 + size, :]
        + jnp.where(col > 0.0, acc_buf[0, 7 : 7 + size, :], 0.0)
        + jnp.where(col < wide - 1.0, acc_buf[2, 9 : 9 + size, :], 0.0)
    )
    term_buf[...] = jnp.zeros_like(term_buf)
    term_buf[:, rim : rim + wide, :] = total.reshape(rows, wide, channels)
    for shift, window in enumerate(windows):
        target = wrap(here_ref[1] + shift, col_count)
        window[...] = term_buf[:, pl.ds(pl.multiple_of(target * width4, 8), span), :].astype(bf16)


def rows_kernel(col_count, high3, wide3, here_ref, bias_ref, lat1_ref, lat2_ref, *refs):
    messages, (lat3_ref, first_ref, second_ref, three_buf, low_buf, high_buf) = (
        refs[:col_count],
        refs[col_count:],
    )
    span = wide3 + 2 * rim
    total = messages[0][0 : high3 * span, :].astype(f32)
    for message in messages[1:]:
        total = total + message[0 : high3 * span, :].astype(f32)
    total = jnp.maximum(total + bias_ref[7:8, :], 0.0)
    col_here = here_ref[1]
    place = lax.broadcasted_iota(jnp.int32, (span, 1), 0) + col_here * wide3 - rim
    inside = (place >= 0) & (place < wide3 * col_count)
    for row in range(high3):
        three_buf[row, :span, :] = jnp.where(inside, total[row * span : (row + 1) * span], 0.0)
    lat3_ref[...] = three_buf[:, :span, :].astype(bf16)
    high1, wide1 = lat1_ref.shape[:2]
    high2, wide2 = lat2_ref.shape[:2]
    before, after = messages[1], messages[col_count - 1]
    sides_at = before.shape[0] - rim * (high1 + high2)
    for pack_buf, last in ((low_buf, False), (high_buf, True)):
        start, at = 0, sides_at
        for lat, high, wide in ((lat1_ref, high1, wide1), (lat2_ref, high2, wide2)):
            whole = wide + 2 * rim
            first = high - rim if last else 0
            left = before[at + rim * first : at + rim * (first + rim), :].astype(f32)
            right = after[at + rim * first : at + rim * (first + rim), :].astype(f32)
            left = jnp.where(col_here > 0, left, 0.0)
            right = jnp.where(col_here < col_count - 1, right, 0.0)
            for step in range(rim):
                pack_buf[start : start + rim, :] = left[rim * step : rim * (step + 1)]
                pack_buf[start + rim : start + rim + wide, :] = lat[first + step].astype(f32)
                pack_buf[start + rim + wide : start + whole, :] = right[rim * step : rim * (step + 1)]
                start += whole
            at += rim * high
        for step in range(rim):
            row = high3 - rim + step if last else step
            pack_buf[start : start + span, :] = three_buf[row, :span, :]
            start += span
    even = lax.rem(here_ref[0], 2) == 0
    low, high = low_buf[...], high_buf[...]
    first_ref[...] = jnp.where(even, high, low).astype(bf16)
    second_ref[...] = jnp.where(even, low, high).astype(bf16)


def tap_terms(small, weight_ref, first, store):
    channels = weight_ref.shape[3]
    for tap in range(9):
        weight = weight_ref[tap // 3, tap % 3, first : first + channels, :]
        store(tap, dot(small, weight).astype(bf16))


def late_kernel(sizes, plans, top_count, here_ref, bias_ref, join_ref, *refs):
    tops, refs = refs[:top_count], refs[top_count:]
    top_ref, base_ref, matrices, refs = refs[0], refs[1], refs[2 : 1 + len(plans)], refs[1 + len(plans) :]
    top_buf, small_buf, terms_buf = refs
    high4, wide4 = sizes[3]
    here = (here_ref[0], here_ref[1])
    total = tops[0][...].astype(f32)
    for ref in tops[1:]:
        total = total + ref[...].astype(f32)
    top_buf[...] = jnp.zeros_like(top_buf)
    top_buf[:, : wide4 + 2 * rim, :] = jnp.maximum(total + bias_ref[4:5, :][None], 0.0)
    top_ref[...] = top_buf[...].astype(bf16).reshape(top_ref.shape)
    tall, broad = compact_shape((high4, wide4), 1)
    small_buf[...] = jnp.zeros_like(small_buf)
    for row in range(tall):
        small_buf[row * broad : (row + 1) * broad, :] = top_buf[
            row + rim - 1, rim - 1 : rim - 1 + broad, :
        ]
    lanes, channels = small_buf.shape

    def store(tap, value):
        terms_buf[tap * lanes : (tap + 1) * lanes, :] = value

    tap_terms(small_buf[...].astype(bf16), join_ref, 3 * channels, store)
    base_ref[...] = dot(stretch_matrix(here, *plans[0]), terms_buf[...])
    for plan, matrix in zip(plans[1:], matrices):
        matrix[...] = stretch_matrix(here, *plan)


def tail_kernel(sizes, part_count, here_ref, *refs):
    (high1, wide1), (high2, wide2), (high3, wide3), _, (row_count, col_count) = sizes
    quarters, refs = refs[:part_count], refs[part_count:]
    (
        top_ref,
        base_ref,
        lat1_ref,
        lat2_ref,
        lat3_ref,
        first_ref,
        second_ref,
        before_ref,
        after_ref,
        bias_ref,
        smooth_w,
        join_w,
        up3_ref,
        up2_ref,
        up1_ref,
        spread3_ref,
        out_ref,
        lat1_buf,
        lat2_buf,
        lat3_buf,
        pyr1_buf,
        pyr2_buf,
        pyr3_buf,
        acc_buf,
        sums_buf,
        stack_buf,
        small3_buf,
        small2_buf,
        terms3_buf,
        terms2_buf,
        above_buf,
        below_buf,
    ) = refs
    channels = bias_ref.shape[1]

    even = lax.rem(here_ref[0], 2) == 0
    first, second = first_ref[...].astype(f32), second_ref[...].astype(f32)
    above_buf[...] = jnp.where(even, second, first)
    below_buf[...] = jnp.where(even, first, second)
    side_start = before_ref.shape[0] - rim * (high1 + high2)
    row_start = 0
    for ref, buf, high, wide in (
        (lat1_ref, lat1_buf, high1, wide1),
        (lat2_ref, lat2_buf, high2, wide2),
        (lat3_ref, lat3_buf, high3, wide3 + 2 * rim),
    ):
        buf[...] = jnp.zeros_like(buf)
        whole = wide
        if buf is lat3_buf:
            buf[rim : rim + high, :wide, :] = ref[...].astype(f32)
        else:
            whole = wide + 2 * rim
            buf[rim : rim + high, rim : rim + wide, :] = ref[...].astype(f32)
            for source, col, keep in (
                (before_ref, 0, here_ref[1] > 0),
                (after_ref, rim + wide, here_ref[1] < col_count - 1),
            ):
                sides = source[side_start : side_start + rim * high, :].astype(f32)
                sides = jnp.where(keep, sides, 0.0)
                for row in range(high):
                    buf[rim + row, col : col + rim, :] = sides[rim * row : rim * row + rim]
            side_start += rim * high
        for source, row in ((above_buf, 0), (below_buf, rim + high)):
            both = source[row_start : row_start + rim * whole, :]
            for step in range(rim):
                buf[row + step, :whole, :] = both[step * whole : (step + 1) * whole]
        row_start += rim * whole

    shape1, shape2, shape3 = lat1_buf.shape[:2], lat2_buf.shape[:2], lat3_buf.shape[:2]
    for lat_buf, matrix, source, out in (
        (lat3_buf, up3_ref, None, pyr3_buf),
        (lat2_buf, up2_ref, pyr3_buf, pyr2_buf),
        (lat1_buf, up1_ref, pyr2_buf, pyr1_buf),
    ):
        source = top_ref[...] if source is None else source[...]
        total = lat_buf[...].reshape(-1, channels) + dot(matrix[...], source)
        out[...] = total.astype(bf16)

    def conv(source, shape, weight_at, rows):
        pitch = shape[1]
        span = rows * pitch
        stacked = jnp.concatenate(
            [source[row_tap * pitch : row_tap * pitch + span, :] for row_tap in range(3)], axis=1
        )
        for col_tap in range(3):
            weight = weight_at(col_tap)
            total = dot(stacked, weight.reshape(-1, channels))
            acc_buf[col_tap, :rows, :pitch, :] = total.reshape(rows, pitch, channels)

    def taps_total(rows, whole):
        total = acc_buf[0, :rows, 0:whole, :]
        for col_tap in (1, 2):
            total = total + acc_buf[col_tap, :rows, col_tap : whole + col_tap, :]
        return total

    def smooth(number, source, shape, wide):
        rows = shape[0] - 2
        conv(source, shape, lambda j: smooth_w[number, :, j], rows)
        total = taps_total(rows, wide + 2)
        return jnp.maximum(total + bias_ref[8 + number : 9 + number, :][None], 0.0)

    value = smooth(2, pyr3_buf, shape3, wide3)
    tall, broad = compact_shape((high3, wide3), 1)
    small3_buf[...] = jnp.zeros_like(small3_buf)
    for row in range(tall):
        small3_buf[row * broad : (row + 1) * broad, :] = value[row]
    lanes3 = small3_buf.shape[0]

    def store3(tap, value):
        terms3_buf[tap * lanes3 : (tap + 1) * lanes3, :] = value

    tap_terms(small3_buf[...].astype(bf16), join_w, 2 * channels, store3)

    rows2, whole2 = compact_shape((high2, wide2), 1)
    sums_buf[:rows2, :whole2, :] = smooth(1, pyr2_buf, shape2, wide2)
    half = (high2 // cuts2, wide2 // cuts2)
    tall, broad = compact_shape(half, 1)
    lanes2 = small2_buf.shape[0] // part_count
    small2_buf[...] = jnp.zeros_like(small2_buf)
    for part in range(part_count):
        row0, col0 = part // cuts2 * half[0], part % cuts2 * half[1]
        for row in range(tall):
            start = part * lanes2 + row * broad
            small2_buf[start : start + broad, :] = sums_buf[row0 + row, col0 : col0 + broad, :]

    def store2(tap, value):
        for part in range(part_count):
            start = (part * 9 + tap) * lanes2
            terms2_buf[start : start + lanes2, :] = value[part * lanes2 : (part + 1) * lanes2]

    tap_terms(small2_buf[...].astype(bf16), join_w, channels, store2)

    rows1, pitch1 = window_shape((high1, wide1), 1)
    value = smooth(0, pyr1_buf, shape1, wide1)
    down = here_ref[0] * high1 - 1 + lax.broadcasted_iota(jnp.int32, (rows1, 1, 1), 0)
    across = here_ref[1] * wide1 - 1 + lax.broadcasted_iota(jnp.int32, (1, wide1 + 2, 1), 1)
    inside = (down >= 0) & (down < high1 * row_count) & (across >= 0) & (across < wide1 * col_count)
    sums_buf[:rows1, : wide1 + 2, :] = jnp.where(inside, value, 0.0)
    stack_buf[...] = sums_buf[...].astype(bf16).reshape(rows1 * pitch1, channels)
    conv(stack_buf, (rows1, pitch1), lambda j: join_w[:, j, 0:channels], high1)
    total = taps_total(high1, wide1)
    spread = base_ref[...] + dot(spread3_ref[...], terms3_buf[...])
    sums_buf[:high1, :wide1, :] = total + spread.reshape(high1, wide1, channels)
    tall, broad = high1 // cuts2, wide1 // cuts2
    for part, matrix in enumerate(quarters):
        terms = terms2_buf[part * 9 * lanes2 : (part + 1) * 9 * lanes2, :]
        value = dot(matrix[...], terms).reshape(tall, broad, channels)
        row0, col0 = part // cuts2 * tall, part % cuts2 * broad
        value = value + sums_buf[row0 : row0 + tall, col0 : col0 + broad, :]
        value = jnp.maximum(value + bias_ref[11:12, :][None], 0.0)
        out_ref[row0 : row0 + tall, col0 : col0 + broad, :] = value.astype(bf16)


def tail(here, top, base, lats, swapped, before, after, biases, weights, matrices, quarters, sizes):
    one, _, _, _, _ = sizes
    channels = biases.shape[1]
    shapes = [window_shape(size, rim) for size in sizes[:3]]
    (rows1, pitch1), (rows2, pitch2), (rows3, pitch3) = shapes
    small3, small2 = matrices[-1].shape[1] // 9, quarters[0].shape[1] // 9 * len(quarters)
    inputs = (*quarters, top, base, *lats, *swapped, before, after, biases, *weights, *matrices)
    return pl.pallas_call(
        functools.partial(tail_kernel, sizes, len(quarters)),
        out_shape=jax.ShapeDtypeStruct((*one, channels), bf16),
        in_specs=[smem_spec] + [vmem_spec] * len(inputs),
        out_specs=vmem_spec,
        scratch_shapes=[
            pltpu.VMEM((rows1, pitch1, channels), f32),
            pltpu.VMEM((rows2, pitch2, channels), f32),
            pltpu.VMEM((rows3, pitch3, channels), f32),
            pltpu.VMEM((rows1 * pitch1, channels), bf16),
            pltpu.VMEM((rows2 * pitch2, channels), bf16),
            pltpu.VMEM((rows3 * pitch3, channels), bf16),
            pltpu.VMEM((3, rows1 - 2, pitch1, channels), f32),
            pltpu.VMEM((rows1 - 2, pitch1, channels), f32),
            pltpu.VMEM(((rows1 - 2) * pitch1, channels), bf16),
            pltpu.VMEM((small3, channels), f32),
            pltpu.VMEM((small2, channels), f32),
            pltpu.VMEM((9 * small3, channels), bf16),
            pltpu.VMEM((9 * small2, channels), bf16),
            pltpu.VMEM(swapped[0].shape, f32),
            pltpu.VMEM(swapped[0].shape, f32),
        ],
        compiler_params=pltpu.CompilerParams(vmem_limit_bytes=30 * 1024 * 1024),
        cost_estimate=pl.CostEstimate(
            flops=8_000_000_000, bytes_accessed=12_000_000, transcendentals=0
        ),
    )(here, *inputs)


def local(
    level_one,
    level_two,
    level_three,
    level_four,
    bin_weight,
    neck_feature,
    neck_pooled,
    lateral_one,
    lateral_two,
    lateral_three,
    smooth_weight,
    join_weight,
    biases,
):
    row_count = lax.axis_size("row")
    col_count = lax.axis_size("col")
    here = jnp.stack([lax.axis_index("row"), lax.axis_index("col")]).astype(jnp.int32)
    high1, wide1 = level_one.shape[:2]
    high2, wide2 = level_two.shape[:2]
    high3, wide3 = level_three.shape[0], level_three.shape[1] // col_count
    high4, grid_cols, part_four = level_four.shape
    wide4 = grid_cols // col_count
    channels = bin_weight.shape[2]
    grid_rows = high4 * row_count
    table = cell_table(grid_rows, grid_cols)
    cells = table.shape[0]
    turned = jnp.asarray(np.ascontiguousarray(table.T))
    table = jnp.asarray(table)

    def shape(dims, kind=bf16):
        return jax.ShapeDtypeStruct(dims, kind)

    others = [shifted(level_four, "row", shift) for shift in range(1, row_count)]
    window_rows = high3 * (wide3 + 2 * rim)
    side_rows = rim * (high1 + high2)
    used = (level_one, lateral_one, level_two, lateral_two, level_three, lateral_three)
    kept = (biases, level_four, table, bin_weight, turned)
    lat1, lat2, *rest = call(
        functools.partial(lateral_kernel, col_count, len(kept)),
        [shape((high1, wide1, channels)), shape((high2, wide2, channels))]
        + [shape((window_rows + side_rows, channels))] * col_count
        + [shape(value.shape, value.dtype) for value in kept],
        [smem_spec] + [hbm_spec] * (len(used) + len(kept)),
        [pltpu.VMEM(value.shape, value.dtype) for value in used]
        + [
            pltpu.VMEM((high3, level_three.shape[1] + 8, channels), f32),
            pltpu.VMEM((high1, wide1, channels), f32),
            pltpu.VMEM((high2, wide2, channels), f32),
            pltpu.VMEM((window_rows + side_rows, channels), f32),
            pltpu.SemaphoreType.DMA((len(used) + len(kept),)),
        ],
        300_000_000,
        4_000_000,
    )(here, *(in_hbm(value) for value in (*used, *kept)))
    pieces = rest[:col_count]
    bias_table, level_four, table, bin_weight, turned = rest[col_count:]
    blocks = [level_four] + others
    near = (1, col_count - 1)
    messages = call(
        functools.partial(bins_kernel, row_count, col_count, window_rows),
        [
            shape((window_rows + cells + (side_rows if shift in near else 0), channels))
            for shift in range(col_count)
        ],
        [smem_spec] + [vmem_spec] * (2 + row_count + col_count),
        [],
        100_000_000,
        1_000_000,
    )(here, table, bin_weight, *blocks, *pieces)

    received = [messages[0]] + [
        shifted(messages[shift], "col", shift) for shift in range(1, col_count)
    ]
    rows = high4 + 2 * rim
    sizes = (
        (high1, wide1),
        (high2, wide2),
        (high3, wide3),
        (high4, wide4),
        (row_count, col_count),
    )
    plans, late_plans = stretches(sizes)
    late = (neck_pooled, smooth_weight, join_weight)
    taps, neck_pooled, smooth_weight, join_weight, *matrices = call(
        functools.partial(feature_kernel, row_count, plans),
        [shape((3, rows * grid_cols, channels), f32)]
        + [shape(value.shape) for value in late]
        + [shape(matrix_shape(plan)) for plan in plans],
        [smem_spec, hbm_spec] + [vmem_spec] * row_count + [hbm_spec] * len(late),
        [
            pltpu.VMEM(neck_feature.shape, bf16),
            pltpu.VMEM((grid_rows + 2 * rim + 2, grid_cols, part_four), bf16),
            pltpu.SemaphoreType.DMA((1 + len(late),)),
        ],
        700_000_000,
        12_000_000,
    )(here, in_hbm(neck_feature), *blocks, *(in_hbm(value) for value in late))
    span4 = wide4 + 2 * rim
    windows = call(
        functools.partial(neck_kernel, row_count, col_count, high4, window_rows),
        [shape((rows, span4, channels))] * col_count,
        [smem_spec] + [vmem_spec] * (5 + col_count),
        [
            pltpu.VMEM((cells, channels), f32),
            pltpu.VMEM((3, rows * grid_cols + 16, channels), f32),
            pltpu.VMEM((rows, grid_cols + 16, channels), f32),
        ],
        300_000_000,
        3_000_000,
    )(here, table, turned, neck_pooled, bias_table, taps, *received)

    tops = [windows[0]] + [shifted(windows[shift], "col", shift) for shift in range(1, col_count)]
    span3 = wide3 + 2 * rim
    packed = rim * (wide1 + wide2 + wide3 + 6 * rim)
    lat3, first_rows, second_rows = call(
        functools.partial(rows_kernel, col_count, high3, wide3),
        [shape((high3, span3, channels))] + [shape((packed, channels))] * 2,
        [smem_spec] + [vmem_spec] * (3 + col_count),
        [
            pltpu.VMEM((high3, (span3 + 7) // 8 * 8, channels), f32),
            pltpu.VMEM((packed, channels), f32),
            pltpu.VMEM((packed, channels), f32),
        ],
        1_000_000,
        1_000_000,
    )(here, bias_table, lat1, lat2, *received)
    swapped = pair_swap(first_rows, second_rows, "row")
    small = late_plans[0][8]
    top, base, *quarters = call(
        functools.partial(late_kernel, sizes, late_plans, col_count),
        [
            shape((rows * pitch_of(span4), channels)),
            shape((high1 * wide1, channels), f32),
        ]
        + [shape(matrix_shape(plan)) for plan in late_plans[1:]],
        [smem_spec] + [vmem_spec] * (2 + col_count),
        [
            pltpu.VMEM((rows, pitch_of(span4), channels), f32),
            pltpu.VMEM((small, channels), f32),
            pltpu.VMEM((9 * small, channels), bf16),
        ],
        700_000_000,
        5_000_000,
    )(here, bias_table, join_weight, *tops)
    return tail(
        here,
        top,
        base,
        (lat1, lat2, lat3),
        swapped,
        received[1],
        received[-1],
        bias_table,
        (smooth_weight, join_weight),
        matrices,
        quarters,
        sizes,
    )


def solution(mesh):
    placed = (
        P(("grp", "row"), "col", None),
        P(("grp", "row"), "col", None),
        P(("grp", "row"), None, "col"),
        P(("grp", "row"), None, "col"),
        P(None, "col", None),
        P(None, None, "col", None),
        P(None, None, "col", None),
        P(),
        P(),
        P(),
        P(),
        P(),
        P(),
    )
    return jax.shard_map(
        local, mesh=mesh, in_specs=placed, out_specs=P(("grp", "row"), "col", None), check_vma=False
    )
```

```python
import functools

import jax
import jax.numpy as jnp
import numpy as np
from jax import lax
from jax.experimental import pallas as pl
from jax.experimental.pallas import tpu as pltpu
from jax.sharding import PartitionSpec as P

highest = lax.Precision.HIGHEST
bin_sides = (1, 2, 3, 6)
rim = 2
cuts2 = 2
f32 = jnp.float32
bf16 = jnp.bfloat16
vmem_spec = pl.BlockSpec(memory_space=pltpu.VMEM)
hbm_spec = pl.BlockSpec(memory_space=pltpu.HBM)
smem_spec = pl.BlockSpec(memory_space=pltpu.SMEM)
params = pltpu.CompilerParams(vmem_limit_bytes=30 * 1024 * 1024)


def shifted(value, axis, shift):
    count = lax.axis_size(axis)
    return lax.ppermute(value, axis, [(i, (i + shift) % count) for i in range(count)])


def pair_swap(first, second, axis):
    count = lax.axis_size(axis)

    def pairs(start):
        return [
            edge
            for i in range(start, count - 1, 2)
            for edge in ((i, i + 1), (i + 1, i))
        ]

    return lax.ppermute(first, axis, pairs(0)), lax.ppermute(second, axis, pairs(1))


def cell_table(extent_rows, extent_cols):
    rows = []
    for number, side in enumerate(bin_sides):
        for i in range(side):
            for j in range(side):
                top, low = i * extent_rows // side, -(-(i + 1) * extent_rows // side)
                left, right = j * extent_cols // side, -(-(j + 1) * extent_cols // side)
                rows.append([number, side, i, j, top, low, left, right, (low - top) * (right - left)])
    padded = (len(rows) + 15) // 16 * 16
    table = np.zeros((padded, 16), np.float32)
    table[:, 0] = -1.0
    table[:, 1] = 1.0
    table[:, 8] = 1.0
    table[: len(rows), :9] = np.array(rows, np.float32)
    return table


def dot(a, b):
    return jnp.dot(a, b, preferred_element_type=f32)


def in_hbm(value):
    return pltpu.with_memory_space_constraint(value, pltpu.HBM)


def call(kernel, outs, specs, scratch, flops, moved):
    return pl.pallas_call(
        kernel,
        out_shape=outs,
        in_specs=specs,
        out_specs=jax.tree.map(lambda _: vmem_spec, outs),
        scratch_shapes=scratch,
        compiler_params=params,
        cost_estimate=pl.CostEstimate(flops=flops, bytes_accessed=moved, transcendentals=0),
    )


def wrap(value, count):
    return lax.rem(value + count, count)


def floor_div(value, step):
    return jnp.floor((value + 0.5) / step)


def stretch_matrix(here, out_shape, out_border, in_shape, in_border, factor, out_size, in_size, counts, lanes, taps=1):
    out_rows, out_pitch = out_shape
    lane = lax.broadcasted_iota(jnp.int32, (1, lanes * taps * taps), 1).astype(f32)
    tap = floor_div(lane, lanes)
    place = lane - tap * lanes
    row_tap = floor_div(tap, taps)
    col_tap = tap - row_tap * taps
    place_row = floor_div(place, in_shape[1])
    place_col = place - place_row * in_shape[1]

    def weights(axis, length, targets, tap_here):
        whole = float(in_size[axis] * counts[axis])
        first_out = (here[axis] * out_size[axis] - out_border[axis]).astype(f32) - (taps // 2)
        first_in = (here[axis] * in_size[axis] - in_border[axis]).astype(f32)
        output = first_out + tap_here + lax.broadcasted_iota(jnp.int32, (length, 1), 0).astype(f32)
        source = (output + 0.5) * (1.0 / factor) - 0.5
        source = jnp.minimum(jnp.maximum(source, 0.0), whole - 1.0)
        inside = jnp.where((output >= 0.0) & (output < whole * factor), 1.0, 0.0)
        return jnp.maximum(0.0, 1.0 - jnp.abs(source - (first_in + targets))) * inside

    down = weights(0, out_rows, place_row, row_tap)
    across = weights(1, out_pitch, place_col, col_tap)
    matrix = down[:, None, :] * across[None, :, :]
    return matrix.astype(bf16).reshape(out_rows * out_pitch, -1)


def pitch_of(width):
    return (width + 15) // 16 * 16


def window_shape(size, border):
    return size[0] + 2 * border, (size[1] + 2 * border + 7) // 8 * 8


def compact_shape(size, border):
    return size[0] + 2 * border, size[1] + 2 * border


def stretches(sizes):
    one, two, three, four, counts = sizes

    def pyramid(out, source):
        shape = window_shape(source, rim)
        borders = (rim, rim)
        factor = out[0] // source[0]
        return (
            window_shape(out, rim), borders, shape, borders, factor, out, source, counts, shape[0] * shape[1]
        )

    def join(source, cuts, part):
        tile = (one[0] // cuts, one[1] // cuts)
        small = (source[0] // cuts, source[1] // cuts)
        shape = compact_shape(small, 1)
        out_border = (-part[0] * tile[0], -part[1] * tile[1])
        in_border = (1 - part[0] * small[0], 1 - part[1] * small[1])
        factor = one[0] // source[0]
        lanes = pitch_of(shape[0] * shape[1])
        return tile, out_border, shape, in_border, factor, one, source, counts, lanes, 3

    parts = [(i, j) for i in range(cuts2) for j in range(cuts2)]
    return (
        (pyramid(three, four), pyramid(two, three), pyramid(one, two), join(three, 1, (0, 0))),
        (join(four, 1, (0, 0)), *(join(two, cuts2, part) for part in parts)),
    )


def matrix_shape(plan):
    return plan[0][0] * plan[0][1], plan[8] * (plan[9] if len(plan) > 9 else 1) ** 2


def lateral_kernel(col_count, kept_count, here_ref, *refs):
    sources, refs = refs[: 6 + kept_count], refs[6 + kept_count :]
    (lat1_ref, lat2_ref), refs = refs[:2], refs[2:]
    pieces, refs = refs[:col_count], refs[col_count:]
    kept, refs = refs[:kept_count], refs[kept_count:]
    fetched, (wide_buf, one_buf, two_buf, piece_buf, sems) = refs[:6], refs[6:]
    copies = [
        pltpu.make_async_copy(source, target, sems.at[number])
        for number, (source, target) in enumerate(zip(sources, (*fetched, *kept)))
    ]
    for copy in copies:
        copy.start()
    one_ref, w1_ref, two_ref, w2_ref, three_ref, w3_ref = fetched
    bias_ref = kept[0]
    copies[6].wait()
    channels = w1_ref.shape[1]
    for number, (source, weight, row, buf, out) in enumerate(
        (
            (one_ref, w1_ref, 5, one_buf, lat1_ref),
            (two_ref, w2_ref, 6, two_buf, lat2_ref),
        )
    ):
        copies[2 * number].wait()
        copies[2 * number + 1].wait()
        high, wide, depth = source.shape
        value = dot(source[...].reshape(high * wide, depth), weight[...])
        value = jnp.maximum(value + bias_ref[row : row + 1, :], 0.0).reshape(high, wide, channels)
        buf[...] = value
        out[...] = value.astype(bf16)
    high3, whole3, share = three_ref.shape
    wide3 = whole3 // col_count
    col_here = here_ref[1]
    copies[4].wait()
    copies[5].wait()
    weight = w3_ref[pl.ds(pl.multiple_of(col_here * share, 16), share), :]
    value = dot(three_ref[...].reshape(high3 * whole3, share), weight)
    wide_buf[...] = jnp.zeros_like(wide_buf)
    wide_buf[:, rim : rim + whole3, :] = value.reshape(high3, whole3, channels)
    span = wide3 + 2 * rim
    for shift, piece in enumerate(pieces):
        target = wrap(col_here + shift, col_count)
        for row in range(high3):
            piece_buf[row * span : (row + 1) * span, :] = wide_buf[
                row, pl.ds(pl.multiple_of(target * wide3, 8), span), :
            ]
        start = high3 * span
        for buf in (one_buf, two_buf):
            high, wide = buf.shape[:2]
            first = wide - rim if shift == 1 else 0
            for row in range(high):
                piece_buf[start : start + rim, :] = buf[row, first : first + rim, :]
                start += rim
        piece[...] = piece_buf[...].astype(bf16)
    for copy in copies[7:]:
        copy.wait()


def bins_kernel(row_count, col_count, window_rows, here_ref, table_ref, weight_ref, *refs):
    blocks, pieces, messages = (
        refs[:row_count],
        refs[row_count : row_count + col_count],
        refs[row_count + col_count :],
    )
    table = table_ref[...]
    high, wide, depth = blocks[0].shape
    place = lax.broadcasted_iota(jnp.int32, (1, high * wide), 1).astype(f32)
    place_row = floor_div(place, wide)
    place_col = place - place_row * wide
    in_cols = (place_col >= table[:, 6:7]) & (place_col < table[:, 7:8])
    pooled = None
    for shift, block in enumerate(blocks):
        row = place_row + (wrap(here_ref[0] - shift, row_count) * high).astype(f32)
        inside = in_cols & (row >= table[:, 4:5]) & (row < table[:, 5:6])
        inside = jnp.where(inside, 1.0, 0.0).astype(bf16)
        term = dot(inside, block[...].reshape(high * wide, depth))
        pooled = term if pooled is None else pooled + term
    pooled = (pooled / table[:, 8:9]).astype(bf16)
    bins = None
    for number in range(len(bin_sides)):
        term = jnp.where(table[:, 0:1] == number, dot(pooled, weight_ref[number]), 0.0)
        bins = term if bins is None else bins + term
    bins = bins.astype(bf16)
    cells = bins.shape[0]
    for piece, message in zip(pieces, messages):
        message[0:window_rows, :] = piece[0:window_rows, :]
        message[window_rows : window_rows + cells, :] = bins
        if message.shape[0] > window_rows + cells:
            message[window_rows + cells :, :] = piece[window_rows:, :]


def feature_kernel(row_count, plans, here_ref, weight_hbm, *refs):
    blocks, refs = refs[:row_count], refs[row_count:]
    late, refs = refs[:3], refs[3:]
    out_ref, kept, matrices = refs[0], refs[1:4], refs[4 : 4 + len(plans)]
    weight_ref, grid_buf, sems = refs[4 + len(plans) :]
    copies = [
        pltpu.make_async_copy(source, target, sems.at[number])
        for number, (source, target) in enumerate(zip((weight_hbm, *late), (weight_ref, *kept)))
    ]
    for copy in copies:
        copy.start()
    here = (here_ref[0], here_ref[1])
    for plan, matrix in zip(plans, matrices):
        matrix[...] = stretch_matrix(here, *plan)
    high, wide, depth = blocks[0].shape
    grid_buf[...] = jnp.zeros_like(grid_buf)
    for shift, block in enumerate(blocks):
        row = wrap(here_ref[0] - shift, row_count) * high + rim + 1
        grid_buf[pl.ds(row, high)] = block[...]
    rows = out_ref.shape[1] // wide
    window = grid_buf[pl.ds(here_ref[0] * high, rows + 2)].reshape((rows + 2) * wide, depth)
    copies[0].wait()
    for col_tap in range(3):
        total = dot(window[0 : rows * wide], weight_ref[0, col_tap])
        for row_tap in (1, 2):
            total = total + dot(
                window[row_tap * wide : (row_tap + rows) * wide], weight_ref[row_tap, col_tap]
            )
        out_ref[col_tap] = total
    for copy in copies[1:]:
        copy.wait()


def neck_kernel(
    row_count, col_count, high, window_rows, here_ref, table_ref, turned_ref, weight_ref, bias_ref, taps_ref, *refs
):
    messages, refs = refs[:col_count], refs[col_count:]
    windows, (bins_buf, acc_buf, term_buf) = refs[:col_count], refs[col_count:]
    rows, span, channels = windows[0].shape
    wide = taps_ref.shape[1] // rows
    width4 = span - 2 * rim
    table = table_ref[...]
    cells = table.shape[0]
    bins = messages[0][window_rows : window_rows + cells, :].astype(f32)
    for message in messages[1:]:
        bins = bins + message[window_rows : window_rows + cells, :].astype(f32)
    bias = jnp.zeros((cells, channels), f32)
    for number in range(len(bin_sides)):
        bias = jnp.where(table[:, 0:1] == number, bias_ref[number : number + 1, :], bias)
    share = weight_ref.shape[2]
    first = here_ref[1] * share
    mine = table[:, 0:1] == (first // channels).astype(f32)
    bins_buf[...] = jnp.where(mine, jnp.maximum(bins + bias, 0.0), 0.0)
    if share == channels:
        binned = bins_buf[...]
    else:
        binned = bins_buf[:, pl.ds(pl.multiple_of(lax.rem(first, channels), 128), share)]
    place = lax.broadcasted_iota(jnp.int32, ((rows + 2) * wide, 1), 0).astype(f32)
    place_row = floor_div(place, wide)
    place_col = place - place_row * wide
    place_row = place_row + (here_ref[0] * high - rim - 1).astype(f32)
    grid_rows = float(high * row_count)
    sides = turned_ref[1:2, :]

    def weights(position, extent, index):
        source = (position + 0.5) * sides / extent - 0.5
        source = jnp.minimum(jnp.maximum(source, 0.0), sides - 1.0)
        return jnp.maximum(0.0, 1.0 - jnp.abs(source - index))

    spread = weights(place_row, grid_rows, turned_ref[2:3, :])
    spread = spread * weights(place_col, float(wide), turned_ref[3:4, :])
    spread = jnp.where((place_row >= 0.0) & (place_row < grid_rows), spread, 0.0)
    ppm = jnp.dot(spread, binned, precision=highest, preferred_element_type=f32).astype(bf16)
    size = rows * wide
    for col_tap in range(3):
        total = taps_ref[col_tap]
        for row_tap in range(3):
            total = total + dot(
                ppm[row_tap * wide : row_tap * wide + size], weight_ref[row_tap, col_tap]
            )
        acc_buf[col_tap, 8 : 8 + size, :] = total
    col = place_col[0:size]
    total = (
        acc_buf[1, 8 : 8 + size, :]
        + jnp.where(col > 0.0, acc_buf[0, 7 : 7 + size, :], 0.0)
        + jnp.where(col < wide - 1.0, acc_buf[2, 9 : 9 + size, :], 0.0)
    )
    term_buf[...] = jnp.zeros_like(term_buf)
    term_buf[:, rim : rim + wide, :] = total.reshape(rows, wide, channels)
    for shift, window in enumerate(windows):
        target = wrap(here_ref[1] + shift, col_count)
        window[...] = term_buf[:, pl.ds(pl.multiple_of(target * width4, 8), span), :].astype(bf16)


def rows_kernel(col_count, high3, wide3, here_ref, bias_ref, lat1_ref, lat2_ref, *refs):
    messages, (lat3_ref, first_ref, second_ref, three_buf, low_buf, high_buf) = (
        refs[:col_count],
        refs[col_count:],
    )
    span = wide3 + 2 * rim
    total = messages[0][0 : high3 * span, :].astype(f32)
    for message in messages[1:]:
        total = total + message[0 : high3 * span, :].astype(f32)
    total = jnp.maximum(total + bias_ref[7:8, :], 0.0)
    col_here = here_ref[1]
    place = lax.broadcasted_iota(jnp.int32, (span, 1), 0) + col_here * wide3 - rim
    inside = (place >= 0) & (place < wide3 * col_count)
    for row in range(high3):
        three_buf[row, :span, :] = jnp.where(inside, total[row * span : (row + 1) * span], 0.0)
    lat3_ref[...] = three_buf[:, :span, :].astype(bf16)
    high1, wide1 = lat1_ref.shape[:2]
    high2, wide2 = lat2_ref.shape[:2]
    before, after = messages[1], messages[col_count - 1]
    sides_at = before.shape[0] - rim * (high1 + high2)
    for pack_buf, last in ((low_buf, False), (high_buf, True)):
        start, at = 0, sides_at
        for lat, high, wide in ((lat1_ref, high1, wide1), (lat2_ref, high2, wide2)):
            whole = wide + 2 * rim
            first = high - rim if last else 0
            left = before[at + rim * first : at + rim * (first + rim), :].astype(f32)
            right = after[at + rim * first : at + rim * (first + rim), :].astype(f32)
            left = jnp.where(col_here > 0, left, 0.0)
            right = jnp.where(col_here < col_count - 1, right, 0.0)
            for step in range(rim):
                pack_buf[start : start + rim, :] = left[rim * step : rim * (step + 1)]
                pack_buf[start + rim : start + rim + wide, :] = lat[first + step].astype(f32)
                pack_buf[start + rim + wide : start + whole, :] = right[rim * step : rim * (step + 1)]
                start += whole
            at += rim * high
        for step in range(rim):
            row = high3 - rim + step if last else step
            pack_buf[start : start + span, :] = three_buf[row, :span, :]
            start += span
    even = lax.rem(here_ref[0], 2) == 0
    low, high = low_buf[...], high_buf[...]
    first_ref[...] = jnp.where(even, high, low).astype(bf16)
    second_ref[...] = jnp.where(even, low, high).astype(bf16)


def tap_terms(small, weight_ref, first, store):
    channels = weight_ref.shape[3]
    for tap in range(9):
        weight = weight_ref[tap // 3, tap % 3, first : first + channels, :]
        store(tap, dot(small, weight).astype(bf16))


def late_kernel(sizes, plans, top_count, here_ref, bias_ref, join_ref, *refs):
    tops, refs = refs[:top_count], refs[top_count:]
    top_ref, base_ref, matrices, refs = refs[0], refs[1], refs[2 : 1 + len(plans)], refs[1 + len(plans) :]
    top_buf, small_buf, terms_buf = refs
    high4, wide4 = sizes[3]
    here = (here_ref[0], here_ref[1])
    total = tops[0][...].astype(f32)
    for ref in tops[1:]:
        total = total + ref[...].astype(f32)
    top_buf[...] = jnp.zeros_like(top_buf)
    top_buf[:, : wide4 + 2 * rim, :] = jnp.maximum(total + bias_ref[4:5, :][None], 0.0)
    top_ref[...] = top_buf[...].reshape(top_ref.shape).astype(bf16)
    tall, broad = compact_shape((high4, wide4), 1)
    small_buf[...] = jnp.zeros_like(small_buf)
    for row in range(tall):
        small_buf[row * broad : (row + 1) * broad, :] = top_buf[
            row + rim - 1, rim - 1 : rim - 1 + broad, :
        ]
    lanes, channels = small_buf.shape

    def store(tap, value):
        terms_buf[tap * lanes : (tap + 1) * lanes, :] = value

    tap_terms(small_buf[...].astype(bf16), join_ref, 3 * channels, store)
    base_ref[...] = dot(stretch_matrix(here, *plans[0]), terms_buf[...])
    for plan, matrix in zip(plans[1:], matrices):
        matrix[...] = stretch_matrix(here, *plan)


def tail_kernel(sizes, part_count, here_ref, *refs):
    (high1, wide1), (high2, wide2), (high3, wide3), _, (row_count, col_count) = sizes
    quarters, refs = refs[:part_count], refs[part_count:]
    (
        top_ref,
        base_ref,
        lat1_ref,
        lat2_ref,
        lat3_ref,
        first_ref,
        second_ref,
        before_ref,
        after_ref,
        bias_ref,
        smooth_w,
        join_w,
        up3_ref,
        up2_ref,
        up1_ref,
        spread3_ref,
        out_ref,
        lat1_buf,
        lat2_buf,
        lat3_buf,
        pyr1_buf,
        pyr2_buf,
        pyr3_buf,
        moved1_buf,
        moved2_buf,
        moved3_buf,
        acc_buf,
        sums_buf,
        stack_buf,
        small3_buf,
        small2_buf,
        terms3_buf,
        terms2_buf,
        above_buf,
        below_buf,
        result_buf,
        sems,
    ) = refs
    channels = bias_ref.shape[1]

    even = lax.rem(here_ref[0], 2) == 0
    first, second = first_ref[...].astype(f32), second_ref[...].astype(f32)
    above_buf[...] = jnp.where(even, second, first)
    below_buf[...] = jnp.where(even, first, second)
    side_start = before_ref.shape[0] - rim * (high1 + high2)
    row_start = 0
    for ref, buf, high, wide in (
        (lat1_ref, lat1_buf, high1, wide1),
        (lat2_ref, lat2_buf, high2, wide2),
        (lat3_ref, lat3_buf, high3, wide3 + 2 * rim),
    ):
        buf[...] = jnp.zeros_like(buf)
        whole = wide
        if buf is lat3_buf:
            buf[rim : rim + high, :wide, :] = ref[...].astype(f32)
        else:
            whole = wide + 2 * rim
            buf[rim : rim + high, rim : rim + wide, :] = ref[...].astype(f32)
            for source, col, keep in (
                (before_ref, 0, here_ref[1] > 0),
                (after_ref, rim + wide, here_ref[1] < col_count - 1),
            ):
                sides = source[side_start : side_start + rim * high, :].astype(f32)
                sides = jnp.where(keep, sides, 0.0)
                for row in range(high):
                    buf[rim + row, col : col + rim, :] = sides[rim * row : rim * row + rim]
            side_start += rim * high
        for source, row in ((above_buf, 0), (below_buf, rim + high)):
            both = source[row_start : row_start + rim * whole, :]
            for step in range(rim):
                buf[row + step, :whole, :] = both[step * whole : (step + 1) * whole]
        row_start += rim * whole

    shape1, shape2, shape3 = lat1_buf.shape[:2], lat2_buf.shape[:2], lat3_buf.shape[:2]

    def put(value, plain, moved):
        plain[0 : value.shape[0], :] = value.astype(bf16)
        later = jnp.concatenate([jnp.zeros((8, channels), f32), value, jnp.zeros((8, channels), f32)])
        moved[0 : later.shape[0], :] = later.astype(bf16)

    for lat_buf, matrix, source, out in (
        (lat3_buf, up3_ref, top_ref, (pyr3_buf, moved3_buf)),
        (lat2_buf, up2_ref, pyr3_buf, (pyr2_buf, moved2_buf)),
        (lat1_buf, up1_ref, pyr2_buf, (pyr1_buf, moved1_buf)),
    ):
        source = source[...]
        total = lat_buf[...].reshape(-1, channels) + dot(matrix[...], source)
        put(total, *out)

    def conv(source, shape, weight_at, rows):
        pitch = shape[1]
        span = rows * pitch
        plain, moved = source
        shift = pitch % 16
        stacked = jnp.concatenate(
            [
                plain[0:span, :],
                (moved if shift else plain)[pitch + shift : pitch + shift + span, :],
                plain[2 * pitch : 2 * pitch + span, :],
            ],
            axis=1,
        )
        for col_tap in range(3):
            weight = weight_at(col_tap)
            total = dot(stacked, weight.reshape(-1, channels))
            acc_buf[col_tap, :rows, :pitch, :] = total.reshape(rows, pitch, channels)

    def taps_total(rows, whole):
        total = acc_buf[0, :rows, 0:whole, :]
        for col_tap in (1, 2):
            total = total + acc_buf[col_tap, :rows, col_tap : whole + col_tap, :]
        return total

    def smooth(number, source, shape, wide):
        rows = shape[0] - 2
        conv(source, shape, lambda j: smooth_w[number, :, j], rows)
        total = taps_total(rows, wide + 2)
        return jnp.maximum(total + bias_ref[8 + number : 9 + number, :][None], 0.0)

    value = smooth(2, (pyr3_buf, moved3_buf), shape3, wide3)
    tall, broad = compact_shape((high3, wide3), 1)
    small3_buf[...] = jnp.zeros_like(small3_buf)
    for row in range(tall):
        small3_buf[row * broad : (row + 1) * broad, :] = value[row]
    lanes3 = small3_buf.shape[0]

    def store3(tap, value):
        terms3_buf[tap * lanes3 : (tap + 1) * lanes3, :] = value

    tap_terms(small3_buf[...].astype(bf16), join_w, 2 * channels, store3)

    rows2, whole2 = compact_shape((high2, wide2), 1)
    sums_buf[:rows2, :whole2, :] = smooth(1, (pyr2_buf, moved2_buf), shape2, wide2)
    half = (high2 // cuts2, wide2 // cuts2)
    tall, broad = compact_shape(half, 1)
    lanes2 = small2_buf.shape[0] // part_count
    small2_buf[...] = jnp.zeros_like(small2_buf)
    for part in range(part_count):
        row0, col0 = part // cuts2 * half[0], part % cuts2 * half[1]
        for row in range(tall):
            start = part * lanes2 + row * broad
            small2_buf[start : start + broad, :] = sums_buf[row0 + row, col0 : col0 + broad, :]

    def store2(tap, value):
        for part in range(part_count):
            start = (part * 9 + tap) * lanes2
            terms2_buf[start : start + lanes2, :] = value[part * lanes2 : (part + 1) * lanes2]

    tap_terms(small2_buf[...].astype(bf16), join_w, channels, store2)

    rows1, pitch1 = window_shape((high1, wide1), 1)
    value = smooth(0, (pyr1_buf, moved1_buf), shape1, wide1)
    down = here_ref[0] * high1 - 1 + lax.broadcasted_iota(jnp.int32, (rows1, 1, 1), 0)
    across = here_ref[1] * wide1 - 1 + lax.broadcasted_iota(jnp.int32, (1, wide1 + 2, 1), 1)
    inside = (down >= 0) & (down < high1 * row_count) & (across >= 0) & (across < wide1 * col_count)
    sums_buf[:rows1, : wide1 + 2, :] = jnp.where(inside, value, 0.0)
    put(sums_buf[...].reshape(rows1 * pitch1, channels), stack_buf, moved1_buf)
    conv((stack_buf, moved1_buf), (rows1, pitch1), lambda j: join_w[:, j, 0:channels], high1)
    total = taps_total(high1, wide1)
    spread = base_ref[...] + dot(spread3_ref[...], terms3_buf[...])
    sums_buf[:high1, :wide1, :] = total + spread.reshape(high1, wide1, channels)
    tall, broad = high1 // cuts2, wide1 // cuts2
    copies = []
    for part, matrix in enumerate(quarters):
        terms = terms2_buf[part * 9 * lanes2 : (part + 1) * 9 * lanes2, :]
        value = dot(matrix[...], terms).reshape(tall, broad, channels)
        row0, col0 = part // cuts2 * tall, part % cuts2 * broad
        value = value + sums_buf[row0 : row0 + tall, col0 : col0 + broad, :]
        value = jnp.maximum(value + bias_ref[11:12, :][None], 0.0)
        result_buf[part] = value.astype(bf16)
        target = out_ref.at[pl.ds(row0, tall), pl.ds(col0, broad), :]
        copies.append(pltpu.make_async_copy(result_buf.at[part], target, sems.at[part]))
        copies[-1].start()
    for copy in copies:
        copy.wait()


def tail(here, top, base, lats, swapped, before, after, biases, weights, matrices, quarters, sizes):
    one, _, _, _, _ = sizes
    channels = biases.shape[1]
    shapes = [window_shape(size, rim) for size in sizes[:3]]
    (rows1, pitch1), (rows2, pitch2), (rows3, pitch3) = shapes
    small3, small2 = matrices[-1].shape[1] // 9, quarters[0].shape[1] // 9 * len(quarters)
    inputs = (*quarters, top, base, *lats, *swapped, before, after, biases, *weights, *matrices)
    return pl.pallas_call(
        functools.partial(tail_kernel, sizes, len(quarters)),
        out_shape=jax.ShapeDtypeStruct((*one, channels), bf16),
        in_specs=[smem_spec] + [vmem_spec] * len(inputs),
        out_specs=hbm_spec,
        scratch_shapes=[
            pltpu.VMEM((rows1, pitch1, channels), f32),
            pltpu.VMEM((rows2, pitch2, channels), f32),
            pltpu.VMEM((rows3, pitch3, channels), f32),
            pltpu.VMEM((rows1 * pitch1, channels), bf16),
            pltpu.VMEM((rows2 * pitch2, channels), bf16),
            pltpu.VMEM((rows3 * pitch3, channels), bf16),
            pltpu.VMEM((rows1 * pitch1 + 16, channels), bf16),
            pltpu.VMEM((rows2 * pitch2 + 16, channels), bf16),
            pltpu.VMEM((rows3 * pitch3 + 16, channels), bf16),
            pltpu.VMEM((3, rows1 - 2, pitch1, channels), f32),
            pltpu.VMEM((rows1 - 2, pitch1, channels), f32),
            pltpu.VMEM(((rows1 - 2) * pitch1, channels), bf16),
            pltpu.VMEM((small3, channels), f32),
            pltpu.VMEM((small2, channels), f32),
            pltpu.VMEM((9 * small3, channels), bf16),
            pltpu.VMEM((9 * small2, channels), bf16),
            pltpu.VMEM(swapped[0].shape, f32),
            pltpu.VMEM(swapped[0].shape, f32),
            pltpu.VMEM((len(quarters), one[0] // cuts2, one[1] // cuts2, channels), bf16),
            pltpu.SemaphoreType.DMA((len(quarters),)),
        ],
        compiler_params=pltpu.CompilerParams(vmem_limit_bytes=30 * 1024 * 1024),
        cost_estimate=pl.CostEstimate(
            flops=8_000_000_000, bytes_accessed=12_000_000, transcendentals=0
        ),
    )(here, *inputs)


def local(
    level_one,
    level_two,
    level_three,
    level_four,
    bin_weight,
    neck_feature,
    neck_pooled,
    lateral_one,
    lateral_two,
    lateral_three,
    smooth_weight,
    join_weight,
    biases,
):
    row_count = lax.axis_size("row")
    col_count = lax.axis_size("col")
    here = jnp.stack([lax.axis_index("row"), lax.axis_index("col")]).astype(jnp.int32)
    high1, wide1 = level_one.shape[:2]
    high2, wide2 = level_two.shape[:2]
    high3, wide3 = level_three.shape[0], level_three.shape[1] // col_count
    high4, grid_cols, part_four = level_four.shape
    wide4 = grid_cols // col_count
    channels = bin_weight.shape[2]
    grid_rows = high4 * row_count
    table = cell_table(grid_rows, grid_cols)
    cells = table.shape[0]
    turned = jnp.asarray(np.ascontiguousarray(table.T))
    table = jnp.asarray(table)

    def shape(dims, kind=bf16):
        return jax.ShapeDtypeStruct(dims, kind)

    others = [shifted(level_four, "row", shift) for shift in range(1, row_count)]
    window_rows = high3 * (wide3 + 2 * rim)
    side_rows = rim * (high1 + high2)
    used = (level_one, lateral_one, level_two, lateral_two, level_three, lateral_three)
    kept = (biases, level_four, table, bin_weight, turned)
    lat1, lat2, *rest = call(
        functools.partial(lateral_kernel, col_count, len(kept)),
        [shape((high1, wide1, channels)), shape((high2, wide2, channels))]
        + [shape((window_rows + side_rows, channels))] * col_count
        + [shape(value.shape, value.dtype) for value in kept],
        [smem_spec] + [hbm_spec] * (len(used) + len(kept)),
        [pltpu.VMEM(value.shape, value.dtype) for value in used]
        + [
            pltpu.VMEM((high3, level_three.shape[1] + 8, channels), f32),
            pltpu.VMEM((high1, wide1, channels), f32),
            pltpu.VMEM((high2, wide2, channels), f32),
            pltpu.VMEM((window_rows + side_rows, channels), f32),
            pltpu.SemaphoreType.DMA((len(used) + len(kept),)),
        ],
        300_000_000,
        4_000_000,
    )(here, *(in_hbm(value) for value in (*used, *kept)))
    pieces = rest[:col_count]
    bias_table, level_four, table, bin_weight, turned = rest[col_count:]
    blocks = [level_four] + others
    near = (1, col_count - 1)
    messages = call(
        functools.partial(bins_kernel, row_count, col_count, window_rows),
        [
            shape((window_rows + cells + (side_rows if shift in near else 0), channels))
            for shift in range(col_count)
        ],
        [smem_spec] + [vmem_spec] * (2 + row_count + col_count),
        [],
        100_000_000,
        1_000_000,
    )(here, table, bin_weight, *blocks, *pieces)

    received = [messages[0]] + [
        shifted(messages[shift], "col", shift) for shift in range(1, col_count)
    ]
    rows = high4 + 2 * rim
    sizes = (
        (high1, wide1),
        (high2, wide2),
        (high3, wide3),
        (high4, wide4),
        (row_count, col_count),
    )
    plans, late_plans = stretches(sizes)
    late = (neck_pooled, smooth_weight, join_weight)
    taps, neck_pooled, smooth_weight, join_weight, *matrices = call(
        functools.partial(feature_kernel, row_count, plans),
        [shape((3, rows * grid_cols, channels), f32)]
        + [shape(value.shape) for value in late]
        + [shape(matrix_shape(plan)) for plan in plans],
        [smem_spec, hbm_spec] + [vmem_spec] * row_count + [hbm_spec] * len(late),
        [
            pltpu.VMEM(neck_feature.shape, bf16),
            pltpu.VMEM((grid_rows + 2 * rim + 2, grid_cols, part_four), bf16),
            pltpu.SemaphoreType.DMA((1 + len(late),)),
        ],
        700_000_000,
        12_000_000,
    )(here, in_hbm(neck_feature), *blocks, *(in_hbm(value) for value in late))
    span4 = wide4 + 2 * rim
    windows = call(
        functools.partial(neck_kernel, row_count, col_count, high4, window_rows),
        [shape((rows, span4, channels))] * col_count,
        [smem_spec] + [vmem_spec] * (5 + col_count),
        [
            pltpu.VMEM((cells, channels), f32),
            pltpu.VMEM((3, rows * grid_cols + 16, channels), f32),
            pltpu.VMEM((rows, grid_cols + 16, channels), f32),
        ],
        300_000_000,
        3_000_000,
    )(here, table, turned, neck_pooled, bias_table, taps, *received)

    tops = [windows[0]] + [shifted(windows[shift], "col", shift) for shift in range(1, col_count)]
    span3 = wide3 + 2 * rim
    packed = rim * (wide1 + wide2 + wide3 + 6 * rim)
    lat3, first_rows, second_rows = call(
        functools.partial(rows_kernel, col_count, high3, wide3),
        [shape((high3, span3, channels))] + [shape((packed, channels))] * 2,
        [smem_spec] + [vmem_spec] * (3 + col_count),
        [
            pltpu.VMEM((high3, (span3 + 7) // 8 * 8, channels), f32),
            pltpu.VMEM((packed, channels), f32),
            pltpu.VMEM((packed, channels), f32),
        ],
        1_000_000,
        1_000_000,
    )(here, bias_table, lat1, lat2, *received)
    swapped = pair_swap(first_rows, second_rows, "row")
    small = late_plans[0][8]
    top_pitch = window_shape((high4, wide4), rim)[1]
    top, base, *quarters = call(
        functools.partial(late_kernel, sizes, late_plans, col_count),
        [
            shape((rows * top_pitch, channels)),
            shape((high1 * wide1, channels), f32),
        ]
        + [shape(matrix_shape(plan)) for plan in late_plans[1:]],
        [smem_spec] + [vmem_spec] * (2 + col_count),
        [
            pltpu.VMEM((rows, top_pitch, channels), f32),
            pltpu.VMEM((small, channels), f32),
            pltpu.VMEM((9 * small, channels), bf16),
        ],
        700_000_000,
        5_000_000,
    )(here, bias_table, join_weight, *tops)
    return tail(
        here,
        top,
        base,
        (lat1, lat2, lat3),
        swapped,
        received[1],
        received[-1],
        bias_table,
        (smooth_weight, join_weight),
        matrices,
        quarters,
        sizes,
    )


def solution(mesh):
    placed = (
        P(("grp", "row"), "col", None),
        P(("grp", "row"), "col", None),
        P(("grp", "row"), None, "col"),
        P(("grp", "row"), None, "col"),
        P(None, "col", None),
        P(None, None, "col", None),
        P(None, None, "col", None),
        P(),
        P(),
        P(),
        P(),
        P(),
        P(),
    )
    return jax.shard_map(
        local, mesh=mesh, in_specs=placed, out_specs=P(("grp", "row"), "col", None), check_vma=False
    )
```

```python
import functools

import jax
import jax.numpy as jnp
import numpy as np
from jax import lax
from jax.experimental import pallas as pl
from jax.experimental.pallas import tpu as pltpu
from jax.sharding import PartitionSpec as P

highest = lax.Precision.HIGHEST
bin_sides = (1, 2, 3, 6)
rim = 2
cuts2 = 2
f32 = jnp.float32
bf16 = jnp.bfloat16
vmem_spec = pl.BlockSpec(memory_space=pltpu.VMEM)
hbm_spec = pl.BlockSpec(memory_space=pltpu.HBM)
smem_spec = pl.BlockSpec(memory_space=pltpu.SMEM)
params = pltpu.CompilerParams(vmem_limit_bytes=30 * 1024 * 1024)


def shifted(value, axis, shift):
    count = lax.axis_size(axis)
    return lax.ppermute(value, axis, [(i, (i + shift) % count) for i in range(count)])


def pair_swap(first, second, axis):
    count = lax.axis_size(axis)

    def pairs(start):
        return [
            edge
            for i in range(start, count - 1, 2)
            for edge in ((i, i + 1), (i + 1, i))
        ]

    return lax.ppermute(first, axis, pairs(0)), lax.ppermute(second, axis, pairs(1))


def cell_table(extent_rows, extent_cols):
    rows = []
    for number, side in enumerate(bin_sides):
        for i in range(side):
            for j in range(side):
                top, low = i * extent_rows // side, -(-(i + 1) * extent_rows // side)
                left, right = j * extent_cols // side, -(-(j + 1) * extent_cols // side)
                rows.append([number, side, i, j, top, low, left, right, (low - top) * (right - left)])
    padded = (len(rows) + 15) // 16 * 16
    table = np.zeros((padded, 16), np.float32)
    table[:, 0] = -1.0
    table[:, 1] = 1.0
    table[:, 8] = 1.0
    table[: len(rows), :9] = np.array(rows, np.float32)
    return table


def dot(a, b):
    rows = a.shape[0]
    half = (rows // 2 + 15) // 16 * 16
    if half >= rows:
        return jnp.dot(a, b, preferred_element_type=f32)
    return jnp.concatenate(
        [
            jnp.dot(a[:half], b, preferred_element_type=f32),
            jnp.dot(a[half:], b, preferred_element_type=f32),
        ],
        axis=0,
    )


def in_hbm(value):
    return pltpu.with_memory_space_constraint(value, pltpu.HBM)


def call(kernel, outs, specs, scratch, flops, moved):
    return pl.pallas_call(
        kernel,
        out_shape=outs,
        in_specs=specs,
        out_specs=jax.tree.map(lambda _: vmem_spec, outs),
        scratch_shapes=scratch,
        compiler_params=params,
        cost_estimate=pl.CostEstimate(flops=flops, bytes_accessed=moved, transcendentals=0),
    )


def wrap(value, count):
    return lax.rem(value + count, count)


def floor_div(value, step):
    return jnp.floor((value + 0.5) / step)


def stretch_matrix(out_ref, here, out_shape, out_border, in_shape, in_border, factor, out_size, in_size, counts, lanes, taps=1):
    out_rows, out_pitch = out_shape
    lane = lax.broadcasted_iota(jnp.int32, (1, lanes * taps * taps), 1).astype(f32)
    tap = floor_div(lane, lanes)
    place = lane - tap * lanes
    row_tap = floor_div(tap, taps)
    col_tap = tap - row_tap * taps
    place_row = floor_div(place, in_shape[1])
    place_col = place - place_row * in_shape[1]

    def weights(axis, length, targets, tap_here):
        whole = float(in_size[axis] * counts[axis])
        first_out = (here[axis] * out_size[axis] - out_border[axis]).astype(f32) - (taps // 2)
        first_in = (here[axis] * in_size[axis] - in_border[axis]).astype(f32)
        output = first_out + tap_here + lax.broadcasted_iota(jnp.int32, (length, 1), 0).astype(f32)
        source = (output + 0.5) * (1.0 / factor) - 0.5
        source = jnp.minimum(jnp.maximum(source, 0.0), whole - 1.0)
        inside = jnp.where((output >= 0.0) & (output < whole * factor), 1.0, 0.0)
        return jnp.maximum(0.0, 1.0 - jnp.abs(source - (first_in + targets))) * inside

    down = weights(0, out_rows, place_row, row_tap)
    across = weights(1, out_pitch, place_col, col_tap)
    for row in range(0, out_rows, 2):
        pair = [down[step : step + 1, :] * across for step in range(row, min(row + 2, out_rows))]
        start = row * out_pitch
        value = jnp.concatenate(pair, axis=0)
        out_ref[start : start + value.shape[0], :] = value.astype(bf16)


def pitch_of(width):
    return (width + 15) // 16 * 16


def window_shape(size, border):
    return size[0] + 2 * border, (size[1] + 2 * border + 7) // 8 * 8


def compact_shape(size, border):
    return size[0] + 2 * border, size[1] + 2 * border


def stretches(sizes):
    one, two, three, four, counts = sizes

    def pyramid(out, source):
        shape = window_shape(source, rim)
        borders = (rim, rim)
        factor = out[0] // source[0]
        return (
            window_shape(out, rim), borders, shape, borders, factor, out, source, counts, shape[0] * shape[1]
        )

    def join(source, cuts, part):
        tile = (one[0] // cuts, one[1] // cuts)
        small = (source[0] // cuts, source[1] // cuts)
        shape = compact_shape(small, 1)
        out_border = (-part[0] * tile[0], -part[1] * tile[1])
        in_border = (1 - part[0] * small[0], 1 - part[1] * small[1])
        factor = one[0] // source[0]
        lanes = pitch_of(shape[0] * shape[1])
        return tile, out_border, shape, in_border, factor, one, source, counts, lanes, 3

    parts = [(i, j) for i in range(cuts2) for j in range(cuts2)]
    return (
        (pyramid(three, four), pyramid(two, three), pyramid(one, two), join(three, 1, (0, 0))),
        (join(four, 1, (0, 0)), *(join(two, cuts2, part) for part in parts)),
    )


def matrix_shape(plan):
    return plan[0][0] * plan[0][1], plan[8] * (plan[9] if len(plan) > 9 else 1) ** 2


def lateral_kernel(col_count, kept_count, here_ref, *refs):
    sources, refs = refs[: 6 + kept_count], refs[6 + kept_count :]
    (lat1_ref, lat2_ref), refs = refs[:2], refs[2:]
    pieces, refs = refs[:col_count], refs[col_count:]
    kept, refs = refs[:kept_count], refs[kept_count:]
    fetched, (wide_buf, one_buf, two_buf, piece_buf, sems) = refs[:6], refs[6:]
    copies = [
        pltpu.make_async_copy(source, target, sems.at[number])
        for number, (source, target) in enumerate(zip(sources, (*fetched, *kept)))
    ]
    for copy in copies:
        copy.start()
    one_ref, w1_ref, two_ref, w2_ref, three_ref, w3_ref = fetched
    bias_ref = kept[0]
    copies[6].wait()
    channels = w1_ref.shape[1]
    for number, (source, weight, row, buf, out) in enumerate(
        (
            (one_ref, w1_ref, 5, one_buf, lat1_ref),
            (two_ref, w2_ref, 6, two_buf, lat2_ref),
        )
    ):
        copies[2 * number].wait()
        copies[2 * number + 1].wait()
        high, wide, depth = source.shape
        value = dot(source[...].reshape(high * wide, depth), weight[...])
        value = jnp.maximum(value + bias_ref[row : row + 1, :], 0.0).reshape(high, wide, channels)
        buf[...] = value
        out[...] = value.astype(bf16)
    high3, whole3, share = three_ref.shape
    wide3 = whole3 // col_count
    col_here = here_ref[1]
    copies[4].wait()
    copies[5].wait()
    weight = w3_ref[pl.ds(pl.multiple_of(col_here * share, 16), share), :]
    value = dot(three_ref[...].reshape(high3 * whole3, share), weight)
    wide_buf[...] = jnp.zeros_like(wide_buf)
    wide_buf[:, rim : rim + whole3, :] = value.reshape(high3, whole3, channels)
    span = wide3 + 2 * rim
    for shift, piece in enumerate(pieces):
        target = wrap(col_here + shift, col_count)
        for row in range(high3):
            piece_buf[row * span : (row + 1) * span, :] = wide_buf[
                row, pl.ds(pl.multiple_of(target * wide3, 8), span), :
            ]
        start = high3 * span
        for buf in (one_buf, two_buf):
            high, wide = buf.shape[:2]
            first = wide - rim if shift == 1 else 0
            for row in range(high):
                piece_buf[start : start + rim, :] = buf[row, first : first + rim, :]
                start += rim
        piece[...] = piece_buf[...].astype(bf16)
    for copy in copies[7:]:
        copy.wait()


def bins_kernel(row_count, col_count, window_rows, here_ref, table_ref, weight_ref, *refs):
    blocks, pieces, messages = (
        refs[:row_count],
        refs[row_count : row_count + col_count],
        refs[row_count + col_count :],
    )
    table = table_ref[...]
    high, wide, depth = blocks[0].shape
    place = lax.broadcasted_iota(jnp.int32, (1, high * wide), 1).astype(f32)
    place_row = floor_div(place, wide)
    place_col = place - place_row * wide
    in_cols = (place_col >= table[:, 6:7]) & (place_col < table[:, 7:8])
    pooled = None
    for shift, block in enumerate(blocks):
        row = place_row + (wrap(here_ref[0] - shift, row_count) * high).astype(f32)
        inside = in_cols & (row >= table[:, 4:5]) & (row < table[:, 5:6])
        inside = jnp.where(inside, 1.0, 0.0).astype(bf16)
        term = dot(inside, block[...].reshape(high * wide, depth))
        pooled = term if pooled is None else pooled + term
    pooled = (pooled / table[:, 8:9]).astype(bf16)
    bins = None
    for number in range(len(bin_sides)):
        term = jnp.where(table[:, 0:1] == number, dot(pooled, weight_ref[number]), 0.0)
        bins = term if bins is None else bins + term
    bins = bins.astype(bf16)
    cells = bins.shape[0]
    for piece, message in zip(pieces, messages):
        message[0:window_rows, :] = piece[0:window_rows, :]
        message[window_rows : window_rows + cells, :] = bins
        if message.shape[0] > window_rows + cells:
            message[window_rows + cells :, :] = piece[window_rows:, :]


def feature_kernel(row_count, plans, here_ref, weight_hbm, *refs):
    blocks, refs = refs[:row_count], refs[row_count:]
    late, refs = refs[:1], refs[1:]
    out_ref, kept, matrices = refs[0], refs[1:2], refs[2 : 2 + len(plans)]
    weight_ref, grid_buf, sems = refs[2 + len(plans) :]
    copies = [
        pltpu.make_async_copy(source, target, sems.at[number])
        for number, (source, target) in enumerate(zip((weight_hbm, *late), (weight_ref, *kept)))
    ]
    for copy in copies:
        copy.start()
    here = (here_ref[0], here_ref[1])
    for plan, matrix in zip(plans, matrices):
        stretch_matrix(matrix, here, *plan)
    high, wide, depth = blocks[0].shape
    grid_buf[...] = jnp.zeros_like(grid_buf)
    for shift, block in enumerate(blocks):
        row = wrap(here_ref[0] - shift, row_count) * high + rim + 1
        grid_buf[pl.ds(row, high)] = block[...]
    rows = out_ref.shape[1] // wide
    window = grid_buf[pl.ds(here_ref[0] * high, rows + 2)].reshape((rows + 2) * wide, depth)
    copies[0].wait()
    for col_tap in range(3):
        total = dot(window[0 : rows * wide], weight_ref[0, col_tap])
        for row_tap in (1, 2):
            total = total + dot(
                window[row_tap * wide : (row_tap + rows) * wide], weight_ref[row_tap, col_tap]
            )
        out_ref[col_tap] = total
    for copy in copies[1:]:
        copy.wait()


def neck_kernel(
    row_count, col_count, high, window_rows, here_ref, table_ref, turned_ref, weight_ref, bias_ref, taps_ref, *refs
):
    messages, refs = refs[:col_count], refs[col_count:]
    windows, (bins_buf, acc_buf, term_buf) = refs[:col_count], refs[col_count:]
    rows, span, channels = windows[0].shape
    wide = taps_ref.shape[1] // rows
    width4 = span - 2 * rim
    table = table_ref[...]
    cells = table.shape[0]
    bins = messages[0][window_rows : window_rows + cells, :].astype(f32)
    for message in messages[1:]:
        bins = bins + message[window_rows : window_rows + cells, :].astype(f32)
    bias = jnp.zeros((cells, channels), f32)
    for number in range(len(bin_sides)):
        bias = jnp.where(table[:, 0:1] == number, bias_ref[number : number + 1, :], bias)
    share = weight_ref.shape[2]
    first = here_ref[1] * share
    mine = table[:, 0:1] == (first // channels).astype(f32)
    bins_buf[...] = jnp.where(mine, jnp.maximum(bins + bias, 0.0), 0.0)
    if share == channels:
        binned = bins_buf[...]
    else:
        binned = bins_buf[:, pl.ds(pl.multiple_of(lax.rem(first, channels), 128), share)]
    place = lax.broadcasted_iota(jnp.int32, ((rows + 2) * wide, 1), 0).astype(f32)
    place_row = floor_div(place, wide)
    place_col = place - place_row * wide
    place_row = place_row + (here_ref[0] * high - rim - 1).astype(f32)
    grid_rows = float(high * row_count)
    sides = turned_ref[1:2, :]

    def weights(position, extent, index):
        source = (position + 0.5) * sides / extent - 0.5
        source = jnp.minimum(jnp.maximum(source, 0.0), sides - 1.0)
        return jnp.maximum(0.0, 1.0 - jnp.abs(source - index))

    spread = weights(place_row, grid_rows, turned_ref[2:3, :])
    spread = spread * weights(place_col, float(wide), turned_ref[3:4, :])
    spread = jnp.where((place_row >= 0.0) & (place_row < grid_rows), spread, 0.0)
    ppm = jnp.dot(spread, binned, precision=highest, preferred_element_type=f32).astype(bf16)
    size = rows * wide
    for col_tap in range(3):
        total = taps_ref[col_tap]
        for row_tap in range(3):
            total = total + dot(
                ppm[row_tap * wide : row_tap * wide + size], weight_ref[row_tap, col_tap]
            )
        acc_buf[col_tap, 8 : 8 + size, :] = total
    col = place_col[0:size]
    total = (
        acc_buf[1, 8 : 8 + size, :]
        + jnp.where(col > 0.0, acc_buf[0, 7 : 7 + size, :], 0.0)
        + jnp.where(col < wide - 1.0, acc_buf[2, 9 : 9 + size, :], 0.0)
    )
    term_buf[...] = jnp.zeros_like(term_buf)
    term_buf[:, rim : rim + wide, :] = total.reshape(rows, wide, channels)
    for shift, window in enumerate(windows):
        target = wrap(here_ref[1] + shift, col_count)
        window[...] = term_buf[:, pl.ds(pl.multiple_of(target * width4, 8), span), :].astype(bf16)


def rows_kernel(col_count, high3, wide3, here_ref, bias_ref, lat1_ref, lat2_ref, *refs):
    messages, (lat3_ref, first_ref, second_ref, three_buf, low_buf, high_buf) = (
        refs[:col_count],
        refs[col_count:],
    )
    span = wide3 + 2 * rim
    total = messages[0][0 : high3 * span, :].astype(f32)
    for message in messages[1:]:
        total = total + message[0 : high3 * span, :].astype(f32)
    total = jnp.maximum(total + bias_ref[7:8, :], 0.0)
    col_here = here_ref[1]
    place = lax.broadcasted_iota(jnp.int32, (span, 1), 0) + col_here * wide3 - rim
    inside = (place >= 0) & (place < wide3 * col_count)
    for row in range(high3):
        three_buf[row, :span, :] = jnp.where(inside, total[row * span : (row + 1) * span], 0.0)
    lat3_ref[...] = three_buf[:, :span, :].astype(bf16)
    high1, wide1 = lat1_ref.shape[:2]
    high2, wide2 = lat2_ref.shape[:2]
    before, after = messages[1], messages[col_count - 1]
    sides_at = before.shape[0] - rim * (high1 + high2)
    for pack_buf, last in ((low_buf, False), (high_buf, True)):
        start, at = 0, sides_at
        for lat, high, wide in ((lat1_ref, high1, wide1), (lat2_ref, high2, wide2)):
            whole = wide + 2 * rim
            first = high - rim if last else 0
            left = before[at + rim * first : at + rim * (first + rim), :].astype(f32)
            right = after[at + rim * first : at + rim * (first + rim), :].astype(f32)
            left = jnp.where(col_here > 0, left, 0.0)
            right = jnp.where(col_here < col_count - 1, right, 0.0)
            for step in range(rim):
                pack_buf[start : start + rim, :] = left[rim * step : rim * (step + 1)]
                pack_buf[start + rim : start + rim + wide, :] = lat[first + step].astype(f32)
                pack_buf[start + rim + wide : start + whole, :] = right[rim * step : rim * (step + 1)]
                start += whole
            at += rim * high
        for step in range(rim):
            row = high3 - rim + step if last else step
            pack_buf[start : start + span, :] = three_buf[row, :span, :]
            start += span
    even = lax.rem(here_ref[0], 2) == 0
    low, high = low_buf[...], high_buf[...]
    first_ref[...] = jnp.where(even, high, low).astype(bf16)
    second_ref[...] = jnp.where(even, low, high).astype(bf16)


def tap_terms(small, weight_ref, first, store):
    channels = weight_ref.shape[3]
    for tap in range(9):
        weight = weight_ref[tap // 3, tap % 3, first : first + channels, :]
        store(tap, dot(small, weight).astype(bf16))


def late_kernel(sizes, plans, top_count, here_ref, bias_ref, join_ref, *refs):
    tops, refs = refs[:top_count], refs[top_count:]
    top_ref, base_ref, matrices, refs = refs[0], refs[1], refs[2 : 1 + len(plans)], refs[1 + len(plans) :]
    top_buf, small_buf, terms_buf, matrix_buf = refs
    high4, wide4 = sizes[3]
    here = (here_ref[0], here_ref[1])
    total = tops[0][...].astype(f32)
    for ref in tops[1:]:
        total = total + ref[...].astype(f32)
    top_buf[...] = jnp.zeros_like(top_buf)
    top_buf[:, : wide4 + 2 * rim, :] = jnp.maximum(total + bias_ref[4:5, :][None], 0.0)
    top_ref[...] = top_buf[...].reshape(top_ref.shape).astype(bf16)
    tall, broad = compact_shape((high4, wide4), 1)
    small_buf[...] = jnp.zeros_like(small_buf)
    for row in range(tall):
        small_buf[row * broad : (row + 1) * broad, :] = top_buf[
            row + rim - 1, rim - 1 : rim - 1 + broad, :
        ]
    lanes, channels = small_buf.shape

    def store(tap, value):
        terms_buf[tap * lanes : (tap + 1) * lanes, :] = value

    tap_terms(small_buf[...].astype(bf16), join_ref, 3 * channels, store)
    for plan, matrix in zip(plans, (matrix_buf, *matrices)):
        stretch_matrix(matrix, here, *plan)
    base_ref[...] = dot(matrix_buf[...], terms_buf[...])


def tail_kernel(sizes, part_count, here_ref, *refs):
    (high1, wide1), (high2, wide2), (high3, wide3), _, (row_count, col_count) = sizes
    quarters, refs = refs[:part_count], refs[part_count:]
    (
        top_ref,
        base_ref,
        lat1_ref,
        lat2_ref,
        lat3_ref,
        first_ref,
        second_ref,
        before_ref,
        after_ref,
        bias_ref,
        smooth_w,
        join_w,
        up3_ref,
        up2_ref,
        up1_ref,
        spread3_ref,
        out_ref,
        lat1_buf,
        lat2_buf,
        lat3_buf,
        pyr1_buf,
        pyr2_buf,
        pyr3_buf,
        moved1_buf,
        moved2_buf,
        moved3_buf,
        acc_buf,
        sums_buf,
        stack_buf,
        small3_buf,
        small2_buf,
        terms3_buf,
        terms2_buf,
        above_buf,
        below_buf,
        result_buf,
        sems,
    ) = refs
    channels = bias_ref.shape[1]

    even = lax.rem(here_ref[0], 2) == 0
    first, second = first_ref[...].astype(f32), second_ref[...].astype(f32)
    above_buf[...] = jnp.where(even, second, first)
    below_buf[...] = jnp.where(even, first, second)
    side_start = before_ref.shape[0] - rim * (high1 + high2)
    row_start = 0
    for ref, buf, high, wide in (
        (lat1_ref, lat1_buf, high1, wide1),
        (lat2_ref, lat2_buf, high2, wide2),
        (lat3_ref, lat3_buf, high3, wide3 + 2 * rim),
    ):
        buf[...] = jnp.zeros_like(buf)
        whole = wide
        if buf is lat3_buf:
            buf[rim : rim + high, :wide, :] = ref[...].astype(f32)
        else:
            whole = wide + 2 * rim
            buf[rim : rim + high, rim : rim + wide, :] = ref[...].astype(f32)
            for source, col, keep in (
                (before_ref, 0, here_ref[1] > 0),
                (after_ref, rim + wide, here_ref[1] < col_count - 1),
            ):
                sides = source[side_start : side_start + rim * high, :].astype(f32)
                sides = jnp.where(keep, sides, 0.0)
                for row in range(high):
                    buf[rim + row, col : col + rim, :] = sides[rim * row : rim * row + rim]
            side_start += rim * high
        for source, row in ((above_buf, 0), (below_buf, rim + high)):
            both = source[row_start : row_start + rim * whole, :]
            for step in range(rim):
                buf[row + step, :whole, :] = both[step * whole : (step + 1) * whole]
        row_start += rim * whole

    shape1, shape2, shape3 = lat1_buf.shape[:2], lat2_buf.shape[:2], lat3_buf.shape[:2]

    def put(value, plain, moved):
        plain[0 : value.shape[0], :] = value.astype(bf16)
        later = jnp.concatenate([jnp.zeros((8, channels), f32), value, jnp.zeros((8, channels), f32)])
        moved[0 : later.shape[0], :] = later.astype(bf16)

    for lat_buf, matrix, source, out in (
        (lat3_buf, up3_ref, top_ref, (pyr3_buf, moved3_buf)),
        (lat2_buf, up2_ref, pyr3_buf, (pyr2_buf, moved2_buf)),
        (lat1_buf, up1_ref, pyr2_buf, (pyr1_buf, moved1_buf)),
    ):
        source = source[...]
        total = lat_buf[...].reshape(-1, channels) + dot(matrix[...], source)
        put(total, *out)

    def conv(source, shape, weight_at, rows):
        pitch = shape[1]
        span = rows * pitch
        plain, moved = source
        shift = pitch % 16
        stacked = jnp.concatenate(
            [
                plain[0:span, :],
                (moved if shift else plain)[pitch + shift : pitch + shift + span, :],
                plain[2 * pitch : 2 * pitch + span, :],
            ],
            axis=1,
        )
        for col_tap in range(3):
            weight = weight_at(col_tap)
            total = dot(stacked, weight.reshape(-1, channels))
            acc_buf[col_tap, :rows, :pitch, :] = total.reshape(rows, pitch, channels)

    def taps_total(rows, whole):
        total = acc_buf[0, :rows, 0:whole, :]
        for col_tap in (1, 2):
            total = total + acc_buf[col_tap, :rows, col_tap : whole + col_tap, :]
        return total

    def smooth(number, source, shape, wide):
        rows = shape[0] - 2
        conv(source, shape, lambda j: smooth_w[number, :, j], rows)
        total = taps_total(rows, wide + 2)
        return jnp.maximum(total + bias_ref[8 + number : 9 + number, :][None], 0.0)

    value = smooth(2, (pyr3_buf, moved3_buf), shape3, wide3)
    tall, broad = compact_shape((high3, wide3), 1)
    small3_buf[...] = jnp.zeros_like(small3_buf)
    for row in range(tall):
        small3_buf[row * broad : (row + 1) * broad, :] = value[row]
    lanes3 = small3_buf.shape[0]

    def store3(tap, value):
        terms3_buf[tap * lanes3 : (tap + 1) * lanes3, :] = value

    tap_terms(small3_buf[...].astype(bf16), join_w, 2 * channels, store3)

    rows2, whole2 = compact_shape((high2, wide2), 1)
    sums_buf[:rows2, :whole2, :] = smooth(1, (pyr2_buf, moved2_buf), shape2, wide2)
    half = (high2 // cuts2, wide2 // cuts2)
    tall, broad = compact_shape(half, 1)
    lanes2 = small2_buf.shape[0] // part_count
    small2_buf[...] = jnp.zeros_like(small2_buf)
    for part in range(part_count):
        row0, col0 = part // cuts2 * half[0], part % cuts2 * half[1]
        for row in range(tall):
            start = part * lanes2 + row * broad
            small2_buf[start : start + broad, :] = sums_buf[row0 + row, col0 : col0 + broad, :]

    def store2(tap, value):
        for part in range(part_count):
            start = (part * 9 + tap) * lanes2
            terms2_buf[start : start + lanes2, :] = value[part * lanes2 : (part + 1) * lanes2]

    tap_terms(small2_buf[...].astype(bf16), join_w, channels, store2)

    rows1, pitch1 = window_shape((high1, wide1), 1)
    value = smooth(0, (pyr1_buf, moved1_buf), shape1, wide1)
    down = here_ref[0] * high1 - 1 + lax.broadcasted_iota(jnp.int32, (rows1, 1, 1), 0)
    across = here_ref[1] * wide1 - 1 + lax.broadcasted_iota(jnp.int32, (1, wide1 + 2, 1), 1)
    inside = (down >= 0) & (down < high1 * row_count) & (across >= 0) & (across < wide1 * col_count)
    sums_buf[:rows1, : wide1 + 2, :] = jnp.where(inside, value, 0.0)
    put(sums_buf[...].reshape(rows1 * pitch1, channels), stack_buf, moved1_buf)
    conv((stack_buf, moved1_buf), (rows1, pitch1), lambda j: join_w[:, j, 0:channels], high1)
    total = taps_total(high1, wide1)
    spread = base_ref[...] + dot(spread3_ref[...], terms3_buf[...])
    sums_buf[:high1, :wide1, :] = total + spread.reshape(high1, wide1, channels)
    tall, broad = high1 // cuts2, wide1 // cuts2
    copies = []
    for part, matrix in enumerate(quarters):
        terms = terms2_buf[part * 9 * lanes2 : (part + 1) * 9 * lanes2, :]
        value = dot(matrix[...], terms).reshape(tall, broad, channels)
        row0, col0 = part // cuts2 * tall, part % cuts2 * broad
        value = value + sums_buf[row0 : row0 + tall, col0 : col0 + broad, :]
        value = jnp.maximum(value + bias_ref[11:12, :][None], 0.0)
        result_buf[part] = value.astype(bf16)
        target = out_ref.at[pl.ds(row0, tall), pl.ds(col0, broad), :]
        copies.append(pltpu.make_async_copy(result_buf.at[part], target, sems.at[part]))
        copies[-1].start()
    for copy in copies:
        copy.wait()


def tail(here, top, base, lats, swapped, before, after, biases, weights, matrices, quarters, sizes):
    one, _, _, _, _ = sizes
    channels = biases.shape[1]
    shapes = [window_shape(size, rim) for size in sizes[:3]]
    (rows1, pitch1), (rows2, pitch2), (rows3, pitch3) = shapes
    small3, small2 = matrices[-1].shape[1] // 9, quarters[0].shape[1] // 9 * len(quarters)
    inputs = (*quarters, top, base, *lats, *swapped, before, after, biases, *weights, *matrices)
    return pl.pallas_call(
        functools.partial(tail_kernel, sizes, len(quarters)),
        out_shape=jax.ShapeDtypeStruct((*one, channels), bf16),
        in_specs=[smem_spec] + [vmem_spec] * len(inputs),
        out_specs=hbm_spec,
        scratch_shapes=[
            pltpu.VMEM((rows1, pitch1, channels), f32),
            pltpu.VMEM((rows2, pitch2, channels), f32),
            pltpu.VMEM((rows3, pitch3, channels), f32),
            pltpu.VMEM((rows1 * pitch1, channels), bf16),
            pltpu.VMEM((rows2 * pitch2, channels), bf16),
            pltpu.VMEM((rows3 * pitch3, channels), bf16),
            pltpu.VMEM((rows1 * pitch1 + 16, channels), bf16),
            pltpu.VMEM((rows2 * pitch2 + 16, channels), bf16),
            pltpu.VMEM((rows3 * pitch3 + 16, channels), bf16),
            pltpu.VMEM((3, rows1 - 2, pitch1, channels), f32),
            pltpu.VMEM((rows1 - 2, pitch1, channels), f32),
            pltpu.VMEM(((rows1 - 2) * pitch1, channels), bf16),
            pltpu.VMEM((small3, channels), f32),
            pltpu.VMEM((small2, channels), f32),
            pltpu.VMEM((9 * small3, channels), bf16),
            pltpu.VMEM((9 * small2, channels), bf16),
            pltpu.VMEM(swapped[0].shape, f32),
            pltpu.VMEM(swapped[0].shape, f32),
            pltpu.VMEM((len(quarters), one[0] // cuts2, one[1] // cuts2, channels), bf16),
            pltpu.SemaphoreType.DMA((len(quarters),)),
        ],
        compiler_params=pltpu.CompilerParams(vmem_limit_bytes=30 * 1024 * 1024),
        cost_estimate=pl.CostEstimate(
            flops=8_000_000_000, bytes_accessed=12_000_000, transcendentals=0
        ),
    )(here, *inputs)


def local(
    level_one,
    level_two,
    level_three,
    level_four,
    bin_weight,
    neck_feature,
    neck_pooled,
    lateral_one,
    lateral_two,
    lateral_three,
    smooth_weight,
    join_weight,
    biases,
):
    row_count = lax.axis_size("row")
    col_count = lax.axis_size("col")
    here = jnp.stack([lax.axis_index("row"), lax.axis_index("col")]).astype(jnp.int32)
    high1, wide1 = level_one.shape[:2]
    high2, wide2 = level_two.shape[:2]
    high3, wide3 = level_three.shape[0], level_three.shape[1] // col_count
    high4, grid_cols, part_four = level_four.shape
    wide4 = grid_cols // col_count
    channels = bin_weight.shape[2]
    grid_rows = high4 * row_count
    table = cell_table(grid_rows, grid_cols)
    cells = table.shape[0]
    turned = jnp.asarray(np.ascontiguousarray(table.T))
    table = jnp.asarray(table)

    def shape(dims, kind=bf16):
        return jax.ShapeDtypeStruct(dims, kind)

    others = [shifted(level_four, "row", shift) for shift in range(1, row_count)]
    window_rows = high3 * (wide3 + 2 * rim)
    side_rows = rim * (high1 + high2)
    used = (level_one, lateral_one, level_two, lateral_two, level_three, lateral_three)
    kept = (biases, level_four, table, bin_weight, turned)
    lat1, lat2, *rest = call(
        functools.partial(lateral_kernel, col_count, len(kept)),
        [shape((high1, wide1, channels)), shape((high2, wide2, channels))]
        + [shape((window_rows + side_rows, channels))] * col_count
        + [shape(value.shape, value.dtype) for value in kept],
        [smem_spec] + [hbm_spec] * (len(used) + len(kept)),
        [pltpu.VMEM(value.shape, value.dtype) for value in used]
        + [
            pltpu.VMEM((high3, level_three.shape[1] + 8, channels), f32),
            pltpu.VMEM((high1, wide1, channels), f32),
            pltpu.VMEM((high2, wide2, channels), f32),
            pltpu.VMEM((window_rows + side_rows, channels), f32),
            pltpu.SemaphoreType.DMA((len(used) + len(kept),)),
        ],
        300_000_000,
        4_000_000,
    )(here, *(in_hbm(value) for value in (*used, *kept)))
    pieces = rest[:col_count]
    bias_table, level_four, table, bin_weight, turned = rest[col_count:]
    blocks = [level_four] + others
    near = (1, col_count - 1)
    messages = call(
        functools.partial(bins_kernel, row_count, col_count, window_rows),
        [
            shape((window_rows + cells + (side_rows if shift in near else 0), channels))
            for shift in range(col_count)
        ],
        [smem_spec] + [vmem_spec] * (2 + row_count + col_count),
        [],
        100_000_000,
        1_000_000,
    )(here, table, bin_weight, *blocks, *pieces)

    received = [messages[0]] + [
        shifted(messages[shift], "col", shift) for shift in range(1, col_count)
    ]
    rows = high4 + 2 * rim
    sizes = (
        (high1, wide1),
        (high2, wide2),
        (high3, wide3),
        (high4, wide4),
        (row_count, col_count),
    )
    plans, late_plans = stretches(sizes)
    late = (neck_pooled,)
    taps, neck_pooled, *matrices = call(
        functools.partial(feature_kernel, row_count, plans),
        [shape((3, rows * grid_cols, channels), f32)]
        + [shape(value.shape) for value in late]
        + [shape(matrix_shape(plan)) for plan in plans],
        [smem_spec, hbm_spec] + [vmem_spec] * row_count + [hbm_spec] * len(late),
        [
            pltpu.VMEM(neck_feature.shape, bf16),
            pltpu.VMEM((grid_rows + 2 * rim + 2, grid_cols, part_four), bf16),
            pltpu.SemaphoreType.DMA((1 + len(late),)),
        ],
        700_000_000,
        12_000_000,
    )(here, in_hbm(neck_feature), *blocks, *(in_hbm(value) for value in late))
    span4 = wide4 + 2 * rim
    windows = call(
        functools.partial(neck_kernel, row_count, col_count, high4, window_rows),
        [shape((rows, span4, channels))] * col_count,
        [smem_spec] + [vmem_spec] * (5 + col_count),
        [
            pltpu.VMEM((cells, channels), f32),
            pltpu.VMEM((3, rows * grid_cols + 16, channels), f32),
            pltpu.VMEM((rows, grid_cols + 16, channels), f32),
        ],
        300_000_000,
        3_000_000,
    )(here, table, turned, neck_pooled, bias_table, taps, *received)

    tops = [windows[0]] + [shifted(windows[shift], "col", shift) for shift in range(1, col_count)]
    span3 = wide3 + 2 * rim
    packed = rim * (wide1 + wide2 + wide3 + 6 * rim)
    lat3, first_rows, second_rows = call(
        functools.partial(rows_kernel, col_count, high3, wide3),
        [shape((high3, span3, channels))] + [shape((packed, channels))] * 2,
        [smem_spec] + [vmem_spec] * (3 + col_count),
        [
            pltpu.VMEM((high3, (span3 + 7) // 8 * 8, channels), f32),
            pltpu.VMEM((packed, channels), f32),
            pltpu.VMEM((packed, channels), f32),
        ],
        1_000_000,
        1_000_000,
    )(here, bias_table, lat1, lat2, *received)
    swapped = pair_swap(first_rows, second_rows, "row")
    small = late_plans[0][8]
    top_pitch = window_shape((high4, wide4), rim)[1]
    top, base, *quarters = call(
        functools.partial(late_kernel, sizes, late_plans, col_count),
        [
            shape((rows * top_pitch, channels)),
            shape((high1 * wide1, channels), f32),
        ]
        + [shape(matrix_shape(plan)) for plan in late_plans[1:]],
        [smem_spec] + [vmem_spec] * (2 + col_count),
        [
            pltpu.VMEM((rows, top_pitch, channels), f32),
            pltpu.VMEM((small, channels), f32),
            pltpu.VMEM((9 * small, channels), bf16),
            pltpu.VMEM(matrix_shape(late_plans[0]), bf16),
        ],
        700_000_000,
        5_000_000,
    )(here, bias_table, join_weight, *tops)
    return tail(
        here,
        top,
        base,
        (lat1, lat2, lat3),
        swapped,
        received[1],
        received[-1],
        bias_table,
        (smooth_weight, join_weight),
        matrices,
        quarters,
        sizes,
    )


def solution(mesh):
    placed = (
        P(("grp", "row"), "col", None),
        P(("grp", "row"), "col", None),
        P(("grp", "row"), None, "col"),
        P(("grp", "row"), None, "col"),
        P(None, "col", None),
        P(None, None, "col", None),
        P(None, None, "col", None),
        P(),
        P(),
        P(),
        P(),
        P(),
        P(),
    )
    return jax.shard_map(
        local, mesh=mesh, in_specs=placed, out_specs=P(("grp", "row"), "col", None), check_vma=False
    )
```

```python
import functools

import jax
import jax.numpy as jnp
import numpy as np
from jax import lax
from jax.experimental import pallas as pl
from jax.experimental.pallas import tpu as pltpu
from jax.sharding import PartitionSpec as P

highest = lax.Precision.HIGHEST
bin_sides = (1, 2, 3, 6)
rim = 2
cuts2 = 2
f32 = jnp.float32
bf16 = jnp.bfloat16
vmem_spec = pl.BlockSpec(memory_space=pltpu.VMEM)
hbm_spec = pl.BlockSpec(memory_space=pltpu.HBM)
smem_spec = pl.BlockSpec(memory_space=pltpu.SMEM)
params = pltpu.CompilerParams(vmem_limit_bytes=30 * 1024 * 1024)


def shifted(value, axis, shift):
    count = lax.axis_size(axis)
    return lax.ppermute(value, axis, [(i, (i + shift) % count) for i in range(count)])


def pair_swap(first, second, axis):
    count = lax.axis_size(axis)

    def pairs(start):
        return [
            edge
            for i in range(start, count - 1, 2)
            for edge in ((i, i + 1), (i + 1, i))
        ]

    return lax.ppermute(first, axis, pairs(0)), lax.ppermute(second, axis, pairs(1))


cell_rows = max(bin_sides) ** 2 + 4
cell_starts = tuple(sum((side * side + 7) // 8 * 8 for side in bin_sides[:k]) for k in range(len(bin_sides)))


def cell_table(extent_rows, extent_cols):
    table = np.zeros((cell_starts[-1] + cell_rows, 8), np.float32)
    table[:, 0] = -1.0
    table[:, 5] = 1.0
    for number, side in enumerate(bin_sides):
        for i in range(side):
            for j in range(side):
                top, low = i * extent_rows // side, -(-(i + 1) * extent_rows // side)
                left, right = j * extent_cols // side, -(-(j + 1) * extent_cols // side)
                size = (low - top) * (right - left)
                table[cell_starts[number] + i * side + j, :6] = (number, top, low, left, right, size)
    return table


def pick(number, values):
    result = values[0]
    for step, value in enumerate(values[1:], 1):
        result = jnp.where(number == step, value, result)
    return result


def dot(a, b):
    rows = a.shape[0]
    half = (rows // 2 + 15) // 16 * 16
    if half >= rows:
        return jnp.dot(a, b, preferred_element_type=f32)
    return jnp.concatenate(
        [
            jnp.dot(a[:half], b, preferred_element_type=f32),
            jnp.dot(a[half:], b, preferred_element_type=f32),
        ],
        axis=0,
    )


def in_hbm(value):
    return pltpu.with_memory_space_constraint(value, pltpu.HBM)


def call(kernel, outs, specs, scratch, flops, moved):
    return pl.pallas_call(
        kernel,
        out_shape=outs,
        in_specs=specs,
        out_specs=jax.tree.map(lambda _: vmem_spec, outs),
        scratch_shapes=scratch,
        compiler_params=params,
        cost_estimate=pl.CostEstimate(flops=flops, bytes_accessed=moved, transcendentals=0),
    )


def wrap(value, count):
    return lax.rem(value + count, count)


def floor_div(value, step):
    return jnp.floor((value + 0.5) / step)


def stretch_matrix(out_ref, here, out_shape, out_border, in_shape, in_border, factor, out_size, in_size, counts, lanes, taps=1):
    out_rows, out_pitch = out_shape
    lane = lax.broadcasted_iota(jnp.int32, (1, lanes * taps * taps), 1).astype(f32)
    tap = floor_div(lane, lanes)
    place = lane - tap * lanes
    row_tap = floor_div(tap, taps)
    col_tap = tap - row_tap * taps
    place_row = floor_div(place, in_shape[1])
    place_col = place - place_row * in_shape[1]

    def weights(axis, length, targets, tap_here):
        whole = float(in_size[axis] * counts[axis])
        first_out = (here[axis] * out_size[axis] - out_border[axis]).astype(f32) - (taps // 2)
        first_in = (here[axis] * in_size[axis] - in_border[axis]).astype(f32)
        output = first_out + tap_here + lax.broadcasted_iota(jnp.int32, (length, 1), 0).astype(f32)
        source = (output + 0.5) * (1.0 / factor) - 0.5
        source = jnp.minimum(jnp.maximum(source, 0.0), whole - 1.0)
        inside = jnp.where((output >= 0.0) & (output < whole * factor), 1.0, 0.0)
        return jnp.maximum(0.0, 1.0 - jnp.abs(source - (first_in + targets))) * inside

    down = weights(0, out_rows, place_row, row_tap)
    across = weights(1, out_pitch, place_col, col_tap)
    for row in range(0, out_rows, 2):
        pair = [down[step : step + 1, :] * across for step in range(row, min(row + 2, out_rows))]
        start = row * out_pitch
        value = jnp.concatenate(pair, axis=0)
        out_ref[start : start + value.shape[0], :] = value.astype(bf16)


def pitch_of(width):
    return (width + 15) // 16 * 16


def window_shape(size, border):
    return size[0] + 2 * border, (size[1] + 2 * border + 7) // 8 * 8


def compact_shape(size, border):
    return size[0] + 2 * border, size[1] + 2 * border


def stretches(sizes):
    one, two, three, four, counts = sizes

    def pyramid(out, source):
        shape = window_shape(source, rim)
        borders = (rim, rim)
        factor = out[0] // source[0]
        return (
            window_shape(out, rim), borders, shape, borders, factor, out, source, counts, shape[0] * shape[1]
        )

    def join(source, cuts, part):
        tile = (one[0] // cuts, one[1] // cuts)
        small = (source[0] // cuts, source[1] // cuts)
        shape = compact_shape(small, 1)
        out_border = (-part[0] * tile[0], -part[1] * tile[1])
        in_border = (1 - part[0] * small[0], 1 - part[1] * small[1])
        factor = one[0] // source[0]
        lanes = pitch_of(shape[0] * shape[1])
        return tile, out_border, shape, in_border, factor, one, source, counts, lanes, 3

    parts = [(i, j) for i in range(cuts2) for j in range(cuts2)]
    return (
        (pyramid(three, four), pyramid(two, three), pyramid(one, two), join(three, 1, (0, 0))),
        (join(four, 1, (0, 0)), *(join(two, cuts2, part) for part in parts)),
    )


def matrix_shape(plan):
    return plan[0][0] * plan[0][1], plan[8] * (plan[9] if len(plan) > 9 else 1) ** 2


def lateral_kernel(col_count, kept_count, here_ref, *refs):
    sources, refs = refs[: 6 + kept_count], refs[6 + kept_count :]
    (lat1_ref, lat2_ref), refs = refs[:2], refs[2:]
    pieces, refs = refs[:col_count], refs[col_count:]
    kept, refs = refs[:kept_count], refs[kept_count:]
    fetched, (wide_buf, one_buf, two_buf, piece_buf, sems) = refs[:6], refs[6:]
    copies = [
        pltpu.make_async_copy(source, target, sems.at[number])
        for number, (source, target) in enumerate(zip(sources, (*fetched, *kept)))
    ]
    for copy in copies:
        copy.start()
    one_ref, w1_ref, two_ref, w2_ref, three_ref, w3_ref = fetched
    bias_ref = kept[0]
    copies[6].wait()
    channels = w1_ref.shape[1]
    for number, (source, weight, row, buf, out) in enumerate(
        (
            (one_ref, w1_ref, 5, one_buf, lat1_ref),
            (two_ref, w2_ref, 6, two_buf, lat2_ref),
        )
    ):
        copies[2 * number].wait()
        copies[2 * number + 1].wait()
        high, wide, depth = source.shape
        value = dot(source[...].reshape(high * wide, depth), weight[...])
        value = jnp.maximum(value + bias_ref[row : row + 1, :], 0.0).reshape(high, wide, channels)
        buf[...] = value
        out[...] = value.astype(bf16)
    high3, whole3, share = three_ref.shape
    wide3 = whole3 // col_count
    col_here = here_ref[1]
    copies[4].wait()
    copies[5].wait()
    weight = w3_ref[pl.ds(pl.multiple_of(col_here * share, 16), share), :]
    value = dot(three_ref[...].reshape(high3 * whole3, share), weight)
    wide_buf[...] = jnp.zeros_like(wide_buf)
    wide_buf[:, rim : rim + whole3, :] = value.reshape(high3, whole3, channels)
    span = wide3 + 2 * rim
    for shift, piece in enumerate(pieces):
        target = wrap(col_here + shift, col_count)
        for row in range(high3):
            piece_buf[row * span : (row + 1) * span, :] = wide_buf[
                row, pl.ds(pl.multiple_of(target * wide3, 8), span), :
            ]
        start = high3 * span
        for buf in (one_buf, two_buf):
            high, wide = buf.shape[:2]
            first = wide - rim if shift == 1 else 0
            for row in range(high):
                piece_buf[start : start + rim, :] = buf[row, first : first + rim, :]
                start += rim
        piece[...] = piece_buf[...].astype(bf16)
    for copy in copies[7:]:
        copy.wait()


def bins_kernel(row_count, col_count, share, here_ref, table_ref, weight_ref, *refs):
    blocks, pieces, messages, (bins_buf,) = (
        refs[:row_count],
        refs[row_count : row_count + col_count],
        refs[row_count + col_count : row_count + 2 * col_count],
        refs[row_count + 2 * col_count :],
    )
    table = table_ref[...]
    high, wide, depth = blocks[0].shape
    place = lax.broadcasted_iota(jnp.int32, (1, high * wide), 1).astype(f32)
    place_row = floor_div(place, wide)
    place_col = place - place_row * wide
    in_cols = (place_col >= table[:, 3:4]) & (place_col < table[:, 4:5])
    pooled = None
    for shift, block in enumerate(blocks):
        row = place_row + (wrap(here_ref[0] - shift, row_count) * high).astype(f32)
        inside = in_cols & (row >= table[:, 1:2]) & (row < table[:, 2:3])
        inside = jnp.where(inside, 1.0, 0.0).astype(bf16)
        term = dot(inside, block[...].reshape(high * wide, depth))
        pooled = term if pooled is None else pooled + term
    pooled = (pooled / table[:, 5:6]).astype(bf16)
    bins = None
    for number in range(len(bin_sides)):
        term = jnp.where(table[:, 0:1] == number, dot(pooled, weight_ref[number]), 0.0)
        bins = term if bins is None else bins + term
    bins_buf[...] = bins
    channels = bins.shape[1]
    for shift, (piece, message) in enumerate(zip(pieces, messages)):
        kept = message.shape[0] - cell_rows
        message[0:kept, :] = piece[0:kept, :]
        target = wrap(here_ref[1] + shift, col_count)
        start = pl.multiple_of(pick(target * share // channels, cell_starts), 8)
        message[kept:, :] = bins_buf[pl.ds(start, cell_rows), :].astype(bf16)


def spread_weights(here, high, wide, rows, row_count, share, channels):
    side = pick(here[1] * share // channels, bin_sides).astype(f32)
    lane = lax.broadcasted_iota(jnp.int32, (1, cell_rows), 1).astype(f32)
    cell_row = floor_div(lane, side)
    cell_col = lane - cell_row * side
    place = lax.broadcasted_iota(jnp.int32, (rows * wide, 1), 0).astype(f32)
    place_row = floor_div(place, wide)
    place_col = place - place_row * wide
    place_row = place_row + (here[0] * high - rim - 1).astype(f32)
    grid_rows = float(high * row_count)

    def weights(position, extent, index):
        source = (position + 0.5) * side / extent - 0.5
        source = jnp.minimum(jnp.maximum(source, 0.0), side - 1.0)
        return jnp.maximum(0.0, 1.0 - jnp.abs(source - index))

    spread = weights(place_row, grid_rows, cell_row) * weights(place_col, float(wide), cell_col)
    return jnp.where((place_row >= 0.0) & (place_row < grid_rows), spread, 0.0)


def feature_kernel(row_count, share, channels, plans, here_ref, weight_hbm, *refs):
    blocks, refs = refs[:row_count], refs[row_count:]
    late, refs = refs[:1], refs[1:]
    (out_ref, spread_ref), kept, matrices = refs[:2], refs[2:3], refs[3 : 3 + len(plans)]
    weight_ref, grid_buf, sems = refs[3 + len(plans) :]
    copies = [
        pltpu.make_async_copy(source, target, sems.at[number])
        for number, (source, target) in enumerate(zip((weight_hbm, *late), (weight_ref, *kept)))
    ]
    for copy in copies:
        copy.start()
    here = (here_ref[0], here_ref[1])
    for plan, matrix in zip(plans, matrices):
        stretch_matrix(matrix, here, *plan)
    high, wide, depth = blocks[0].shape
    rows = out_ref.shape[1] // wide
    spread_ref[...] = spread_weights(here, high, wide, rows + 2, row_count, share, channels)
    grid_buf[...] = jnp.zeros_like(grid_buf)
    for shift, block in enumerate(blocks):
        row = wrap(here_ref[0] - shift, row_count) * high + rim + 1
        grid_buf[pl.ds(row, high)] = block[...]
    window = grid_buf[pl.ds(here_ref[0] * high, rows + 2)].reshape((rows + 2) * wide, depth)
    copies[0].wait()
    for col_tap in range(3):
        total = dot(window[0 : rows * wide], weight_ref[0, col_tap])
        for row_tap in (1, 2):
            total = total + dot(
                window[row_tap * wide : (row_tap + rows) * wide], weight_ref[row_tap, col_tap]
            )
        out_ref[col_tap] = total
    for copy in copies[1:]:
        copy.wait()


def neck_kernel(col_count, here_ref, weight_ref, bias_ref, taps_ref, spread_ref, *refs):
    messages, refs = refs[:col_count], refs[col_count:]
    windows, (bins_buf, acc_buf, term_buf) = refs[:col_count], refs[col_count:]
    rows, span, channels = windows[0].shape
    wide = taps_ref.shape[1] // rows
    width4 = span - 2 * rim
    bins = messages[0][messages[0].shape[0] - cell_rows :, :].astype(f32)
    for message in messages[1:]:
        bins = bins + message[message.shape[0] - cell_rows :, :].astype(f32)
    share = weight_ref.shape[2]
    first = here_ref[1] * share
    branch = first // channels
    side = pick(branch, bin_sides)
    used = lax.broadcasted_iota(jnp.int32, (cell_rows, 1), 0) < side * side
    bins = jnp.where(used, jnp.maximum(bins + bias_ref[pl.ds(branch, 1), :], 0.0), 0.0)
    if share != channels:
        bins_buf[...] = bins
        bins = bins_buf[:, pl.ds(pl.multiple_of(lax.rem(first, channels), 128), share)]
    ppm = jnp.dot(spread_ref[...], bins, precision=highest, preferred_element_type=f32).astype(bf16)
    size = rows * wide
    stacked = jnp.concatenate([ppm[tap * wide : tap * wide + size] for tap in range(3)], axis=1)
    for col_tap in range(3):
        total = dot(stacked, weight_ref[:, col_tap].reshape(3 * share, channels))
        acc_buf[col_tap, 8 : 8 + size, :] = total + taps_ref[col_tap]
    place = lax.broadcasted_iota(jnp.int32, (size, 1), 0).astype(f32)
    col = place - floor_div(place, wide) * wide
    total = (
        acc_buf[1, 8 : 8 + size, :]
        + jnp.where(col > 0.0, acc_buf[0, 7 : 7 + size, :], 0.0)
        + jnp.where(col < wide - 1.0, acc_buf[2, 9 : 9 + size, :], 0.0)
    )
    term_buf[...] = jnp.zeros_like(term_buf)
    term_buf[:, rim : rim + wide, :] = total.reshape(rows, wide, channels)
    for shift, window in enumerate(windows):
        target = wrap(here_ref[1] + shift, col_count)
        window[...] = term_buf[:, pl.ds(pl.multiple_of(target * width4, 8), span), :].astype(bf16)


def rows_kernel(col_count, high3, wide3, here_ref, bias_ref, lat1_ref, lat2_ref, *refs):
    messages, (lat3_ref, first_ref, second_ref, three_buf, low_buf, high_buf) = (
        refs[:col_count],
        refs[col_count:],
    )
    span = wide3 + 2 * rim
    total = messages[0][0 : high3 * span, :].astype(f32)
    for message in messages[1:]:
        total = total + message[0 : high3 * span, :].astype(f32)
    total = jnp.maximum(total + bias_ref[7:8, :], 0.0)
    col_here = here_ref[1]
    place = lax.broadcasted_iota(jnp.int32, (span, 1), 0) + col_here * wide3 - rim
    inside = (place >= 0) & (place < wide3 * col_count)
    for row in range(high3):
        three_buf[row, :span, :] = jnp.where(inside, total[row * span : (row + 1) * span], 0.0)
    lat3_ref[...] = three_buf[:, :span, :].astype(bf16)
    high1, wide1 = lat1_ref.shape[:2]
    high2, wide2 = lat2_ref.shape[:2]
    before, after = messages[1], messages[col_count - 1]
    sides_at = high3 * span
    for pack_buf, last in ((low_buf, False), (high_buf, True)):
        start, at = 0, sides_at
        for lat, high, wide in ((lat1_ref, high1, wide1), (lat2_ref, high2, wide2)):
            whole = wide + 2 * rim
            first = high - rim if last else 0
            left = before[at + rim * first : at + rim * (first + rim), :].astype(f32)
            right = after[at + rim * first : at + rim * (first + rim), :].astype(f32)
            left = jnp.where(col_here > 0, left, 0.0)
            right = jnp.where(col_here < col_count - 1, right, 0.0)
            for step in range(rim):
                pack_buf[start : start + rim, :] = left[rim * step : rim * (step + 1)]
                pack_buf[start + rim : start + rim + wide, :] = lat[first + step].astype(f32)
                pack_buf[start + rim + wide : start + whole, :] = right[rim * step : rim * (step + 1)]
                start += whole
            at += rim * high
        for step in range(rim):
            row = high3 - rim + step if last else step
            pack_buf[start : start + span, :] = three_buf[row, :span, :]
            start += span
    even = lax.rem(here_ref[0], 2) == 0
    low, high = low_buf[...], high_buf[...]
    first_ref[...] = jnp.where(even, high, low).astype(bf16)
    second_ref[...] = jnp.where(even, low, high).astype(bf16)


def tap_terms(small, weight_ref, first, store):
    channels = weight_ref.shape[3]
    for tap in range(9):
        weight = weight_ref[tap // 3, tap % 3, first : first + channels, :]
        store(tap, dot(small, weight).astype(bf16))


def late_kernel(sizes, plans, top_count, here_ref, bias_ref, join_ref, *refs):
    tops, refs = refs[:top_count], refs[top_count:]
    top_ref, base_ref, matrices, refs = refs[0], refs[1], refs[2 : 1 + len(plans)], refs[1 + len(plans) :]
    top_buf, small_buf, terms_buf, matrix_buf = refs
    high4, wide4 = sizes[3]
    here = (here_ref[0], here_ref[1])
    total = tops[0][...].astype(f32)
    for ref in tops[1:]:
        total = total + ref[...].astype(f32)
    top_buf[...] = jnp.zeros_like(top_buf)
    top_buf[:, : wide4 + 2 * rim, :] = jnp.maximum(total + bias_ref[4:5, :][None], 0.0)
    top_ref[...] = top_buf[...].reshape(top_ref.shape).astype(bf16)
    tall, broad = compact_shape((high4, wide4), 1)
    small_buf[...] = jnp.zeros_like(small_buf)
    for row in range(tall):
        small_buf[row * broad : (row + 1) * broad, :] = top_buf[
            row + rim - 1, rim - 1 : rim - 1 + broad, :
        ]
    lanes, channels = small_buf.shape

    def store(tap, value):
        terms_buf[tap * lanes : (tap + 1) * lanes, :] = value

    tap_terms(small_buf[...].astype(bf16), join_ref, 3 * channels, store)
    for plan, matrix in zip(plans, (matrix_buf, *matrices)):
        stretch_matrix(matrix, here, *plan)
    base_ref[...] = dot(matrix_buf[...], terms_buf[...])


def tail_kernel(sizes, part_count, here_ref, *refs):
    (high1, wide1), (high2, wide2), (high3, wide3), _, (row_count, col_count) = sizes
    quarters, refs = refs[:part_count], refs[part_count:]
    (
        top_ref,
        base_ref,
        lat1_ref,
        lat2_ref,
        lat3_ref,
        first_ref,
        second_ref,
        before_ref,
        after_ref,
        bias_ref,
        smooth_w,
        join_w,
        up3_ref,
        up2_ref,
        up1_ref,
        spread3_ref,
        out_ref,
        lat1_buf,
        lat2_buf,
        lat3_buf,
        pyr1_buf,
        pyr2_buf,
        pyr3_buf,
        moved1_buf,
        moved2_buf,
        moved3_buf,
        acc_buf,
        sums_buf,
        stack_buf,
        small3_buf,
        small2_buf,
        terms3_buf,
        terms2_buf,
        above_buf,
        below_buf,
        result_buf,
        sems,
    ) = refs
    channels = bias_ref.shape[1]

    even = lax.rem(here_ref[0], 2) == 0
    first, second = first_ref[...].astype(f32), second_ref[...].astype(f32)
    above_buf[...] = jnp.where(even, second, first)
    below_buf[...] = jnp.where(even, first, second)
    side_start = high3 * (wide3 + 2 * rim)
    row_start = 0
    for ref, buf, high, wide in (
        (lat1_ref, lat1_buf, high1, wide1),
        (lat2_ref, lat2_buf, high2, wide2),
        (lat3_ref, lat3_buf, high3, wide3 + 2 * rim),
    ):
        buf[...] = jnp.zeros_like(buf)
        whole = wide
        if buf is lat3_buf:
            buf[rim : rim + high, :wide, :] = ref[...].astype(f32)
        else:
            whole = wide + 2 * rim
            buf[rim : rim + high, rim : rim + wide, :] = ref[...].astype(f32)
            for source, col, keep in (
                (before_ref, 0, here_ref[1] > 0),
                (after_ref, rim + wide, here_ref[1] < col_count - 1),
            ):
                sides = source[side_start : side_start + rim * high, :].astype(f32)
                sides = jnp.where(keep, sides, 0.0)
                for row in range(high):
                    buf[rim + row, col : col + rim, :] = sides[rim * row : rim * row + rim]
            side_start += rim * high
        for source, row in ((above_buf, 0), (below_buf, rim + high)):
            both = source[row_start : row_start + rim * whole, :]
            for step in range(rim):
                buf[row + step, :whole, :] = both[step * whole : (step + 1) * whole]
        row_start += rim * whole

    shape1, shape2, shape3 = lat1_buf.shape[:2], lat2_buf.shape[:2], lat3_buf.shape[:2]

    def put(value, plain, moved):
        plain[0 : value.shape[0], :] = value.astype(bf16)
        later = jnp.concatenate([jnp.zeros((8, channels), f32), value, jnp.zeros((8, channels), f32)])
        moved[0 : later.shape[0], :] = later.astype(bf16)

    for lat_buf, matrix, source, out in (
        (lat3_buf, up3_ref, top_ref, (pyr3_buf, moved3_buf)),
        (lat2_buf, up2_ref, pyr3_buf, (pyr2_buf, moved2_buf)),
        (lat1_buf, up1_ref, pyr2_buf, (pyr1_buf, moved1_buf)),
    ):
        source = source[...]
        total = lat_buf[...].reshape(-1, channels) + dot(matrix[...], source)
        put(total, *out)

    def conv(source, shape, weight_at, rows):
        pitch = shape[1]
        span = rows * pitch
        plain, moved = source
        shift = pitch % 16
        stacked = jnp.concatenate(
            [
                plain[0:span, :],
                (moved if shift else plain)[pitch + shift : pitch + shift + span, :],
                plain[2 * pitch : 2 * pitch + span, :],
            ],
            axis=1,
        )
        for col_tap in range(3):
            weight = weight_at(col_tap)
            total = dot(stacked, weight.reshape(-1, channels))
            acc_buf[col_tap, :rows, :pitch, :] = total.reshape(rows, pitch, channels)

    def taps_total(rows, whole):
        total = acc_buf[0, :rows, 0:whole, :]
        for col_tap in (1, 2):
            total = total + acc_buf[col_tap, :rows, col_tap : whole + col_tap, :]
        return total

    def smooth(number, source, shape, wide):
        rows = shape[0] - 2
        conv(source, shape, lambda j: smooth_w[number, :, j], rows)
        total = taps_total(rows, wide + 2)
        return jnp.maximum(total + bias_ref[8 + number : 9 + number, :][None], 0.0)

    value = smooth(2, (pyr3_buf, moved3_buf), shape3, wide3)
    tall, broad = compact_shape((high3, wide3), 1)
    small3_buf[...] = jnp.zeros_like(small3_buf)
    for row in range(tall):
        small3_buf[row * broad : (row + 1) * broad, :] = value[row]
    lanes3 = small3_buf.shape[0]

    def store3(tap, value):
        terms3_buf[tap * lanes3 : (tap + 1) * lanes3, :] = value

    tap_terms(small3_buf[...].astype(bf16), join_w, 2 * channels, store3)

    rows2, whole2 = compact_shape((high2, wide2), 1)
    sums_buf[:rows2, :whole2, :] = smooth(1, (pyr2_buf, moved2_buf), shape2, wide2)
    half = (high2 // cuts2, wide2 // cuts2)
    tall, broad = compact_shape(half, 1)
    lanes2 = small2_buf.shape[0] // part_count
    small2_buf[...] = jnp.zeros_like(small2_buf)
    for part in range(part_count):
        row0, col0 = part // cuts2 * half[0], part % cuts2 * half[1]
        for row in range(tall):
            start = part * lanes2 + row * broad
            small2_buf[start : start + broad, :] = sums_buf[row0 + row, col0 : col0 + broad, :]

    def store2(tap, value):
        for part in range(part_count):
            start = (part * 9 + tap) * lanes2
            terms2_buf[start : start + lanes2, :] = value[part * lanes2 : (part + 1) * lanes2]

    tap_terms(small2_buf[...].astype(bf16), join_w, channels, store2)

    rows1, pitch1 = window_shape((high1, wide1), 1)
    value = smooth(0, (pyr1_buf, moved1_buf), shape1, wide1)
    down = here_ref[0] * high1 - 1 + lax.broadcasted_iota(jnp.int32, (rows1, 1, 1), 0)
    across = here_ref[1] * wide1 - 1 + lax.broadcasted_iota(jnp.int32, (1, wide1 + 2, 1), 1)
    inside = (down >= 0) & (down < high1 * row_count) & (across >= 0) & (across < wide1 * col_count)
    sums_buf[:rows1, : wide1 + 2, :] = jnp.where(inside, value, 0.0)
    put(sums_buf[...].reshape(rows1 * pitch1, channels), stack_buf, moved1_buf)
    conv((stack_buf, moved1_buf), (rows1, pitch1), lambda j: join_w[:, j, 0:channels], high1)
    total = taps_total(high1, wide1)
    spread = base_ref[...] + dot(spread3_ref[...], terms3_buf[...])
    sums_buf[:high1, :wide1, :] = total + spread.reshape(high1, wide1, channels)
    tall, broad = high1 // cuts2, wide1 // cuts2
    copies = []
    for part, matrix in enumerate(quarters):
        terms = terms2_buf[part * 9 * lanes2 : (part + 1) * 9 * lanes2, :]
        value = dot(matrix[...], terms).reshape(tall, broad, channels)
        row0, col0 = part // cuts2 * tall, part % cuts2 * broad
        value = value + sums_buf[row0 : row0 + tall, col0 : col0 + broad, :]
        value = jnp.maximum(value + bias_ref[11:12, :][None], 0.0)
        result_buf[part] = value.astype(bf16)
        target = out_ref.at[pl.ds(row0, tall), pl.ds(col0, broad), :]
        copies.append(pltpu.make_async_copy(result_buf.at[part], target, sems.at[part]))
        copies[-1].start()
    for copy in copies:
        copy.wait()


def tail(here, top, base, lats, swapped, before, after, biases, weights, matrices, quarters, sizes):
    one, _, _, _, _ = sizes
    channels = biases.shape[1]
    shapes = [window_shape(size, rim) for size in sizes[:3]]
    (rows1, pitch1), (rows2, pitch2), (rows3, pitch3) = shapes
    small3, small2 = matrices[-1].shape[1] // 9, quarters[0].shape[1] // 9 * len(quarters)
    inputs = (*quarters, top, base, *lats, *swapped, before, after, biases, *weights, *matrices)
    return pl.pallas_call(
        functools.partial(tail_kernel, sizes, len(quarters)),
        out_shape=jax.ShapeDtypeStruct((*one, channels), bf16),
        in_specs=[smem_spec] + [vmem_spec] * len(inputs),
        out_specs=hbm_spec,
        scratch_shapes=[
            pltpu.VMEM((rows1, pitch1, channels), f32),
            pltpu.VMEM((rows2, pitch2, channels), f32),
            pltpu.VMEM((rows3, pitch3, channels), f32),
            pltpu.VMEM((rows1 * pitch1, channels), bf16),
            pltpu.VMEM((rows2 * pitch2, channels), bf16),
            pltpu.VMEM((rows3 * pitch3, channels), bf16),
            pltpu.VMEM((rows1 * pitch1 + 16, channels), bf16),
            pltpu.VMEM((rows2 * pitch2 + 16, channels), bf16),
            pltpu.VMEM((rows3 * pitch3 + 16, channels), bf16),
            pltpu.VMEM((3, rows1 - 2, pitch1, channels), f32),
            pltpu.VMEM((rows1 - 2, pitch1, channels), f32),
            pltpu.VMEM(((rows1 - 2) * pitch1, channels), bf16),
            pltpu.VMEM((small3, channels), f32),
            pltpu.VMEM((small2, channels), f32),
            pltpu.VMEM((9 * small3, channels), bf16),
            pltpu.VMEM((9 * small2, channels), bf16),
            pltpu.VMEM(swapped[0].shape, f32),
            pltpu.VMEM(swapped[0].shape, f32),
            pltpu.VMEM((len(quarters), one[0] // cuts2, one[1] // cuts2, channels), bf16),
            pltpu.SemaphoreType.DMA((len(quarters),)),
        ],
        compiler_params=pltpu.CompilerParams(vmem_limit_bytes=30 * 1024 * 1024),
        cost_estimate=pl.CostEstimate(
            flops=8_000_000_000, bytes_accessed=12_000_000, transcendentals=0
        ),
    )(here, *inputs)


def local(
    level_one,
    level_two,
    level_three,
    level_four,
    bin_weight,
    neck_feature,
    neck_pooled,
    lateral_one,
    lateral_two,
    lateral_three,
    smooth_weight,
    join_weight,
    biases,
):
    row_count = lax.axis_size("row")
    col_count = lax.axis_size("col")
    here = jnp.stack([lax.axis_index("row"), lax.axis_index("col")]).astype(jnp.int32)
    high1, wide1 = level_one.shape[:2]
    high2, wide2 = level_two.shape[:2]
    high3, wide3 = level_three.shape[0], level_three.shape[1] // col_count
    high4, grid_cols, part_four = level_four.shape
    wide4 = grid_cols // col_count
    channels = bin_weight.shape[2]
    grid_rows = high4 * row_count
    table = cell_table(grid_rows, grid_cols)
    table = jnp.asarray(table)
    share_ppm = neck_pooled.shape[2]

    def shape(dims, kind=bf16):
        return jax.ShapeDtypeStruct(dims, kind)

    others = [shifted(level_four, "row", shift) for shift in range(1, row_count)]
    window_rows = high3 * (wide3 + 2 * rim)
    side_rows = rim * (high1 + high2)
    used = (level_one, lateral_one, level_two, lateral_two, level_three, lateral_three)
    kept = (biases, level_four, table, bin_weight)
    lat1, lat2, *rest = call(
        functools.partial(lateral_kernel, col_count, len(kept)),
        [shape((high1, wide1, channels)), shape((high2, wide2, channels))]
        + [shape((window_rows + side_rows, channels))] * col_count
        + [shape(value.shape, value.dtype) for value in kept],
        [smem_spec] + [hbm_spec] * (len(used) + len(kept)),
        [pltpu.VMEM(value.shape, value.dtype) for value in used]
        + [
            pltpu.VMEM((high3, level_three.shape[1] + 8, channels), f32),
            pltpu.VMEM((high1, wide1, channels), f32),
            pltpu.VMEM((high2, wide2, channels), f32),
            pltpu.VMEM((window_rows + side_rows, channels), f32),
            pltpu.SemaphoreType.DMA((len(used) + len(kept),)),
        ],
        300_000_000,
        4_000_000,
    )(here, *(in_hbm(value) for value in (*used, *kept)))
    pieces = rest[:col_count]
    bias_table, level_four, table, bin_weight = rest[col_count:]
    blocks = [level_four] + others
    near = (1, col_count - 1)
    messages = call(
        functools.partial(bins_kernel, row_count, col_count, share_ppm),
        [
            shape((window_rows + cell_rows + (side_rows if shift in near else 0), channels))
            for shift in range(col_count)
        ],
        [smem_spec] + [vmem_spec] * (2 + row_count + col_count),
        [pltpu.VMEM((table.shape[0], channels), f32)],
        100_000_000,
        1_000_000,
    )(here, table, bin_weight, *blocks, *pieces)

    received = [messages[0]] + [
        shifted(messages[shift], "col", shift) for shift in range(1, col_count)
    ]
    rows = high4 + 2 * rim
    sizes = (
        (high1, wide1),
        (high2, wide2),
        (high3, wide3),
        (high4, wide4),
        (row_count, col_count),
    )
    plans, late_plans = stretches(sizes)
    late = (neck_pooled,)
    taps, spread, neck_pooled, *matrices = call(
        functools.partial(feature_kernel, row_count, share_ppm, channels, plans),
        [
            shape((3, rows * grid_cols, channels), f32),
            shape(((rows + 2) * grid_cols, cell_rows), f32),
        ]
        + [shape(value.shape) for value in late]
        + [shape(matrix_shape(plan)) for plan in plans],
        [smem_spec, hbm_spec] + [vmem_spec] * row_count + [hbm_spec] * len(late),
        [
            pltpu.VMEM(neck_feature.shape, bf16),
            pltpu.VMEM((grid_rows + 2 * rim + 2, grid_cols, part_four), bf16),
            pltpu.SemaphoreType.DMA((1 + len(late),)),
        ],
        700_000_000,
        12_000_000,
    )(here, in_hbm(neck_feature), *blocks, *(in_hbm(value) for value in late))
    span4 = wide4 + 2 * rim
    windows = call(
        functools.partial(neck_kernel, col_count),
        [shape((rows, span4, channels))] * col_count,
        [smem_spec] + [vmem_spec] * (4 + col_count),
        [
            pltpu.VMEM((cell_rows, channels), f32),
            pltpu.VMEM((3, rows * grid_cols + 16, channels), f32),
            pltpu.VMEM((rows, grid_cols + 16, channels), f32),
        ],
        300_000_000,
        3_000_000,
    )(here, neck_pooled, bias_table, taps, spread, *received)

    tops = [windows[0]] + [shifted(windows[shift], "col", shift) for shift in range(1, col_count)]
    span3 = wide3 + 2 * rim
    packed = rim * (wide1 + wide2 + wide3 + 6 * rim)
    lat3, first_rows, second_rows = call(
        functools.partial(rows_kernel, col_count, high3, wide3),
        [shape((high3, span3, channels))] + [shape((packed, channels))] * 2,
        [smem_spec] + [vmem_spec] * (3 + col_count),
        [
            pltpu.VMEM((high3, (span3 + 7) // 8 * 8, channels), f32),
            pltpu.VMEM((packed, channels), f32),
            pltpu.VMEM((packed, channels), f32),
        ],
        1_000_000,
        1_000_000,
    )(here, bias_table, lat1, lat2, *received)
    swapped = pair_swap(first_rows, second_rows, "row")
    small = late_plans[0][8]
    top_pitch = window_shape((high4, wide4), rim)[1]
    top, base, *quarters = call(
        functools.partial(late_kernel, sizes, late_plans, col_count),
        [
            shape((rows * top_pitch, channels)),
            shape((high1 * wide1, channels), f32),
        ]
        + [shape(matrix_shape(plan)) for plan in late_plans[1:]],
        [smem_spec] + [vmem_spec] * (2 + col_count),
        [
            pltpu.VMEM((rows, top_pitch, channels), f32),
            pltpu.VMEM((small, channels), f32),
            pltpu.VMEM((9 * small, channels), bf16),
            pltpu.VMEM(matrix_shape(late_plans[0]), bf16),
        ],
        700_000_000,
        5_000_000,
    )(here, bias_table, join_weight, *tops)
    return tail(
        here,
        top,
        base,
        (lat1, lat2, lat3),
        swapped,
        received[1],
        received[-1],
        bias_table,
        (smooth_weight, join_weight),
        matrices,
        quarters,
        sizes,
    )


def solution(mesh):
    placed = (
        P(("grp", "row"), "col", None),
        P(("grp", "row"), "col", None),
        P(("grp", "row"), None, "col"),
        P(("grp", "row"), None, "col"),
        P(None, "col", None),
        P(None, None, "col", None),
        P(None, None, "col", None),
        P(),
        P(),
        P(),
        P(),
        P(),
        P(),
    )
    return jax.shard_map(
        local, mesh=mesh, in_specs=placed, out_specs=P(("grp", "row"), "col", None), check_vma=False
    )
```

```python
import functools

import jax
import jax.numpy as jnp
import numpy as np
from jax import lax
from jax.experimental import pallas as pl
from jax.experimental.pallas import tpu as pltpu
from jax.sharding import PartitionSpec as P

highest = lax.Precision.HIGHEST
bin_sides = (1, 2, 3, 6)
rim = 2
cuts2 = 2
f32 = jnp.float32
bf16 = jnp.bfloat16
vmem_spec = pl.BlockSpec(memory_space=pltpu.VMEM)
hbm_spec = pl.BlockSpec(memory_space=pltpu.HBM)
params = pltpu.CompilerParams(vmem_limit_bytes=30 * 1024 * 1024)


def shifted(value, axis, shift):
    count = lax.axis_size(axis)
    return lax.ppermute(value, axis, [(i, (i + shift) % count) for i in range(count)])


def place_here():
    return lax.axis_index("row").astype(jnp.int32), lax.axis_index("col").astype(jnp.int32)


def pair_swap(first, second, axis):
    count = lax.axis_size(axis)

    def pairs(start):
        return [
            edge
            for i in range(start, count - 1, 2)
            for edge in ((i, i + 1), (i + 1, i))
        ]

    return lax.ppermute(first, axis, pairs(0)), lax.ppermute(second, axis, pairs(1))


cell_rows = max(bin_sides) ** 2 + 4
cell_starts = tuple(sum((side * side + 7) // 8 * 8 for side in bin_sides[:k]) for k in range(len(bin_sides)))


def cell_table(extent_rows, extent_cols):
    table = np.zeros((cell_starts[-1] + cell_rows, 8), np.float32)
    table[:, 0] = -1.0
    table[:, 5] = 1.0
    for number, side in enumerate(bin_sides):
        for i in range(side):
            for j in range(side):
                top, low = i * extent_rows // side, -(-(i + 1) * extent_rows // side)
                left, right = j * extent_cols // side, -(-(j + 1) * extent_cols // side)
                size = (low - top) * (right - left)
                table[cell_starts[number] + i * side + j, :6] = (number, top, low, left, right, size)
    return table


def pick(number, values):
    result = values[0]
    for step, value in enumerate(values[1:], 1):
        result = jnp.where(number == step, value, result)
    return result


def dot(a, b):
    rows = a.shape[0]
    half = (rows // 2 + 15) // 16 * 16
    if half >= rows:
        return jnp.dot(a, b, preferred_element_type=f32)
    return jnp.concatenate(
        [
            jnp.dot(a[:half], b, preferred_element_type=f32),
            jnp.dot(a[half:], b, preferred_element_type=f32),
        ],
        axis=0,
    )


def in_hbm(value):
    return pltpu.with_memory_space_constraint(value, pltpu.HBM)


def call(kernel, outs, specs, scratch, flops, moved):
    return pl.pallas_call(
        kernel,
        out_shape=outs,
        in_specs=specs,
        out_specs=jax.tree.map(lambda _: vmem_spec, outs),
        scratch_shapes=scratch,
        compiler_params=params,
        cost_estimate=pl.CostEstimate(flops=flops, bytes_accessed=moved, transcendentals=0),
    )


def wrap(value, count):
    return lax.rem(value + count, count)


def floor_div(value, step):
    return jnp.floor((value + 0.5) / step)


def stretch_matrix(out_ref, here, out_shape, out_border, in_shape, in_border, factor, out_size, in_size, counts, lanes, taps=1):
    out_rows, out_pitch = out_shape
    lane = lax.broadcasted_iota(jnp.int32, (1, lanes * taps * taps), 1).astype(f32)
    tap = floor_div(lane, lanes)
    place = lane - tap * lanes
    row_tap = floor_div(tap, taps)
    col_tap = tap - row_tap * taps
    place_row = floor_div(place, in_shape[1])
    place_col = place - place_row * in_shape[1]

    def weights(axis, length, targets, tap_here):
        whole = float(in_size[axis] * counts[axis])
        first_out = (here[axis] * out_size[axis] - out_border[axis]).astype(f32) - (taps // 2)
        first_in = (here[axis] * in_size[axis] - in_border[axis]).astype(f32)
        output = first_out + tap_here + lax.broadcasted_iota(jnp.int32, (length, 1), 0).astype(f32)
        source = (output + 0.5) * (1.0 / factor) - 0.5
        source = jnp.minimum(jnp.maximum(source, 0.0), whole - 1.0)
        inside = jnp.where((output >= 0.0) & (output < whole * factor), 1.0, 0.0)
        return jnp.maximum(0.0, 1.0 - jnp.abs(source - (first_in + targets))) * inside

    down = weights(0, out_rows, place_row, row_tap)
    across = weights(1, out_pitch, place_col, col_tap)
    for row in range(0, out_rows, 2):
        pair = [down[step : step + 1, :] * across for step in range(row, min(row + 2, out_rows))]
        start = row * out_pitch
        value = jnp.concatenate(pair, axis=0)
        out_ref[start : start + value.shape[0], :] = value.astype(bf16)


def pitch_of(width):
    return (width + 15) // 16 * 16


def window_shape(size, border):
    return size[0] + 2 * border, (size[1] + 2 * border + 7) // 8 * 8


def compact_shape(size, border):
    return size[0] + 2 * border, size[1] + 2 * border


def stretches(sizes):
    one, two, three, four, counts = sizes

    def pyramid(out, source):
        shape = window_shape(source, rim)
        borders = (rim, rim)
        factor = out[0] // source[0]
        return (
            window_shape(out, rim), borders, shape, borders, factor, out, source, counts, shape[0] * shape[1]
        )

    def join(source, cuts, part):
        tile = (one[0] // cuts, one[1] // cuts)
        small = (source[0] // cuts, source[1] // cuts)
        shape = compact_shape(small, 1)
        out_border = (-part[0] * tile[0], -part[1] * tile[1])
        in_border = (1 - part[0] * small[0], 1 - part[1] * small[1])
        factor = one[0] // source[0]
        lanes = pitch_of(shape[0] * shape[1])
        return tile, out_border, shape, in_border, factor, one, source, counts, lanes, 3

    parts = [(i, j) for i in range(cuts2) for j in range(cuts2)]
    return (
        (pyramid(three, four), pyramid(two, three), pyramid(one, two), join(three, 1, (0, 0))),
        (join(four, 1, (0, 0)), *(join(two, cuts2, part) for part in parts)),
    )


def matrix_shape(plan):
    return plan[0][0] * plan[0][1], plan[8] * (plan[9] if len(plan) > 9 else 1) ** 2


def lateral_kernel(col_count, kept_count, *refs):
    here_ref = place_here()
    sources, refs = refs[: 6 + kept_count], refs[6 + kept_count :]
    (lat1_ref, lat2_ref), refs = refs[:2], refs[2:]
    pieces, refs = refs[:col_count], refs[col_count:]
    kept, refs = refs[:kept_count], refs[kept_count:]
    fetched, (wide_buf, one_buf, two_buf, piece_buf, sems) = refs[:6], refs[6:]
    copies = [
        pltpu.make_async_copy(source, target, sems.at[number])
        for number, (source, target) in enumerate(zip(sources, (*fetched, *kept)))
    ]
    for copy in copies:
        copy.start()
    one_ref, w1_ref, two_ref, w2_ref, three_ref, w3_ref = fetched
    bias_ref = kept[0]
    copies[6].wait()
    channels = w1_ref.shape[1]
    for number, (source, weight, row, buf, out) in enumerate(
        (
            (one_ref, w1_ref, 5, one_buf, lat1_ref),
            (two_ref, w2_ref, 6, two_buf, lat2_ref),
        )
    ):
        copies[2 * number].wait()
        copies[2 * number + 1].wait()
        high, wide, depth = source.shape
        value = dot(source[...].reshape(high * wide, depth), weight[...])
        value = jnp.maximum(value + bias_ref[row : row + 1, :], 0.0).reshape(high, wide, channels)
        buf[...] = value
        out[...] = value.astype(bf16)
    high3, whole3, share = three_ref.shape
    wide3 = whole3 // col_count
    col_here = here_ref[1]
    copies[4].wait()
    copies[5].wait()
    weight = w3_ref[pl.ds(pl.multiple_of(col_here * share, 16), share), :]
    value = dot(three_ref[...].reshape(high3 * whole3, share), weight)
    wide_buf[...] = jnp.zeros_like(wide_buf)
    wide_buf[:, rim : rim + whole3, :] = value.reshape(high3, whole3, channels)
    span = wide3 + 2 * rim
    for shift, piece in enumerate(pieces):
        target = wrap(col_here + shift, col_count)
        for row in range(high3):
            piece_buf[row * span : (row + 1) * span, :] = wide_buf[
                row, pl.ds(pl.multiple_of(target * wide3, 8), span), :
            ]
        start = high3 * span
        for buf in (one_buf, two_buf):
            high, wide = buf.shape[:2]
            first = wide - rim if shift == 1 else 0
            for row in range(high):
                piece_buf[start : start + rim, :] = buf[row, first : first + rim, :]
                start += rim
        piece[...] = piece_buf[...].astype(bf16)
    for copy in copies[7:]:
        copy.wait()


def bins_kernel(row_count, col_count, share, table_ref, weight_ref, *refs):
    here_ref = place_here()
    blocks, pieces, messages, (bins_buf,) = (
        refs[:row_count],
        refs[row_count : row_count + col_count],
        refs[row_count + col_count : row_count + 2 * col_count],
        refs[row_count + 2 * col_count :],
    )
    table = table_ref[...]
    high, wide, depth = blocks[0].shape
    place = lax.broadcasted_iota(jnp.int32, (1, high * wide), 1).astype(f32)
    place_row = floor_div(place, wide)
    place_col = place - place_row * wide
    in_cols = (place_col >= table[:, 3:4]) & (place_col < table[:, 4:5])
    pooled = None
    for shift, block in enumerate(blocks):
        row = place_row + (wrap(here_ref[0] - shift, row_count) * high).astype(f32)
        inside = in_cols & (row >= table[:, 1:2]) & (row < table[:, 2:3])
        inside = jnp.where(inside, 1.0, 0.0).astype(bf16)
        term = dot(inside, block[...].reshape(high * wide, depth))
        pooled = term if pooled is None else pooled + term
    pooled = (pooled / table[:, 5:6]).astype(bf16)
    bins = None
    for number in range(len(bin_sides)):
        term = jnp.where(table[:, 0:1] == number, dot(pooled, weight_ref[number]), 0.0)
        bins = term if bins is None else bins + term
    bins_buf[...] = bins
    channels = bins.shape[1]
    for shift, (piece, message) in enumerate(zip(pieces, messages)):
        kept = message.shape[0] - cell_rows
        message[0:kept, :] = piece[0:kept, :]
        target = wrap(here_ref[1] + shift, col_count)
        start = pl.multiple_of(pick(target * share // channels, cell_starts), 8)
        message[kept:, :] = bins_buf[pl.ds(start, cell_rows), :].astype(bf16)


def spread_weights(here, high, wide, rows, row_count, share, channels):
    side = pick(here[1] * share // channels, bin_sides).astype(f32)
    lane = lax.broadcasted_iota(jnp.int32, (1, cell_rows), 1).astype(f32)
    cell_row = floor_div(lane, side)
    cell_col = lane - cell_row * side
    place = lax.broadcasted_iota(jnp.int32, (rows * wide, 1), 0).astype(f32)
    place_row = floor_div(place, wide)
    place_col = place - place_row * wide
    place_row = place_row + (here[0] * high - rim - 1).astype(f32)
    grid_rows = float(high * row_count)

    def weights(position, extent, index):
        source = (position + 0.5) * side / extent - 0.5
        source = jnp.minimum(jnp.maximum(source, 0.0), side - 1.0)
        return jnp.maximum(0.0, 1.0 - jnp.abs(source - index))

    spread = weights(place_row, grid_rows, cell_row) * weights(place_col, float(wide), cell_col)
    return jnp.where((place_row >= 0.0) & (place_row < grid_rows), spread, 0.0)


def feature_kernel(row_count, share, channels, plans, weight_hbm, *refs):
    here_ref = place_here()
    blocks, refs = refs[:row_count], refs[row_count:]
    late, refs = refs[:2], refs[2:]
    (out_ref, spread_ref), kept, matrices = refs[:2], refs[2:4], refs[4 : 4 + len(plans)]
    weight_ref, grid_buf, sems = refs[4 + len(plans) :]
    copies = [
        pltpu.make_async_copy(source, target, sems.at[number])
        for number, (source, target) in enumerate(zip((weight_hbm, *late), (weight_ref, *kept)))
    ]
    for copy in copies:
        copy.start()
    here = (here_ref[0], here_ref[1])
    for plan, matrix in zip(plans, matrices):
        stretch_matrix(matrix, here, *plan)
    high, wide, depth = blocks[0].shape
    rows = out_ref.shape[1] // wide
    spread_ref[...] = spread_weights(here, high, wide, rows + 2, row_count, share, channels)
    grid_buf[...] = jnp.zeros_like(grid_buf)
    for shift, block in enumerate(blocks):
        row = wrap(here_ref[0] - shift, row_count) * high + rim + 1
        grid_buf[pl.ds(row, high)] = block[...]
    window = grid_buf[pl.ds(here_ref[0] * high, rows + 2)].reshape((rows + 2) * wide, depth)
    copies[0].wait()
    for col_tap in range(3):
        total = dot(window[0 : rows * wide], weight_ref[0, col_tap])
        for row_tap in (1, 2):
            total = total + dot(
                window[row_tap * wide : (row_tap + rows) * wide], weight_ref[row_tap, col_tap]
            )
        out_ref[col_tap] = total
    for copy in copies[1:]:
        copy.wait()


def neck_kernel(col_count, weight_ref, bias_ref, taps_ref, spread_ref, *refs):
    here_ref = place_here()
    messages, refs = refs[:col_count], refs[col_count:]
    windows, (bins_buf, acc_buf, term_buf) = refs[:col_count], refs[col_count:]
    rows, span, channels = windows[0].shape
    wide = taps_ref.shape[1] // rows
    width4 = span - 2 * rim
    bins = messages[0][messages[0].shape[0] - cell_rows :, :].astype(f32)
    for message in messages[1:]:
        bins = bins + message[message.shape[0] - cell_rows :, :].astype(f32)
    share = weight_ref.shape[2]
    first = here_ref[1] * share
    branch = first // channels
    side = pick(branch, bin_sides)
    used = lax.broadcasted_iota(jnp.int32, (cell_rows, 1), 0) < side * side
    bins = jnp.where(used, jnp.maximum(bins + bias_ref[pl.ds(branch, 1), :], 0.0), 0.0)
    if share != channels:
        bins_buf[...] = bins
        bins = bins_buf[:, pl.ds(pl.multiple_of(lax.rem(first, channels), 128), share)]
    ppm = jnp.dot(spread_ref[...], bins, precision=highest, preferred_element_type=f32).astype(bf16)
    size = rows * wide
    stacked = jnp.concatenate([ppm[tap * wide : tap * wide + size] for tap in range(3)], axis=1)
    for col_tap in range(3):
        total = dot(stacked, weight_ref[:, col_tap].reshape(3 * share, channels))
        acc_buf[col_tap, 8 : 8 + size, :] = total + taps_ref[col_tap]
    place = lax.broadcasted_iota(jnp.int32, (size, 1), 0).astype(f32)
    col = place - floor_div(place, wide) * wide
    total = (
        acc_buf[1, 8 : 8 + size, :]
        + jnp.where(col > 0.0, acc_buf[0, 7 : 7 + size, :], 0.0)
        + jnp.where(col < wide - 1.0, acc_buf[2, 9 : 9 + size, :], 0.0)
    )
    term_buf[...] = jnp.zeros_like(term_buf)
    term_buf[:, rim : rim + wide, :] = total.reshape(rows, wide, channels)
    for shift, window in enumerate(windows):
        target = wrap(here_ref[1] + shift, col_count)
        window[...] = term_buf[:, pl.ds(pl.multiple_of(target * width4, 8), span), :].astype(bf16)


def rows_kernel(col_count, high3, wide3, bias_ref, lat1_ref, lat2_ref, *refs):
    here_ref = place_here()
    messages, (lat3_ref, first_ref, second_ref, three_buf, low_buf, high_buf) = (
        refs[:col_count],
        refs[col_count:],
    )
    span = wide3 + 2 * rim
    total = messages[0][0 : high3 * span, :].astype(f32)
    for message in messages[1:]:
        total = total + message[0 : high3 * span, :].astype(f32)
    total = jnp.maximum(total + bias_ref[7:8, :], 0.0)
    col_here = here_ref[1]
    place = lax.broadcasted_iota(jnp.int32, (span, 1), 0) + col_here * wide3 - rim
    inside = (place >= 0) & (place < wide3 * col_count)
    for row in range(high3):
        three_buf[row, :span, :] = jnp.where(inside, total[row * span : (row + 1) * span], 0.0)
    lat3_ref[...] = three_buf[:, :span, :].astype(bf16)
    high1, wide1 = lat1_ref.shape[:2]
    high2, wide2 = lat2_ref.shape[:2]
    before, after = messages[1], messages[col_count - 1]
    sides_at = high3 * span
    for pack_buf, last in ((low_buf, False), (high_buf, True)):
        start, at = 0, sides_at
        for lat, high, wide in ((lat1_ref, high1, wide1), (lat2_ref, high2, wide2)):
            whole = wide + 2 * rim
            first = high - rim if last else 0
            left = before[at + rim * first : at + rim * (first + rim), :].astype(f32)
            right = after[at + rim * first : at + rim * (first + rim), :].astype(f32)
            left = jnp.where(col_here > 0, left, 0.0)
            right = jnp.where(col_here < col_count - 1, right, 0.0)
            for step in range(rim):
                pack_buf[start : start + rim, :] = left[rim * step : rim * (step + 1)]
                pack_buf[start + rim : start + rim + wide, :] = lat[first + step].astype(f32)
                pack_buf[start + rim + wide : start + whole, :] = right[rim * step : rim * (step + 1)]
                start += whole
            at += rim * high
        for step in range(rim):
            row = high3 - rim + step if last else step
            pack_buf[start : start + span, :] = three_buf[row, :span, :]
            start += span
    even = lax.rem(here_ref[0], 2) == 0
    low, high = low_buf[...], high_buf[...]
    first_ref[...] = jnp.where(even, high, low).astype(bf16)
    second_ref[...] = jnp.where(even, low, high).astype(bf16)


def tap_terms(small, weight_ref, first, store):
    channels = weight_ref.shape[3]
    for tap in range(9):
        weight = weight_ref[tap // 3, tap % 3, first : first + channels, :]
        store(tap, dot(small, weight).astype(bf16))


def late_kernel(sizes, plans, top_count, bias_ref, join_ref, *refs):
    here_ref = place_here()
    tops, refs = refs[:top_count], refs[top_count:]
    top_ref, base_ref, matrices, refs = refs[0], refs[1], refs[2 : 1 + len(plans)], refs[1 + len(plans) :]
    top_buf, small_buf, terms_buf, matrix_buf = refs
    high4, wide4 = sizes[3]
    here = (here_ref[0], here_ref[1])
    total = tops[0][...].astype(f32)
    for ref in tops[1:]:
        total = total + ref[...].astype(f32)
    top_buf[...] = jnp.zeros_like(top_buf)
    top_buf[:, : wide4 + 2 * rim, :] = jnp.maximum(total + bias_ref[4:5, :][None], 0.0)
    top_ref[...] = top_buf[...].reshape(top_ref.shape).astype(bf16)
    tall, broad = compact_shape((high4, wide4), 1)
    small_buf[...] = jnp.zeros_like(small_buf)
    for row in range(tall):
        small_buf[row * broad : (row + 1) * broad, :] = top_buf[
            row + rim - 1, rim - 1 : rim - 1 + broad, :
        ]
    lanes, channels = small_buf.shape

    def store(tap, value):
        terms_buf[tap * lanes : (tap + 1) * lanes, :] = value

    tap_terms(small_buf[...].astype(bf16), join_ref, 3 * channels, store)
    for plan, matrix in zip(plans, (matrix_buf, *matrices)):
        stretch_matrix(matrix, here, *plan)
    base_ref[...] = dot(matrix_buf[...], terms_buf[...])


def tail_kernel(sizes, part_count, *refs):
    here_ref = place_here()
    (high1, wide1), (high2, wide2), (high3, wide3), _, (row_count, col_count) = sizes
    quarters, refs = refs[:part_count], refs[part_count:]
    (
        top_ref,
        base_ref,
        lat1_ref,
        lat2_ref,
        lat3_ref,
        first_ref,
        second_ref,
        before_ref,
        after_ref,
        bias_ref,
        smooth_w,
        join_w,
        up3_ref,
        up2_ref,
        up1_ref,
        spread3_ref,
        out_ref,
        lat1_buf,
        lat2_buf,
        lat3_buf,
        pyr1_buf,
        pyr2_buf,
        pyr3_buf,
        moved1_buf,
        moved2_buf,
        moved3_buf,
        acc_buf,
        sums_buf,
        stack_buf,
        small3_buf,
        small2_buf,
        terms3_buf,
        terms2_buf,
        above_buf,
        below_buf,
        result_buf,
        sems,
    ) = refs
    channels = bias_ref.shape[1]

    even = lax.rem(here_ref[0], 2) == 0
    first, second = first_ref[...].astype(f32), second_ref[...].astype(f32)
    above_buf[...] = jnp.where(even, second, first)
    below_buf[...] = jnp.where(even, first, second)
    side_start = high3 * (wide3 + 2 * rim)
    row_start = 0
    for ref, buf, high, wide in (
        (lat1_ref, lat1_buf, high1, wide1),
        (lat2_ref, lat2_buf, high2, wide2),
        (lat3_ref, lat3_buf, high3, wide3 + 2 * rim),
    ):
        buf[...] = jnp.zeros_like(buf)
        whole = wide
        if buf is lat3_buf:
            buf[rim : rim + high, :wide, :] = ref[...].astype(f32)
        else:
            whole = wide + 2 * rim
            buf[rim : rim + high, rim : rim + wide, :] = ref[...].astype(f32)
            for source, col, keep in (
                (before_ref, 0, here_ref[1] > 0),
                (after_ref, rim + wide, here_ref[1] < col_count - 1),
            ):
                sides = source[side_start : side_start + rim * high, :].astype(f32)
                sides = jnp.where(keep, sides, 0.0)
                for row in range(high):
                    buf[rim + row, col : col + rim, :] = sides[rim * row : rim * row + rim]
            side_start += rim * high
        for source, row in ((above_buf, 0), (below_buf, rim + high)):
            both = source[row_start : row_start + rim * whole, :]
            for step in range(rim):
                buf[row + step, :whole, :] = both[step * whole : (step + 1) * whole]
        row_start += rim * whole

    shape1, shape2, shape3 = lat1_buf.shape[:2], lat2_buf.shape[:2], lat3_buf.shape[:2]

    def put(value, plain, moved):
        plain[0 : value.shape[0], :] = value.astype(bf16)
        later = jnp.concatenate([jnp.zeros((8, channels), f32), value, jnp.zeros((8, channels), f32)])
        moved[0 : later.shape[0], :] = later.astype(bf16)

    for lat_buf, matrix, source, out in (
        (lat3_buf, up3_ref, top_ref, (pyr3_buf, moved3_buf)),
        (lat2_buf, up2_ref, pyr3_buf, (pyr2_buf, moved2_buf)),
        (lat1_buf, up1_ref, pyr2_buf, (pyr1_buf, moved1_buf)),
    ):
        source = source[...]
        total = lat_buf[...].reshape(-1, channels) + dot(matrix[...], source)
        put(total, *out)

    def conv(source, shape, weight_at, rows):
        pitch = shape[1]
        span = rows * pitch
        plain, moved = source
        shift = pitch % 16
        stacked = jnp.concatenate(
            [
                plain[0:span, :],
                (moved if shift else plain)[pitch + shift : pitch + shift + span, :],
                plain[2 * pitch : 2 * pitch + span, :],
            ],
            axis=1,
        )
        for col_tap in range(3):
            weight = weight_at(col_tap)
            total = dot(stacked, weight.reshape(-1, channels))
            acc_buf[col_tap, :rows, :pitch, :] = total.reshape(rows, pitch, channels)

    def taps_total(rows, whole):
        total = acc_buf[0, :rows, 0:whole, :]
        for col_tap in (1, 2):
            total = total + acc_buf[col_tap, :rows, col_tap : whole + col_tap, :]
        return total

    def smooth(number, source, shape, wide):
        rows = shape[0] - 2
        conv(source, shape, lambda j: smooth_w[number, :, j], rows)
        total = taps_total(rows, wide + 2)
        return jnp.maximum(total + bias_ref[8 + number : 9 + number, :][None], 0.0)

    value = smooth(2, (pyr3_buf, moved3_buf), shape3, wide3)
    tall, broad = compact_shape((high3, wide3), 1)
    small3_buf[...] = jnp.zeros_like(small3_buf)
    for row in range(tall):
        small3_buf[row * broad : (row + 1) * broad, :] = value[row]
    lanes3 = small3_buf.shape[0]

    def store3(tap, value):
        terms3_buf[tap * lanes3 : (tap + 1) * lanes3, :] = value

    tap_terms(small3_buf[...].astype(bf16), join_w, 2 * channels, store3)

    rows2, whole2 = compact_shape((high2, wide2), 1)
    sums_buf[:rows2, :whole2, :] = smooth(1, (pyr2_buf, moved2_buf), shape2, wide2)
    half = (high2 // cuts2, wide2 // cuts2)
    tall, broad = compact_shape(half, 1)
    lanes2 = small2_buf.shape[0] // part_count
    small2_buf[...] = jnp.zeros_like(small2_buf)
    for part in range(part_count):
        row0, col0 = part // cuts2 * half[0], part % cuts2 * half[1]
        for row in range(tall):
            start = part * lanes2 + row * broad
            small2_buf[start : start + broad, :] = sums_buf[row0 + row, col0 : col0 + broad, :]

    def store2(tap, value):
        for part in range(part_count):
            start = (part * 9 + tap) * lanes2
            terms2_buf[start : start + lanes2, :] = value[part * lanes2 : (part + 1) * lanes2]

    tap_terms(small2_buf[...].astype(bf16), join_w, channels, store2)

    rows1, pitch1 = window_shape((high1, wide1), 1)
    value = smooth(0, (pyr1_buf, moved1_buf), shape1, wide1)
    down = here_ref[0] * high1 - 1 + lax.broadcasted_iota(jnp.int32, (rows1, 1, 1), 0)
    across = here_ref[1] * wide1 - 1 + lax.broadcasted_iota(jnp.int32, (1, wide1 + 2, 1), 1)
    inside = (down >= 0) & (down < high1 * row_count) & (across >= 0) & (across < wide1 * col_count)
    sums_buf[:rows1, : wide1 + 2, :] = jnp.where(inside, value, 0.0)
    put(sums_buf[...].reshape(rows1 * pitch1, channels), stack_buf, moved1_buf)
    conv((stack_buf, moved1_buf), (rows1, pitch1), lambda j: join_w[:, j, 0:channels], high1)
    total = taps_total(high1, wide1)
    spread = base_ref[...] + dot(spread3_ref[...], terms3_buf[...])
    sums_buf[:high1, :wide1, :] = total + spread.reshape(high1, wide1, channels)
    tall, broad = high1 // cuts2, wide1 // cuts2
    copies = []
    for part, matrix in enumerate(quarters):
        terms = terms2_buf[part * 9 * lanes2 : (part + 1) * 9 * lanes2, :]
        value = dot(matrix[...], terms).reshape(tall, broad, channels)
        row0, col0 = part // cuts2 * tall, part % cuts2 * broad
        value = value + sums_buf[row0 : row0 + tall, col0 : col0 + broad, :]
        value = jnp.maximum(value + bias_ref[11:12, :][None], 0.0)
        result_buf[part] = value.astype(bf16)
        target = out_ref.at[pl.ds(row0, tall), pl.ds(col0, broad), :]
        copies.append(pltpu.make_async_copy(result_buf.at[part], target, sems.at[part]))
        copies[-1].start()
    for copy in copies:
        copy.wait()


def tail(top, base, lats, swapped, before, after, biases, weights, matrices, quarters, sizes):
    one, _, _, _, _ = sizes
    channels = biases.shape[1]
    shapes = [window_shape(size, rim) for size in sizes[:3]]
    (rows1, pitch1), (rows2, pitch2), (rows3, pitch3) = shapes
    small3, small2 = matrices[-1].shape[1] // 9, quarters[0].shape[1] // 9 * len(quarters)
    inputs = (*quarters, top, base, *lats, *swapped, before, after, biases, *weights, *matrices)
    return pl.pallas_call(
        functools.partial(tail_kernel, sizes, len(quarters)),
        out_shape=jax.ShapeDtypeStruct((*one, channels), bf16),
        in_specs=[vmem_spec] * len(inputs),
        out_specs=hbm_spec,
        scratch_shapes=[
            pltpu.VMEM((rows1, pitch1, channels), f32),
            pltpu.VMEM((rows2, pitch2, channels), f32),
            pltpu.VMEM((rows3, pitch3, channels), f32),
            pltpu.VMEM((rows1 * pitch1, channels), bf16),
            pltpu.VMEM((rows2 * pitch2, channels), bf16),
            pltpu.VMEM((rows3 * pitch3, channels), bf16),
            pltpu.VMEM((rows1 * pitch1 + 16, channels), bf16),
            pltpu.VMEM((rows2 * pitch2 + 16, channels), bf16),
            pltpu.VMEM((rows3 * pitch3 + 16, channels), bf16),
            pltpu.VMEM((3, rows1 - 2, pitch1, channels), f32),
            pltpu.VMEM((rows1 - 2, pitch1, channels), f32),
            pltpu.VMEM(((rows1 - 2) * pitch1, channels), bf16),
            pltpu.VMEM((small3, channels), f32),
            pltpu.VMEM((small2, channels), f32),
            pltpu.VMEM((9 * small3, channels), bf16),
            pltpu.VMEM((9 * small2, channels), bf16),
            pltpu.VMEM(swapped[0].shape, f32),
            pltpu.VMEM(swapped[0].shape, f32),
            pltpu.VMEM((len(quarters), one[0] // cuts2, one[1] // cuts2, channels), bf16),
            pltpu.SemaphoreType.DMA((len(quarters),)),
        ],
        compiler_params=pltpu.CompilerParams(vmem_limit_bytes=30 * 1024 * 1024),
        cost_estimate=pl.CostEstimate(
            flops=8_000_000_000, bytes_accessed=12_000_000, transcendentals=0
        ),
    )(*inputs)


def local(
    level_one,
    level_two,
    level_three,
    level_four,
    bin_weight,
    neck_feature,
    neck_pooled,
    lateral_one,
    lateral_two,
    lateral_three,
    smooth_weight,
    join_weight,
    biases,
):
    row_count = lax.axis_size("row")
    col_count = lax.axis_size("col")
    high1, wide1 = level_one.shape[:2]
    high2, wide2 = level_two.shape[:2]
    high3, wide3 = level_three.shape[0], level_three.shape[1] // col_count
    high4, grid_cols, part_four = level_four.shape
    wide4 = grid_cols // col_count
    channels = bin_weight.shape[2]
    grid_rows = high4 * row_count
    table = cell_table(grid_rows, grid_cols)
    table = jnp.asarray(table)
    share_ppm = neck_pooled.shape[2]

    def shape(dims, kind=bf16):
        return jax.ShapeDtypeStruct(dims, kind)

    others = [shifted(level_four, "row", shift) for shift in range(1, row_count)]
    window_rows = high3 * (wide3 + 2 * rim)
    side_rows = rim * (high1 + high2)
    used = (level_one, lateral_one, level_two, lateral_two, level_three, lateral_three)
    kept = (biases, level_four, table, bin_weight)
    lat1, lat2, *rest = call(
        functools.partial(lateral_kernel, col_count, len(kept)),
        [shape((high1, wide1, channels)), shape((high2, wide2, channels))]
        + [shape((window_rows + side_rows, channels))] * col_count
        + [shape(value.shape, value.dtype) for value in kept],
        [hbm_spec] * (len(used) + len(kept)),
        [pltpu.VMEM(value.shape, value.dtype) for value in used]
        + [
            pltpu.VMEM((high3, level_three.shape[1] + 8, channels), f32),
            pltpu.VMEM((high1, wide1, channels), f32),
            pltpu.VMEM((high2, wide2, channels), f32),
            pltpu.VMEM((window_rows + side_rows, channels), f32),
            pltpu.SemaphoreType.DMA((len(used) + len(kept),)),
        ],
        300_000_000,
        4_000_000,
    )(*(in_hbm(value) for value in (*used, *kept)))
    pieces = rest[:col_count]
    bias_table, level_four, table, bin_weight = rest[col_count:]
    blocks = [level_four] + others
    near = (1, col_count - 1)
    messages = call(
        functools.partial(bins_kernel, row_count, col_count, share_ppm),
        [
            shape((window_rows + cell_rows + (side_rows if shift in near else 0), channels))
            for shift in range(col_count)
        ],
        [vmem_spec] * (2 + row_count + col_count),
        [pltpu.VMEM((table.shape[0], channels), f32)],
        100_000_000,
        1_000_000,
    )(table, bin_weight, *blocks, *pieces)

    received = [messages[0]] + [
        shifted(messages[shift], "col", shift) for shift in range(1, col_count)
    ]
    rows = high4 + 2 * rim
    sizes = (
        (high1, wide1),
        (high2, wide2),
        (high3, wide3),
        (high4, wide4),
        (row_count, col_count),
    )
    plans, late_plans = stretches(sizes)
    late = (neck_pooled, smooth_weight)
    taps, spread, neck_pooled, smooth_weight, *matrices = call(
        functools.partial(feature_kernel, row_count, share_ppm, channels, plans),
        [
            shape((3, rows * grid_cols, channels), f32),
            shape(((rows + 2) * grid_cols, cell_rows), f32),
        ]
        + [shape(value.shape) for value in late]
        + [shape(matrix_shape(plan)) for plan in plans],
        [hbm_spec] + [vmem_spec] * row_count + [hbm_spec] * len(late),
        [
            pltpu.VMEM(neck_feature.shape, bf16),
            pltpu.VMEM((grid_rows + 2 * rim + 2, grid_cols, part_four), bf16),
            pltpu.SemaphoreType.DMA((1 + len(late),)),
        ],
        700_000_000,
        12_000_000,
    )(in_hbm(neck_feature), *blocks, *(in_hbm(value) for value in late))
    span4 = wide4 + 2 * rim
    windows = call(
        functools.partial(neck_kernel, col_count),
        [shape((rows, span4, channels))] * col_count,
        [vmem_spec] * (4 + col_count),
        [
            pltpu.VMEM((cell_rows, channels), f32),
            pltpu.VMEM((3, rows * grid_cols + 16, channels), f32),
            pltpu.VMEM((rows, grid_cols + 16, channels), f32),
        ],
        300_000_000,
        3_000_000,
    )(neck_pooled, bias_table, taps, spread, *received)

    tops = [windows[0]] + [shifted(windows[shift], "col", shift) for shift in range(1, col_count)]
    span3 = wide3 + 2 * rim
    packed = rim * (wide1 + wide2 + wide3 + 6 * rim)
    lat3, first_rows, second_rows = call(
        functools.partial(rows_kernel, col_count, high3, wide3),
        [shape((high3, span3, channels))] + [shape((packed, channels))] * 2,
        [vmem_spec] * (3 + col_count),
        [
            pltpu.VMEM((high3, (span3 + 7) // 8 * 8, channels), f32),
            pltpu.VMEM((packed, channels), f32),
            pltpu.VMEM((packed, channels), f32),
        ],
        1_000_000,
        1_000_000,
    )(bias_table, lat1, lat2, *received)
    swapped = pair_swap(first_rows, second_rows, "row")
    small = late_plans[0][8]
    top_pitch = window_shape((high4, wide4), rim)[1]
    top, base, *quarters = call(
        functools.partial(late_kernel, sizes, late_plans, col_count),
        [
            shape((rows * top_pitch, channels)),
            shape((high1 * wide1, channels), f32),
        ]
        + [shape(matrix_shape(plan)) for plan in late_plans[1:]],
        [vmem_spec] * (2 + col_count),
        [
            pltpu.VMEM((rows, top_pitch, channels), f32),
            pltpu.VMEM((small, channels), f32),
            pltpu.VMEM((9 * small, channels), bf16),
            pltpu.VMEM(matrix_shape(late_plans[0]), bf16),
        ],
        700_000_000,
        5_000_000,
    )(bias_table, join_weight, *tops)
    return tail(
        top,
        base,
        (lat1, lat2, lat3),
        swapped,
        received[1],
        received[-1],
        bias_table,
        (smooth_weight, join_weight),
        matrices,
        quarters,
        sizes,
    )


def solution(mesh):
    placed = (
        P(("grp", "row"), "col", None),
        P(("grp", "row"), "col", None),
        P(("grp", "row"), None, "col"),
        P(("grp", "row"), None, "col"),
        P(None, "col", None),
        P(None, None, "col", None),
        P(None, None, "col", None),
        P(),
        P(),
        P(),
        P(),
        P(),
        P(),
    )
    return jax.shard_map(
        local, mesh=mesh, in_specs=placed, out_specs=P(("grp", "row"), "col", None), check_vma=False
    )
```

```python
import functools

import jax
import jax.numpy as jnp
import numpy as np
from jax import lax
from jax.experimental import pallas as pl
from jax.experimental.pallas import tpu as pltpu
from jax.sharding import PartitionSpec as P

highest = lax.Precision.HIGHEST
bin_sides = (1, 2, 3, 6)
rim = 2
cuts2 = 2
f32 = jnp.float32
bf16 = jnp.bfloat16
vmem_spec = pl.BlockSpec(memory_space=pltpu.VMEM)
hbm_spec = pl.BlockSpec(memory_space=pltpu.HBM)
params = pltpu.CompilerParams(vmem_limit_bytes=30 * 1024 * 1024)


def shifted(value, axis, shift):
    count = lax.axis_size(axis)
    return lax.ppermute(value, axis, [(i, (i + shift) % count) for i in range(count)])


def place_here():
    return lax.axis_index("row").astype(jnp.int32), lax.axis_index("col").astype(jnp.int32)


cell_rows = max(bin_sides) ** 2 + 4
cell_starts = tuple(sum((side * side + 7) // 8 * 8 for side in bin_sides[:k]) for k in range(len(bin_sides)))


def cell_table(extent_rows, extent_cols):
    table = np.zeros((cell_starts[-1] + cell_rows, 8), np.float32)
    table[:, 0] = -1.0
    table[:, 5] = 1.0
    for number, side in enumerate(bin_sides):
        for i in range(side):
            for j in range(side):
                top, low = i * extent_rows // side, -(-(i + 1) * extent_rows // side)
                left, right = j * extent_cols // side, -(-(j + 1) * extent_cols // side)
                size = (low - top) * (right - left)
                table[cell_starts[number] + i * side + j, :6] = (number, top, low, left, right, size)
    return table


def pick(number, values):
    result = values[0]
    for step, value in enumerate(values[1:], 1):
        result = jnp.where(number == step, value, result)
    return result


def dot(a, b):
    rows = a.shape[0]
    half = (rows // 2 + 15) // 16 * 16
    if half >= rows:
        return jnp.dot(a, b, preferred_element_type=f32)
    return jnp.concatenate(
        [
            jnp.dot(a[:half], b, preferred_element_type=f32),
            jnp.dot(a[half:], b, preferred_element_type=f32),
        ],
        axis=0,
    )


def in_hbm(value):
    return pltpu.with_memory_space_constraint(value, pltpu.HBM)


def call(kernel, outs, specs, scratch, flops, moved):
    return pl.pallas_call(
        kernel,
        out_shape=outs,
        in_specs=specs,
        out_specs=jax.tree.map(lambda _: vmem_spec, outs),
        scratch_shapes=scratch,
        compiler_params=params,
        cost_estimate=pl.CostEstimate(flops=flops, bytes_accessed=moved, transcendentals=0),
    )


def wrap(value, count):
    return lax.rem(value + count, count)


def floor_div(value, step):
    return jnp.floor((value + 0.5) / step)


def stretch_matrix(out_ref, here, out_shape, out_border, in_shape, in_border, factor, out_size, in_size, counts, lanes, taps=1):
    out_rows, out_pitch = out_shape
    lane = lax.broadcasted_iota(jnp.int32, (1, lanes * taps * taps), 1).astype(f32)
    tap = floor_div(lane, lanes)
    place = lane - tap * lanes
    row_tap = floor_div(tap, taps)
    col_tap = tap - row_tap * taps
    place_row = floor_div(place, in_shape[1])
    place_col = place - place_row * in_shape[1]

    def weights(axis, length, targets, tap_here):
        whole = float(in_size[axis] * counts[axis])
        first_out = (here[axis] * out_size[axis] - out_border[axis]).astype(f32) - (taps // 2)
        first_in = (here[axis] * in_size[axis] - in_border[axis]).astype(f32)
        output = first_out + tap_here + lax.broadcasted_iota(jnp.int32, (length, 1), 0).astype(f32)
        source = (output + 0.5) * (1.0 / factor) - 0.5
        source = jnp.minimum(jnp.maximum(source, 0.0), whole - 1.0)
        inside = jnp.where((output >= 0.0) & (output < whole * factor), 1.0, 0.0)
        return jnp.maximum(0.0, 1.0 - jnp.abs(source - (first_in + targets))) * inside

    down = weights(0, out_rows, place_row, row_tap)
    across = weights(1, out_pitch, place_col, col_tap)
    for row in range(0, out_rows, 2):
        pair = [down[step : step + 1, :] * across for step in range(row, min(row + 2, out_rows))]
        start = row * out_pitch
        value = jnp.concatenate(pair, axis=0)
        out_ref[start : start + value.shape[0], :] = value.astype(bf16)


def pitch_of(width):
    return (width + 15) // 16 * 16


def window_shape(size, border):
    return size[0] + 2 * border, (size[1] + 2 * border + 7) // 8 * 8


def compact_shape(size, border):
    return size[0] + 2 * border, size[1] + 2 * border


def stretches(sizes):
    one, two, three, four, counts = sizes

    def pyramid(out, source):
        shape = window_shape(source, rim)
        borders = (rim, rim)
        factor = out[0] // source[0]
        return (
            window_shape(out, rim), borders, shape, borders, factor, out, source, counts, shape[0] * shape[1]
        )

    def join(source, cuts, part):
        tile = (one[0] // cuts, one[1] // cuts)
        small = (source[0] // cuts, source[1] // cuts)
        shape = compact_shape(small, 1)
        out_border = (-part[0] * tile[0], -part[1] * tile[1])
        in_border = (1 - part[0] * small[0], 1 - part[1] * small[1])
        factor = one[0] // source[0]
        lanes = pitch_of(shape[0] * shape[1])
        return tile, out_border, shape, in_border, factor, one, source, counts, lanes, 3

    parts = [(i, j) for i in range(cuts2) for j in range(cuts2)]
    return (
        (pyramid(three, four), pyramid(two, three), pyramid(one, two), join(three, 1, (0, 0))),
        (join(four, 1, (0, 0)), *(join(two, cuts2, part) for part in parts)),
    )


def matrix_shape(plan):
    return plan[0][0] * plan[0][1], plan[8] * (plan[9] if len(plan) > 9 else 1) ** 2


def lateral_kernel(col_count, kept_count, *refs):
    here_ref = place_here()
    sources, refs = refs[: 6 + kept_count], refs[6 + kept_count :]
    (lat1_ref, lat2_ref), refs = refs[:2], refs[2:]
    pieces, refs = refs[:col_count], refs[col_count:]
    kept, refs = refs[:kept_count], refs[kept_count:]
    fetched, (wide_buf, one_buf, two_buf, piece_buf, sems) = refs[:6], refs[6:]
    copies = [
        pltpu.make_async_copy(source, target, sems.at[number])
        for number, (source, target) in enumerate(zip(sources, (*fetched, *kept)))
    ]
    for copy in copies:
        copy.start()
    one_ref, w1_ref, two_ref, w2_ref, three_ref, w3_ref = fetched
    bias_ref = kept[0]
    copies[6].wait()
    channels = w1_ref.shape[1]
    for number, (source, weight, row, buf, out) in enumerate(
        (
            (one_ref, w1_ref, 5, one_buf, lat1_ref),
            (two_ref, w2_ref, 6, two_buf, lat2_ref),
        )
    ):
        copies[2 * number].wait()
        copies[2 * number + 1].wait()
        high, wide, depth = source.shape
        value = dot(source[...].reshape(high * wide, depth), weight[...])
        value = jnp.maximum(value + bias_ref[row : row + 1, :], 0.0).reshape(high, wide, channels)
        buf[...] = value
        out[...] = value.astype(bf16)
    high3, whole3, share = three_ref.shape
    wide3 = whole3 // col_count
    col_here = here_ref[1]
    copies[4].wait()
    copies[5].wait()
    weight = w3_ref[pl.ds(pl.multiple_of(col_here * share, 16), share), :]
    value = dot(three_ref[...].reshape(high3 * whole3, share), weight)
    wide_buf[...] = jnp.zeros_like(wide_buf)
    wide_buf[:, rim : rim + whole3, :] = value.reshape(high3, whole3, channels)
    span = wide3 + 2 * rim
    for shift, piece in enumerate(pieces):
        target = wrap(col_here + shift, col_count)
        for row in range(high3):
            piece_buf[row * span : (row + 1) * span, :] = wide_buf[
                row, pl.ds(pl.multiple_of(target * wide3, 8), span), :
            ]
        start = high3 * span
        for buf in (one_buf, two_buf):
            high, wide = buf.shape[:2]
            first = wide - rim if shift == 1 else 0
            for row in range(high):
                piece_buf[start : start + rim, :] = buf[row, first : first + rim, :]
                start += rim
        piece[...] = piece_buf[...].astype(bf16)
    for copy in copies[7:]:
        copy.wait()


def bins_kernel(row_count, col_count, share, table_ref, weight_ref, *refs):
    here_ref = place_here()
    blocks, pieces, messages, (bins_buf,) = (
        refs[:row_count],
        refs[row_count : row_count + col_count],
        refs[row_count + col_count : row_count + 2 * col_count],
        refs[row_count + 2 * col_count :],
    )
    table = table_ref[...]
    high, wide, depth = blocks[0].shape
    place = lax.broadcasted_iota(jnp.int32, (1, high * wide), 1).astype(f32)
    place_row = floor_div(place, wide)
    place_col = place - place_row * wide
    in_cols = (place_col >= table[:, 3:4]) & (place_col < table[:, 4:5])
    pooled = None
    for shift, block in enumerate(blocks):
        row = place_row + (wrap(here_ref[0] - shift, row_count) * high).astype(f32)
        inside = in_cols & (row >= table[:, 1:2]) & (row < table[:, 2:3])
        inside = jnp.where(inside, 1.0, 0.0).astype(bf16)
        term = dot(inside, block[...].reshape(high * wide, depth))
        pooled = term if pooled is None else pooled + term
    pooled = (pooled / table[:, 5:6]).astype(bf16)
    bins = None
    for number in range(len(bin_sides)):
        term = jnp.where(table[:, 0:1] == number, dot(pooled, weight_ref[number]), 0.0)
        bins = term if bins is None else bins + term
    bins_buf[...] = bins
    channels = bins.shape[1]
    for shift, (piece, message) in enumerate(zip(pieces, messages)):
        kept = message.shape[0] - cell_rows
        message[0:kept, :] = piece[0:kept, :]
        target = wrap(here_ref[1] + shift, col_count)
        start = pl.multiple_of(pick(target * share // channels, cell_starts), 8)
        message[kept:, :] = bins_buf[pl.ds(start, cell_rows), :].astype(bf16)


def spread_weights(here, high, wide, rows, row_count, share, channels):
    side = pick(here[1] * share // channels, bin_sides).astype(f32)
    lane = lax.broadcasted_iota(jnp.int32, (1, cell_rows), 1).astype(f32)
    cell_row = floor_div(lane, side)
    cell_col = lane - cell_row * side
    place = lax.broadcasted_iota(jnp.int32, (rows * wide, 1), 0).astype(f32)
    place_row = floor_div(place, wide)
    place_col = place - place_row * wide
    place_row = place_row + (here[0] * high - rim - 1).astype(f32)
    grid_rows = float(high * row_count)

    def weights(position, extent, index):
        source = (position + 0.5) * side / extent - 0.5
        source = jnp.minimum(jnp.maximum(source, 0.0), side - 1.0)
        return jnp.maximum(0.0, 1.0 - jnp.abs(source - index))

    spread = weights(place_row, grid_rows, cell_row) * weights(place_col, float(wide), cell_col)
    return jnp.where((place_row >= 0.0) & (place_row < grid_rows), spread, 0.0)


def feature_kernel(row_count, share, channels, plans, weight_hbm, *refs):
    here_ref = place_here()
    blocks, refs = refs[:row_count], refs[row_count:]
    late, refs = refs[:2], refs[2:]
    (out_ref, spread_ref), kept, matrices = refs[:2], refs[2:4], refs[4 : 4 + len(plans)]
    weight_ref, grid_buf, sems = refs[4 + len(plans) :]
    copies = [
        pltpu.make_async_copy(source, target, sems.at[number])
        for number, (source, target) in enumerate(zip((weight_hbm, *late), (weight_ref, *kept)))
    ]
    for copy in copies:
        copy.start()
    here = (here_ref[0], here_ref[1])
    for plan, matrix in zip(plans, matrices):
        stretch_matrix(matrix, here, *plan)
    high, wide, depth = blocks[0].shape
    rows = out_ref.shape[1] // wide
    spread_ref[...] = spread_weights(here, high, wide, rows + 2, row_count, share, channels)
    grid_buf[...] = jnp.zeros_like(grid_buf)
    for shift, block in enumerate(blocks):
        row = wrap(here_ref[0] - shift, row_count) * high + rim + 1
        grid_buf[pl.ds(row, high)] = block[...]
    window = grid_buf[pl.ds(here_ref[0] * high, rows + 2)].reshape((rows + 2) * wide, depth)
    copies[0].wait()
    for col_tap in range(3):
        total = dot(window[0 : rows * wide], weight_ref[0, col_tap])
        for row_tap in (1, 2):
            total = total + dot(
                window[row_tap * wide : (row_tap + rows) * wide], weight_ref[row_tap, col_tap]
            )
        out_ref[col_tap] = total
    for copy in copies[1:]:
        copy.wait()


def neck_kernel(col_count, weight_ref, bias_ref, taps_ref, spread_ref, *refs):
    here_ref = place_here()
    messages, refs = refs[:col_count], refs[col_count:]
    windows, (bins_buf, acc_buf, term_buf) = refs[:col_count], refs[col_count:]
    rows, span, channels = windows[0].shape
    wide = taps_ref.shape[1] // rows
    width4 = span - 2 * rim
    bins = messages[0][messages[0].shape[0] - cell_rows :, :].astype(f32)
    for message in messages[1:]:
        bins = bins + message[message.shape[0] - cell_rows :, :].astype(f32)
    share = weight_ref.shape[2]
    first = here_ref[1] * share
    branch = first // channels
    side = pick(branch, bin_sides)
    used = lax.broadcasted_iota(jnp.int32, (cell_rows, 1), 0) < side * side
    bins = jnp.where(used, jnp.maximum(bins + bias_ref[pl.ds(branch, 1), :], 0.0), 0.0)
    if share != channels:
        bins_buf[...] = bins
        bins = bins_buf[:, pl.ds(pl.multiple_of(lax.rem(first, channels), 128), share)]
    ppm = jnp.dot(spread_ref[...], bins, precision=highest, preferred_element_type=f32).astype(bf16)
    size = rows * wide
    stacked = jnp.concatenate([ppm[tap * wide : tap * wide + size] for tap in range(3)], axis=1)
    for col_tap in range(3):
        total = dot(stacked, weight_ref[:, col_tap].reshape(3 * share, channels))
        acc_buf[col_tap, 8 : 8 + size, :] = total + taps_ref[col_tap]
    place = lax.broadcasted_iota(jnp.int32, (size, 1), 0).astype(f32)
    col = place - floor_div(place, wide) * wide
    total = (
        acc_buf[1, 8 : 8 + size, :]
        + jnp.where(col > 0.0, acc_buf[0, 7 : 7 + size, :], 0.0)
        + jnp.where(col < wide - 1.0, acc_buf[2, 9 : 9 + size, :], 0.0)
    )
    term_buf[...] = jnp.zeros_like(term_buf)
    term_buf[:, rim : rim + wide, :] = total.reshape(rows, wide, channels)
    for shift, window in enumerate(windows):
        target = wrap(here_ref[1] + shift, col_count)
        window[...] = term_buf[:, pl.ds(pl.multiple_of(target * width4, 8), span), :].astype(bf16)


def rows_kernel(col_count, high3, wide3, bias_ref, lat1_ref, lat2_ref, *refs):
    here_ref = place_here()
    messages, (lat3_ref, first_ref, second_ref, three_buf, low_buf, high_buf) = (
        refs[:col_count],
        refs[col_count:],
    )
    span = wide3 + 2 * rim
    total = messages[0][0 : high3 * span, :].astype(f32)
    for message in messages[1:]:
        total = total + message[0 : high3 * span, :].astype(f32)
    total = jnp.maximum(total + bias_ref[7:8, :], 0.0)
    col_here = here_ref[1]
    place = lax.broadcasted_iota(jnp.int32, (span, 1), 0) + col_here * wide3 - rim
    inside = (place >= 0) & (place < wide3 * col_count)
    for row in range(high3):
        three_buf[row, :span, :] = jnp.where(inside, total[row * span : (row + 1) * span], 0.0)
    lat3_ref[...] = three_buf[:, :span, :].astype(bf16)
    high1, wide1 = lat1_ref.shape[:2]
    high2, wide2 = lat2_ref.shape[:2]
    before, after = messages[1], messages[col_count - 1]
    sides_at = high3 * span
    for pack_buf, last in ((low_buf, False), (high_buf, True)):
        start, at = 0, sides_at
        for lat, high, wide in ((lat1_ref, high1, wide1), (lat2_ref, high2, wide2)):
            whole = wide + 2 * rim
            first = high - rim if last else 0
            left = before[at + rim * first : at + rim * (first + rim), :].astype(f32)
            right = after[at + rim * first : at + rim * (first + rim), :].astype(f32)
            left = jnp.where(col_here > 0, left, 0.0)
            right = jnp.where(col_here < col_count - 1, right, 0.0)
            for step in range(rim):
                pack_buf[start : start + rim, :] = left[rim * step : rim * (step + 1)]
                pack_buf[start + rim : start + rim + wide, :] = lat[first + step].astype(f32)
                pack_buf[start + rim + wide : start + whole, :] = right[rim * step : rim * (step + 1)]
                start += whole
            at += rim * high
        for step in range(rim):
            row = high3 - rim + step if last else step
            pack_buf[start : start + span, :] = three_buf[row, :span, :]
            start += span
    first_ref[...] = high_buf[...].astype(bf16)
    second_ref[...] = low_buf[...].astype(bf16)


def tap_terms(small, weight_ref, first, store):
    channels = weight_ref.shape[3]
    for tap in range(9):
        weight = weight_ref[tap // 3, tap % 3, first : first + channels, :]
        store(tap, dot(small, weight).astype(bf16))


def late_kernel(sizes, plans, top_count, bias_ref, join_ref, *refs):
    here_ref = place_here()
    tops, refs = refs[:top_count], refs[top_count:]
    top_ref, base_ref, matrices, refs = refs[0], refs[1], refs[2 : 1 + len(plans)], refs[1 + len(plans) :]
    top_buf, small_buf, terms_buf, matrix_buf = refs
    high4, wide4 = sizes[3]
    here = (here_ref[0], here_ref[1])
    total = tops[0][...].astype(f32)
    for ref in tops[1:]:
        total = total + ref[...].astype(f32)
    top_buf[...] = jnp.zeros_like(top_buf)
    top_buf[:, : wide4 + 2 * rim, :] = jnp.maximum(total + bias_ref[4:5, :][None], 0.0)
    top_ref[...] = top_buf[...].reshape(top_ref.shape).astype(bf16)
    tall, broad = compact_shape((high4, wide4), 1)
    small_buf[...] = jnp.zeros_like(small_buf)
    for row in range(tall):
        small_buf[row * broad : (row + 1) * broad, :] = top_buf[
            row + rim - 1, rim - 1 : rim - 1 + broad, :
        ]
    lanes, channels = small_buf.shape

    def store(tap, value):
        terms_buf[tap * lanes : (tap + 1) * lanes, :] = value

    tap_terms(small_buf[...].astype(bf16), join_ref, 3 * channels, store)
    for plan, matrix in zip(plans, (matrix_buf, *matrices)):
        stretch_matrix(matrix, here, *plan)
    base_ref[...] = dot(matrix_buf[...], terms_buf[...])


def tail_kernel(sizes, part_count, *refs):
    here_ref = place_here()
    (high1, wide1), (high2, wide2), (high3, wide3), _, (row_count, col_count) = sizes
    quarters, refs = refs[:part_count], refs[part_count:]
    (
        top_ref,
        base_ref,
        lat1_ref,
        lat2_ref,
        lat3_ref,
        first_ref,
        second_ref,
        before_ref,
        after_ref,
        bias_ref,
        smooth_w,
        join_w,
        up3_ref,
        up2_ref,
        up1_ref,
        spread3_ref,
        out_ref,
        lat1_buf,
        lat2_buf,
        lat3_buf,
        pyr1_buf,
        pyr2_buf,
        pyr3_buf,
        moved1_buf,
        moved2_buf,
        moved3_buf,
        acc_buf,
        sums_buf,
        stack_buf,
        small3_buf,
        small2_buf,
        terms3_buf,
        terms2_buf,
        above_buf,
        below_buf,
        result_buf,
        sems,
    ) = refs
    channels = bias_ref.shape[1]

    above_buf[...] = jnp.where(here_ref[0] > 0, first_ref[...].astype(f32), 0.0)
    below_buf[...] = jnp.where(here_ref[0] < row_count - 1, second_ref[...].astype(f32), 0.0)
    side_start = high3 * (wide3 + 2 * rim)
    row_start = 0
    for ref, buf, high, wide in (
        (lat1_ref, lat1_buf, high1, wide1),
        (lat2_ref, lat2_buf, high2, wide2),
        (lat3_ref, lat3_buf, high3, wide3 + 2 * rim),
    ):
        buf[...] = jnp.zeros_like(buf)
        whole = wide
        if buf is lat3_buf:
            buf[rim : rim + high, :wide, :] = ref[...].astype(f32)
        else:
            whole = wide + 2 * rim
            buf[rim : rim + high, rim : rim + wide, :] = ref[...].astype(f32)
            for source, col, keep in (
                (before_ref, 0, here_ref[1] > 0),
                (after_ref, rim + wide, here_ref[1] < col_count - 1),
            ):
                sides = source[side_start : side_start + rim * high, :].astype(f32)
                sides = jnp.where(keep, sides, 0.0)
                for row in range(high):
                    buf[rim + row, col : col + rim, :] = sides[rim * row : rim * row + rim]
            side_start += rim * high
        for source, row in ((above_buf, 0), (below_buf, rim + high)):
            both = source[row_start : row_start + rim * whole, :]
            for step in range(rim):
                buf[row + step, :whole, :] = both[step * whole : (step + 1) * whole]
        row_start += rim * whole

    shape1, shape2, shape3 = lat1_buf.shape[:2], lat2_buf.shape[:2], lat3_buf.shape[:2]

    def put(value, plain, moved):
        plain[0 : value.shape[0], :] = value.astype(bf16)
        later = jnp.concatenate([jnp.zeros((8, channels), f32), value, jnp.zeros((8, channels), f32)])
        moved[0 : later.shape[0], :] = later.astype(bf16)

    for lat_buf, matrix, source, out in (
        (lat3_buf, up3_ref, top_ref, (pyr3_buf, moved3_buf)),
        (lat2_buf, up2_ref, pyr3_buf, (pyr2_buf, moved2_buf)),
        (lat1_buf, up1_ref, pyr2_buf, (pyr1_buf, moved1_buf)),
    ):
        source = source[...]
        total = lat_buf[...].reshape(-1, channels) + dot(matrix[...], source)
        put(total, *out)

    def conv(source, shape, weight_at, rows):
        pitch = shape[1]
        span = rows * pitch
        plain, moved = source
        shift = pitch % 16
        stacked = jnp.concatenate(
            [
                plain[0:span, :],
                (moved if shift else plain)[pitch + shift : pitch + shift + span, :],
                plain[2 * pitch : 2 * pitch + span, :],
            ],
            axis=1,
        )
        for col_tap in range(3):
            weight = weight_at(col_tap)
            total = dot(stacked, weight.reshape(-1, channels))
            acc_buf[col_tap, :rows, :pitch, :] = total.reshape(rows, pitch, channels)

    def taps_total(rows, whole):
        total = acc_buf[0, :rows, 0:whole, :]
        for col_tap in (1, 2):
            total = total + acc_buf[col_tap, :rows, col_tap : whole + col_tap, :]
        return total

    def smooth(number, source, shape, wide):
        rows = shape[0] - 2
        conv(source, shape, lambda j: smooth_w[number, :, j], rows)
        total = taps_total(rows, wide + 2)
        return jnp.maximum(total + bias_ref[8 + number : 9 + number, :][None], 0.0)

    value = smooth(2, (pyr3_buf, moved3_buf), shape3, wide3)
    tall, broad = compact_shape((high3, wide3), 1)
    small3_buf[...] = jnp.zeros_like(small3_buf)
    for row in range(tall):
        small3_buf[row * broad : (row + 1) * broad, :] = value[row]
    lanes3 = small3_buf.shape[0]

    def store3(tap, value):
        terms3_buf[tap * lanes3 : (tap + 1) * lanes3, :] = value

    tap_terms(small3_buf[...].astype(bf16), join_w, 2 * channels, store3)

    rows2, whole2 = compact_shape((high2, wide2), 1)
    sums_buf[:rows2, :whole2, :] = smooth(1, (pyr2_buf, moved2_buf), shape2, wide2)
    half = (high2 // cuts2, wide2 // cuts2)
    tall, broad = compact_shape(half, 1)
    lanes2 = small2_buf.shape[0] // part_count
    small2_buf[...] = jnp.zeros_like(small2_buf)
    for part in range(part_count):
        row0, col0 = part // cuts2 * half[0], part % cuts2 * half[1]
        for row in range(tall):
            start = part * lanes2 + row * broad
            small2_buf[start : start + broad, :] = sums_buf[row0 + row, col0 : col0 + broad, :]

    def store2(tap, value):
        for part in range(part_count):
            start = (part * 9 + tap) * lanes2
            terms2_buf[start : start + lanes2, :] = value[part * lanes2 : (part + 1) * lanes2]

    tap_terms(small2_buf[...].astype(bf16), join_w, channels, store2)

    rows1, pitch1 = window_shape((high1, wide1), 1)
    value = smooth(0, (pyr1_buf, moved1_buf), shape1, wide1)
    down = here_ref[0] * high1 - 1 + lax.broadcasted_iota(jnp.int32, (rows1, 1, 1), 0)
    across = here_ref[1] * wide1 - 1 + lax.broadcasted_iota(jnp.int32, (1, wide1 + 2, 1), 1)
    inside = (down >= 0) & (down < high1 * row_count) & (across >= 0) & (across < wide1 * col_count)
    sums_buf[:rows1, : wide1 + 2, :] = jnp.where(inside, value, 0.0)
    put(sums_buf[...].reshape(rows1 * pitch1, channels), stack_buf, moved1_buf)
    conv((stack_buf, moved1_buf), (rows1, pitch1), lambda j: join_w[:, j, 0:channels], high1)
    total = taps_total(high1, wide1)
    spread = base_ref[...] + dot(spread3_ref[...], terms3_buf[...])
    sums_buf[:high1, :wide1, :] = total + spread.reshape(high1, wide1, channels)
    tall, broad = high1 // cuts2, wide1 // cuts2
    copies = []
    for part, matrix in enumerate(quarters):
        terms = terms2_buf[part * 9 * lanes2 : (part + 1) * 9 * lanes2, :]
        value = dot(matrix[...], terms).reshape(tall, broad, channels)
        row0, col0 = part // cuts2 * tall, part % cuts2 * broad
        value = value + sums_buf[row0 : row0 + tall, col0 : col0 + broad, :]
        value = jnp.maximum(value + bias_ref[11:12, :][None], 0.0)
        result_buf[part] = value.astype(bf16)
        target = out_ref.at[pl.ds(row0, tall), pl.ds(col0, broad), :]
        copies.append(pltpu.make_async_copy(result_buf.at[part], target, sems.at[part]))
        copies[-1].start()
    for copy in copies:
        copy.wait()


def tail(top, base, lats, swapped, before, after, biases, weights, matrices, quarters, sizes):
    one, _, _, _, _ = sizes
    channels = biases.shape[1]
    shapes = [window_shape(size, rim) for size in sizes[:3]]
    (rows1, pitch1), (rows2, pitch2), (rows3, pitch3) = shapes
    small3, small2 = matrices[-1].shape[1] // 9, quarters[0].shape[1] // 9 * len(quarters)
    inputs = (*quarters, top, base, *lats, *swapped, before, after, biases, *weights, *matrices)
    return pl.pallas_call(
        functools.partial(tail_kernel, sizes, len(quarters)),
        out_shape=jax.ShapeDtypeStruct((*one, channels), bf16),
        in_specs=[vmem_spec] * len(inputs),
        out_specs=hbm_spec,
        scratch_shapes=[
            pltpu.VMEM((rows1, pitch1, channels), f32),
            pltpu.VMEM((rows2, pitch2, channels), f32),
            pltpu.VMEM((rows3, pitch3, channels), f32),
            pltpu.VMEM((rows1 * pitch1, channels), bf16),
            pltpu.VMEM((rows2 * pitch2, channels), bf16),
            pltpu.VMEM((rows3 * pitch3, channels), bf16),
            pltpu.VMEM((rows1 * pitch1 + 16, channels), bf16),
            pltpu.VMEM((rows2 * pitch2 + 16, channels), bf16),
            pltpu.VMEM((rows3 * pitch3 + 16, channels), bf16),
            pltpu.VMEM((3, rows1 - 2, pitch1, channels), f32),
            pltpu.VMEM((rows1 - 2, pitch1, channels), f32),
            pltpu.VMEM(((rows1 - 2) * pitch1, channels), bf16),
            pltpu.VMEM((small3, channels), f32),
            pltpu.VMEM((small2, channels), f32),
            pltpu.VMEM((9 * small3, channels), bf16),
            pltpu.VMEM((9 * small2, channels), bf16),
            pltpu.VMEM(swapped[0].shape, f32),
            pltpu.VMEM(swapped[0].shape, f32),
            pltpu.VMEM((len(quarters), one[0] // cuts2, one[1] // cuts2, channels), bf16),
            pltpu.SemaphoreType.DMA((len(quarters),)),
        ],
        compiler_params=pltpu.CompilerParams(vmem_limit_bytes=30 * 1024 * 1024),
        cost_estimate=pl.CostEstimate(
            flops=8_000_000_000, bytes_accessed=12_000_000, transcendentals=0
        ),
    )(*inputs)


def local(
    level_one,
    level_two,
    level_three,
    level_four,
    bin_weight,
    neck_feature,
    neck_pooled,
    lateral_one,
    lateral_two,
    lateral_three,
    smooth_weight,
    join_weight,
    biases,
):
    row_count = lax.axis_size("row")
    col_count = lax.axis_size("col")
    high1, wide1 = level_one.shape[:2]
    high2, wide2 = level_two.shape[:2]
    high3, wide3 = level_three.shape[0], level_three.shape[1] // col_count
    high4, grid_cols, part_four = level_four.shape
    wide4 = grid_cols // col_count
    channels = bin_weight.shape[2]
    grid_rows = high4 * row_count
    table = cell_table(grid_rows, grid_cols)
    table = jnp.asarray(table)
    share_ppm = neck_pooled.shape[2]

    def shape(dims, kind=bf16):
        return jax.ShapeDtypeStruct(dims, kind)

    others = [shifted(level_four, "row", shift) for shift in range(1, row_count)]
    window_rows = high3 * (wide3 + 2 * rim)
    side_rows = rim * (high1 + high2)
    used = (level_one, lateral_one, level_two, lateral_two, level_three, lateral_three)
    kept = (biases, level_four, table, bin_weight)
    lat1, lat2, *rest = call(
        functools.partial(lateral_kernel, col_count, len(kept)),
        [shape((high1, wide1, channels)), shape((high2, wide2, channels))]
        + [shape((window_rows + side_rows, channels))] * col_count
        + [shape(value.shape, value.dtype) for value in kept],
        [hbm_spec] * (len(used) + len(kept)),
        [pltpu.VMEM(value.shape, value.dtype) for value in used]
        + [
            pltpu.VMEM((high3, level_three.shape[1] + 8, channels), f32),
            pltpu.VMEM((high1, wide1, channels), f32),
            pltpu.VMEM((high2, wide2, channels), f32),
            pltpu.VMEM((window_rows + side_rows, channels), f32),
            pltpu.SemaphoreType.DMA((len(used) + len(kept),)),
        ],
        300_000_000,
        4_000_000,
    )(*(in_hbm(value) for value in (*used, *kept)))
    pieces = rest[:col_count]
    bias_table, level_four, table, bin_weight = rest[col_count:]
    blocks = [level_four] + others
    near = (1, col_count - 1)
    messages = call(
        functools.partial(bins_kernel, row_count, col_count, share_ppm),
        [
            shape((window_rows + cell_rows + (side_rows if shift in near else 0), channels))
            for shift in range(col_count)
        ],
        [vmem_spec] * (2 + row_count + col_count),
        [pltpu.VMEM((table.shape[0], channels), f32)],
        100_000_000,
        1_000_000,
    )(table, bin_weight, *blocks, *pieces)

    received = [messages[0]] + [
        shifted(messages[shift], "col", shift) for shift in range(1, col_count)
    ]
    rows = high4 + 2 * rim
    sizes = (
        (high1, wide1),
        (high2, wide2),
        (high3, wide3),
        (high4, wide4),
        (row_count, col_count),
    )
    plans, late_plans = stretches(sizes)
    late = (neck_pooled, smooth_weight)
    taps, spread, neck_pooled, smooth_weight, *matrices = call(
        functools.partial(feature_kernel, row_count, share_ppm, channels, plans),
        [
            shape((3, rows * grid_cols, channels), f32),
            shape(((rows + 2) * grid_cols, cell_rows), f32),
        ]
        + [shape(value.shape) for value in late]
        + [shape(matrix_shape(plan)) for plan in plans],
        [hbm_spec] + [vmem_spec] * row_count + [hbm_spec] * len(late),
        [
            pltpu.VMEM(neck_feature.shape, bf16),
            pltpu.VMEM((grid_rows + 2 * rim + 2, grid_cols, part_four), bf16),
            pltpu.SemaphoreType.DMA((1 + len(late),)),
        ],
        700_000_000,
        12_000_000,
    )(in_hbm(neck_feature), *blocks, *(in_hbm(value) for value in late))
    span4 = wide4 + 2 * rim
    windows = call(
        functools.partial(neck_kernel, col_count),
        [shape((rows, span4, channels))] * col_count,
        [vmem_spec] * (4 + col_count),
        [
            pltpu.VMEM((cell_rows, channels), f32),
            pltpu.VMEM((3, rows * grid_cols + 16, channels), f32),
            pltpu.VMEM((rows, grid_cols + 16, channels), f32),
        ],
        300_000_000,
        3_000_000,
    )(neck_pooled, bias_table, taps, spread, *received)

    tops = [windows[0]] + [shifted(windows[shift], "col", shift) for shift in range(1, col_count)]
    span3 = wide3 + 2 * rim
    packed = rim * (wide1 + wide2 + wide3 + 6 * rim)
    lat3, first_rows, second_rows = call(
        functools.partial(rows_kernel, col_count, high3, wide3),
        [shape((high3, span3, channels))] + [shape((packed, channels))] * 2,
        [vmem_spec] * (3 + col_count),
        [
            pltpu.VMEM((high3, (span3 + 7) // 8 * 8, channels), f32),
            pltpu.VMEM((packed, channels), f32),
            pltpu.VMEM((packed, channels), f32),
        ],
        1_000_000,
        1_000_000,
    )(bias_table, lat1, lat2, *received)
    swapped = shifted(first_rows, "row", 1), shifted(second_rows, "row", row_count - 1)
    small = late_plans[0][8]
    top_pitch = window_shape((high4, wide4), rim)[1]
    top, base, *quarters = call(
        functools.partial(late_kernel, sizes, late_plans, col_count),
        [
            shape((rows * top_pitch, channels)),
            shape((high1 * wide1, channels), f32),
        ]
        + [shape(matrix_shape(plan)) for plan in late_plans[1:]],
        [vmem_spec] * (2 + col_count),
        [
            pltpu.VMEM((rows, top_pitch, channels), f32),
            pltpu.VMEM((small, channels), f32),
            pltpu.VMEM((9 * small, channels), bf16),
            pltpu.VMEM(matrix_shape(late_plans[0]), bf16),
        ],
        700_000_000,
        5_000_000,
    )(bias_table, join_weight, *tops)
    return tail(
        top,
        base,
        (lat1, lat2, lat3),
        swapped,
        received[1],
        received[-1],
        bias_table,
        (smooth_weight, join_weight),
        matrices,
        quarters,
        sizes,
    )


def solution(mesh):
    placed = (
        P(("grp", "row"), "col", None),
        P(("grp", "row"), "col", None),
        P(("grp", "row"), None, "col"),
        P(("grp", "row"), None, "col"),
        P(None, "col", None),
        P(None, None, "col", None),
        P(None, None, "col", None),
        P(),
        P(),
        P(),
        P(),
        P(),
        P(),
    )
    return jax.shard_map(
        local, mesh=mesh, in_specs=placed, out_specs=P(("grp", "row"), "col", None), check_vma=False
    )
```
